128 devices in a mesh: seq: 16 (over y, z), head: 4 (over x), batch: 2 (over core).
Axes of the slice: x: 4, y: 4, z: 4, core: 2. Of those that a mesh axis runs over, the one named last changes fastest.
Arguments:
- tokens: bfloat16 [16384, 2560], P(('batch', 'seq'), 'head'), parts along dimension 0, may hold values from -6 to 6
- resets: int32 [16384], P(('batch', 'seq')), parts along dimension 0, may hold values 0 or 1
- w_x: bfloat16 [2560, 5120], P(None, 'head'), may hold values from -0.125 to 0.125
- w_z: bfloat16 [2560, 5120], P(None, 'head'), may hold values from -0.125 to 0.125
- w_bc: bfloat16 [2560, 256], replicated, may hold values from -0.125 to 0.125
- w_dt: bfloat16 [2560, 80], P(None, 'head'), may hold values from -0.125 to 0.125
- dt_bias: float32 [80], P('head'), may hold values from -2 to 1
- decay_rate: float32 [80], P('head'), may hold values from 6.1035156e-05 to 0.08
- d_skip: float32 [80], P('head'), may hold values from 0.5 to 1.5
- norm_gain: float32 [5120], P('head'), may hold values from 0.5 to 1.5
- w_out: bfloat16 [5120, 2560], P('head'), may hold values from -0.078125 to 0.078125
Outputs:
- mixed: bfloat16 [16384, 2560], P(('batch', 'seq'), 'head'), parts along dimension 0
The draws below stay inside these ranges and needn't reach their ends.
There are 2 independent parts, one for each index of `batch`. The reference program is written for one: setup_inputs(seed, part) draws one part's arguments, and reference() takes and returns one part's arrays. A program takes and returns all parts, laid end to end along the dimension named above; an argument that names none is the same for every part. Nothing has to cross between parts.
All inputs are finite; a program needn't handle non-finite values. No bound on the sum of `resets` on one device may be relied on, other than what follows from the above.
Results may differ from the reference program's by a relative error of at most 0.013.
Values may be sent and summed in bfloat16 or wider, within the bound.
No kernel may reach another device: no remote copies, remote signals or barrier semaphores. Data moves between devices by JAX's collectives and lax.ppermute only.
A program may use at most 128 MiB of HBM per device.

```python
import math
import jax
import jax.numpy as jnp
from jax import lax

D = 2560
DI = 5120
HEADS = 80
HEADDIM = 64
NSTATE = 128
L_DEV = 512
GROUP = 256
LENGTH = 8192


def with_ends(array, own_key, smallest, high):
    longest = array.shape.index(max(array.shape))
    spots = []
    for shift in (0, 1):
        where = [jax.random.randint(jax.random.fold_in(own_key, axis), (), 0, length) for axis, length in enumerate(array.shape)]
        where[longest] = (where[longest] + shift) % array.shape[longest]
        spots.append(tuple(where))
    return array.at[spots[0]].set(smallest).at[spots[1]].set(high)


def level_of(stream_key, extent, cuts, least, high):
    level, own = 1.0, jax.random.fold_in(stream_key, 6)
    for dim, shards_of in cuts:
        heights = jnp.exp(jax.random.uniform(jax.random.fold_in(own, dim), (shards_of,), jnp.float32, least / len(cuts), high / len(cuts)))
        level = level * jnp.repeat(heights, extent[dim] // shards_of).reshape([-1 if axis == dim else 1 for axis in range(len(extent))])
    return level


def normal_values(own_key, dims, scale, most, split=(), kind=jnp.bfloat16):
    result = scale * jax.random.normal(own_key, dims, jnp.float32)
    if split:
        result = result * level_of(own_key, dims, split, -0.22, 0.18)
    return jnp.clip(result, -most, most).astype(kind)


def setup_inputs(seed: int = 0, part: int = 0) -> dict:
    keys = jax.random.split(jax.random.key(seed), 12)
    part_splits = jax.random.split(jax.random.fold_in(keys[11], part), 12)
    tokens = normal_values(part_splits[0], (LENGTH, D), 1.0, 6.0, ((0, 16), (1, 4)))
    resets = with_ends((jax.random.randint(part_splits[1], (LENGTH,), 0, 2 * L_DEV) < 1).astype(jnp.int32), jax.random.fold_in(part_splits[1], 1), 0, 1)
    w_x = normal_values(keys[2], (D, DI), D ** -0.5, 0.125, ((1, 4),))
    w_z = normal_values(keys[3], (D, DI), D ** -0.5, 0.125, ((1, 4),))
    w_bc = normal_values(keys[4], (D, 2 * NSTATE), D ** -0.5, 0.125)
    w_dt = normal_values(keys[5], (D, HEADS), D ** -0.5, 0.125, ((1, 4),))
    dt_bias = jnp.clip(-2.0 + 3.0 * jax.random.uniform(keys[6], (HEADS,), jnp.float32) ** level_of(keys[6], (HEADS,), ((0, 4),), -0.2, 0.2), -2.0, 1.0)
    decay_rate = jnp.clip(jnp.exp(math.log(0.08) - 7.178332 * jax.random.uniform(keys[7], (HEADS,), jnp.float32) ** level_of(keys[7], (HEADS,), ((0, 4),), -0.2, 0.2)), 6.103515625e-05, 0.08)
    d_skip = jnp.clip(0.5 + 1.0 * jax.random.uniform(keys[8], (HEADS,), jnp.float32) ** level_of(keys[8], (HEADS,), ((0, 4),), -0.2, 0.2), 0.5, 1.5)
    norm_gain = jnp.clip(1.0 + 0.1 * jax.random.normal(keys[9], (DI,), jnp.float32), 0.5, 1.5)
    w_out = normal_values(keys[10], (DI, D), DI ** -0.5, 0.078125, ((0, 4),))
    return {"tokens": tokens, "resets": resets, "w_x": w_x, "w_z": w_z, "w_bc": w_bc, "w_dt": w_dt, "dt_bias": dt_bias, "decay_rate": decay_rate, "d_skip": d_skip, "norm_gain": norm_gain, "w_out": w_out}


def decay_block(inputs, step_size, log_decay, in_proj, out_proj, restart, state_in):
    cumulative = jnp.cumsum(log_decay, axis=0)
    segment = jnp.cumsum(restart)
    places = jnp.arange(restart.shape[0], dtype=jnp.int32)
    same_doc = (segment[:, None] == segment[None, :]) & (places[:, None] >= places[None, :])
    scores = jnp.dot(out_proj, in_proj.T, preferred_element_type=jnp.float32)
    spread = cumulative.T[:, :, None] - cumulative.T[:, None, :]
    factor = jnp.exp(jnp.where(same_doc[None], spread, -jnp.inf))
    mixing = (factor * scores[None] * step_size.T[:, None, :]).astype(jnp.bfloat16)
    output = jnp.einsum('hts,shp->thp', mixing.astype(jnp.float32), inputs.astype(jnp.float32))
    entering = jnp.where((segment == 0)[:, None], jnp.exp(cumulative), 0.0)
    carried = jnp.einsum('tn,hpn->thp', out_proj.astype(jnp.float32), state_in, precision=lax.Precision.HIGHEST)
    output = output + entering[:, :, None] * carried
    closing = segment[-1]
    keeping = jnp.where((segment == closing)[:, None], jnp.exp(cumulative[-1][None, :] - cumulative), 0.0) * step_size
    scaled = (keeping[:, :, None] * inputs.astype(jnp.float32)).astype(jnp.bfloat16)
    update = jnp.einsum('shp,sn->hpn', scaled.astype(jnp.float32), in_proj.astype(jnp.float32))
    through = jnp.where(closing == 0, jnp.exp(cumulative[-1]), 0.0)
    return (output, update + through[:, None, None] * state_in)

def reference(tokens, resets, w_x, w_z, w_bc, w_dt, dt_bias, decay_rate, d_skip, norm_gain, w_out):
    inner = jax.nn.silu(jnp.dot(tokens, w_x, preferred_element_type=jnp.float32)).astype(jnp.bfloat16)
    gating = jnp.dot(tokens, w_z, preferred_element_type=jnp.float32).astype(jnp.bfloat16)
    mapped = jax.nn.silu(jnp.dot(tokens, w_bc, preferred_element_type=jnp.float32)).astype(jnp.bfloat16)
    step_size = jax.nn.softplus(jnp.dot(tokens, w_dt, preferred_element_type=jnp.float32) + dt_bias)
    log_decay = -step_size * decay_rate
    blocks = LENGTH // GROUP
    sliced = (inner.reshape(blocks, GROUP, HEADS, HEADDIM), step_size.reshape(blocks, GROUP, HEADS), log_decay.reshape(blocks, GROUP, HEADS), mapped[:, :NSTATE].reshape(blocks, GROUP, NSTATE), mapped[:, NSTATE:].reshape(blocks, GROUP, NSTATE), resets.reshape(blocks, GROUP))

    def advance(state_in, pieces):
        output, state_out = decay_block(pieces[0], pieces[1], pieces[2], pieces[3], pieces[4], pieces[5], state_in)
        return (state_out, output)
    final_state, outputs = lax.scan(advance, jnp.zeros((HEADS, HEADDIM, NSTATE), jnp.float32), sliced)
    mixed_heads = outputs.reshape(LENGTH, HEADS, HEADDIM) + d_skip[None, :, None] * inner.reshape(LENGTH, HEADS, HEADDIM).astype(jnp.float32)
    gated = mixed_heads.reshape(LENGTH, DI) * jax.nn.silu(gating.astype(jnp.float32))
    meansq = lax.optimization_barrier(jnp.mean(gated * gated, axis=1, keepdims=True))
    normed = (gated * lax.rsqrt(meansq + 1e-05) * norm_gain).astype(jnp.bfloat16)
    return jnp.dot(normed, w_out, preferred_element_type=jnp.float32).astype(jnp.bfloat16)
```

```python
import functools

import jax
import jax.numpy as jnp
from jax import lax
from jax.experimental import pallas as pl
from jax.experimental.pallas import tpu as pltpu
from jax.sharding import Mesh
from jax.sharding import PartitionSpec as P

DI = 5120
HEADDIM = 64
NSTATE = 128
GROUP = 256
ROWS = 512
FEAT = 640
WIDTH = 1280
TILE = 256
STEPS = WIDTH // TILE
PER = TILE // HEADDIM
LANES = 128
BD = 384
QUARTER = NSTATE // 4
MSG = QUARTER + 16
OUTROWS = ROWS + 16
LOG2E = 1.4426950408889634
BATCH_SEQ = ("batch", "seq_0", "seq_1")
F32 = jnp.float32
BF16 = jnp.bfloat16
MIB = 1 << 20


def dot(a, b):
    return lax.dot_general(a, b, (((1,), (0,)), ((), ())), preferred_element_type=F32)


def dot_nt(a, b):
    return lax.dot_general(a, b, (((1,), (1,)), ((), ())), preferred_element_type=F32)


def dot_tn(a, b):
    return lax.dot_general(a, b, (((0,), (0,)), ((), ())), preferred_element_type=F32)


def silu(v):
    return v / (1.0 + jnp.exp(-v))


def three(v):
    hi = v.astype(BF16)
    rest = v - hi.astype(F32)
    mid = rest.astype(BF16)
    return hi, mid, (rest - mid.astype(F32)).astype(BF16)


def shifted(array, axis, shift):
    return lax.ppermute(array, axis, [(i, (i + shift) % 4) for i in range(4)])


def whole(shape):
    return pl.BlockSpec(shape, lambda *_: (0,) * len(shape))


def tile(rows):
    return pl.BlockSpec((rows, TILE), lambda j, s: (0, j))


def params(mib):
    return pltpu.CompilerParams(vmem_limit_bytes=mib * MIB)


def cost(flops, nbytes, trans=0):
    return pl.CostEstimate(flops=int(flops), bytes_accessed=int(nbytes), transcendentals=int(trans))


def sds(shape, dtype):
    return jax.ShapeDtypeStruct(shape, dtype)


def project_body(add, idx, tok, w_x, w_z, w_bd, *refs):
    tokens = tok[...]
    out_x, out_z, out_bd = refs[-3:]
    part_x, part_z = dot(tokens, w_x[...]), dot(tokens, w_z[...])
    if add:
        part_x, part_z = refs[0][...] + part_x, refs[1][...] + part_z
    out_x[...] = part_x
    out_z[...] = part_z

    @pl.when(pl.program_id(0) == 0)
    def _():
        part = dot(tokens, w_bd[...])
        out_bd[...] = refs[2][...] + part if add else part


def project(owner, tok, w_x, w_z, w_bd, sums=()):
    weight = pl.BlockSpec((FEAT, TILE), lambda j, s: (s[0], j))
    narrow = pl.BlockSpec((FEAT, BD), lambda j, s: (s[0], 0))
    add = bool(sums)
    outs = [tile(ROWS), tile(ROWS), whole((ROWS, BD))]
    return pl.pallas_call(
        functools.partial(project_body, add),
        grid_spec=pltpu.PrefetchScalarGridSpec(
            num_scalar_prefetch=1,
            grid=(STEPS,),
            in_specs=[whole((ROWS, FEAT)), weight, weight, narrow, *(outs if add else [])],
            out_specs=outs,
        ),
        out_shape=[sds((ROWS, WIDTH), F32), sds((ROWS, WIDTH), F32), sds((ROWS, BD), F32)],
        input_output_aliases={5: 0, 6: 1, 7: 2} if add else {},
        compiler_params=params(20),
        cost_estimate=cost(2 * ROWS * FEAT * (2 * WIDTH + BD), 10e6),
        name="project_add" if add else "project",
    )(owner, tok, w_x, w_z, w_bd, *sums)


def head_rows(j):
    head = lax.broadcasted_iota(jnp.int32, (LANES, TILE), 0)
    channel = lax.broadcasted_iota(jnp.int32, (LANES, TILE), 1)
    return (head == PER * j + channel // HEADDIM).astype(BF16)


def state_body(
    idx, tok, w_x, w_bd, acc_x, acc_bd, resets, bias, rate,
    inner_o, b_o, c_o, cum_o, step_o, first_o, thr_o, m0, m1, m2, m3,
    b_t, keep_hi, keep_lo, thr_s, state_s,
):
    j = pl.program_id(0)
    tokens = tok[...]

    @pl.when(j == 0)
    def _():
        bd = acc_bd[...] + dot(tokens, w_bd[...])
        mapped = silu(bd[:, : 2 * NSTATE])
        b_t[...] = mapped[:, :NSTATE].T.astype(BF16)
        b_o[...] = mapped[:, :NSTATE].astype(BF16)
        c_o[...] = mapped[:, NSTATE:].astype(BF16)
        logits = bd[:, 2 * NSTATE :] + bias[...]
        step = jnp.maximum(logits, 0.0) + jnp.log1p(jnp.exp(-jnp.abs(logits)))
        step_o[...] = step
        lane = lax.broadcasted_iota(jnp.int32, (ROWS, LANES), 1)
        decay = jnp.where(lane == LANES - 1, resets[...], -step * rate[...])
        row = lax.broadcasted_iota(jnp.int32, (GROUP, GROUP), 0)
        col = lax.broadcasted_iota(jnp.int32, (GROUP, GROUP), 1)
        lower = (row >= col).astype(BF16)
        thr_s[...] = jnp.zeros_like(thr_s)
        for g in range(2):
            span = slice(g * GROUP, (g + 1) * GROUP)
            hi, mid, lo = three(decay[span])
            cum = dot(lower, hi) + (dot(lower, mid) + dot(lower, lo))
            cum_o[span, :] = cum
            last = cum[GROUP - 1 :, :]
            seg, closing = cum[:, LANES - 1 :], last[:, LANES - 1 :]
            keep = jnp.where(seg == closing, jnp.exp(last - cum), 0.0) * step[span]
            hi = keep.astype(BF16)
            keep_hi[span, :] = hi
            keep_lo[span, :] = (keep - hi.astype(F32)).astype(BF16)
            through = jnp.where(closing == 0.0, jnp.exp(last), 0.0)
            for k, part in enumerate(three(through)):
                thr_s[pl.ds(8 * g + k, 1), :] = part.astype(F32)

    acc = acc_x[...] + dot(tokens, w_x[...])
    inner = silu(acc).astype(BF16)
    inner_o[...] = inner
    heads = head_rows(j)
    keep = dot(keep_hi[...], heads) + dot(keep_lo[...], heads)
    scaled = (keep * inner.astype(F32)).astype(BF16)
    state0 = dot(b_t[:, :GROUP], scaled[:GROUP])
    state1 = dot(b_t[:, GROUP:], scaled[GROUP:])
    thr = dot(thr_s[...].astype(BF16), heads)
    thr0 = thr[0:1] + thr[1:2] + thr[2:3]
    thr1 = thr[8:9] + thr[9:10] + thr[10:11]
    first_o[...] = state0
    thr_o[...] = jnp.broadcast_to(thr0, (8, TILE))
    state_s[...] = thr1 * state0 + state1
    hi, mid, lo = three(thr0 * thr1)
    row = lax.broadcasted_iota(jnp.int32, (16, TILE), 0)
    tail = jnp.where(
        row == 0, hi.astype(F32), jnp.where(row == 1, mid.astype(F32), lo.astype(F32))
    ).astype(BF16)
    for d, message in enumerate((m0, m1, m2, m3)):
        quarter = lax.rem(idx[1] + d, 4)
        start = pl.multiple_of(quarter * QUARTER, QUARTER)
        message[:QUARTER, :] = state_s[pl.ds(start, QUARTER), :].astype(BF16)
        message[QUARTER:, :] = tail


def device_state(idx, tok, w_x, w_bd, acc_x, acc_bd, resets, bias, rate):
    weight = pl.BlockSpec((FEAT, TILE), lambda j, s: (s[0], j))
    narrow = pl.BlockSpec((FEAT, BD), lambda j, s: (s[0], 0))
    small = whole((ROWS, LANES))
    return pl.pallas_call(
        state_body,
        grid_spec=pltpu.PrefetchScalarGridSpec(
            num_scalar_prefetch=1,
            grid=(STEPS,),
            in_specs=[
                whole((ROWS, FEAT)), weight, narrow, tile(ROWS), whole((ROWS, BD)),
                small, whole((1, LANES)), whole((1, LANES)),
            ],
            out_specs=[
                tile(ROWS), small, small, small, small, tile(NSTATE), tile(8),
                tile(MSG), tile(MSG), tile(MSG), tile(MSG),
            ],
            scratch_shapes=[
                pltpu.VMEM((NSTATE, ROWS), BF16),
                pltpu.VMEM((ROWS, LANES), BF16),
                pltpu.VMEM((ROWS, LANES), BF16),
                pltpu.VMEM((16, LANES), F32),
                pltpu.VMEM((NSTATE, TILE), F32),
            ],
        ),
        out_shape=[
            sds((ROWS, WIDTH), BF16), sds((ROWS, LANES), BF16), sds((ROWS, LANES), BF16),
            sds((ROWS, LANES), F32), sds((ROWS, LANES), F32), sds((NSTATE, WIDTH), F32),
            sds((8, WIDTH), F32), *[sds((MSG, WIDTH), BF16)] * 4,
        ],
        compiler_params=params(24),
        cost_estimate=cost(2 * ROWS * FEAT * (WIDTH + BD), 9e6),
        name="device_state",
    )(idx, tok, w_x, w_bd, acc_x, acc_bd, resets, bias, rate)


def decay_of(message):
    tail = message[QUARTER : QUARTER + 3, :].astype(F32)
    return tail[0:1] + tail[1:2] + tail[2:3]


def total_body(idx, m0, m1, m2, m3, out, held):
    for d, message in enumerate((m0, m1, m2, m3)):
        held[lax.rem(idx[1] + 4 - d, 4)] = message[...]
    state = held[0][:QUARTER].astype(F32)
    through = decay_of(held[0])
    for k in range(1, 4):
        decay = decay_of(held[k])
        state = decay * state + held[k][:QUARTER].astype(F32)
        through = through * decay
    hi, mid, lo = three(through)
    row = lax.broadcasted_iota(jnp.int32, (16, WIDTH), 0)
    out[:QUARTER, :] = state.astype(BF16)
    out[QUARTER:, :] = jnp.where(
        row == 0, hi.astype(F32), jnp.where(row == 1, mid.astype(F32), lo.astype(F32))
    ).astype(BF16)


def prefix_body(idx, m0, m1, m2, m3, t0, t1, t2, t3, h0, h1, h2, h3, held, rows, found):
    for d, message in enumerate((m0, m1, m2, m3)):
        held[lax.rem(idx[1] + 4 - d, 4)] = message[...]
    for d, message in enumerate((t0, t1, t2, t3)):
        rows[lax.rem(idx[0] + 4 - d, 4)] = message[...]
    state = jnp.zeros((QUARTER, WIDTH), F32)
    for k in range(3):
        after = decay_of(rows[k]) * state + rows[k][:QUARTER].astype(F32)
        state = jnp.where(k < idx[0], after, state)
    for k in range(4):
        found[k] = state.astype(BF16)
        if k < 3:
            state = decay_of(held[k]) * state + held[k][:QUARTER].astype(F32)
    for d, out in enumerate((h0, h1, h2, h3)):
        out[...] = found[lax.rem(idx[1] + d, 4)]


def row_total(idx, messages):
    return pl.pallas_call(
        total_body,
        grid_spec=pltpu.PrefetchScalarGridSpec(
            num_scalar_prefetch=1,
            grid=(1,),
            in_specs=[whole((MSG, WIDTH))] * 4,
            out_specs=whole((MSG, WIDTH)),
            scratch_shapes=[pltpu.VMEM((4, MSG, WIDTH), BF16)],
        ),
        out_shape=sds((MSG, WIDTH), BF16),
        compiler_params=params(12),
        cost_estimate=cost(1e6, 1e6),
        name="row_total",
    )(idx, *messages)


def prefixes(idx, messages, totals):
    return pl.pallas_call(
        prefix_body,
        grid_spec=pltpu.PrefetchScalarGridSpec(
            num_scalar_prefetch=1,
            grid=(1,),
            in_specs=[whole((MSG, WIDTH))] * 8,
            out_specs=[whole((QUARTER, WIDTH))] * 4,
            scratch_shapes=[
                pltpu.VMEM((4, MSG, WIDTH), BF16),
                pltpu.VMEM((4, MSG, WIDTH), BF16),
                pltpu.VMEM((4, QUARTER, WIDTH), BF16),
            ],
        ),
        out_shape=[sds((QUARTER, WIDTH), BF16)] * 4,
        compiler_params=params(16),
        cost_estimate=cost(1e6, 1.5e6),
        name="prefixes",
    )(idx, *messages, *totals)


def gate_body(idx, tok, w_z, acc_z, out):
    gating = (acc_z[...] + dot(tok[...], w_z[...])).astype(BF16).astype(F32)
    out[...] = silu(gating)


def gate(idx, tok, w_z, acc_z):
    weight = pl.BlockSpec((FEAT, TILE), lambda j, s: (s[0], j))
    return pl.pallas_call(
        gate_body,
        grid_spec=pltpu.PrefetchScalarGridSpec(
            num_scalar_prefetch=1,
            grid=(STEPS,),
            in_specs=[whole((ROWS, FEAT)), weight, tile(ROWS)],
            out_specs=tile(ROWS),
        ),
        out_shape=sds((ROWS, WIDTH), F32),
        input_output_aliases={3: 0},
        compiler_params=params(16),
        cost_estimate=cost(2 * ROWS * FEAT * WIDTH, 8e6),
        name="gate",
    )(idx, tok, w_z, acc_z)


def mix_body(inner_r, b_r, c_r, cum_r, step_r, skip, out, ent_o, scores, cum_t, step_t, cum_2, ent):
    j = pl.program_id(1)
    half = GROUP // 2

    @pl.when(j == 0)
    def _():
        cum = cum_r[...]
        across = cum.T
        cum_2[...] = cum * LOG2E
        cum_t[...] = across * LOG2E
        step_t[...] = step_r[...].T
        row = lax.broadcasted_iota(jnp.int32, (GROUP, GROUP), 0)
        col = lax.broadcasted_iota(jnp.int32, (GROUP, GROUP), 1)
        seg = cum[:, LANES - 1 :]
        same = (seg == across[LANES - 1 :, :]) & (row >= col)
        scores[...] = jnp.where(same, dot_nt(c_r[...], b_r[...]), 0.0)
        ent[...] = jnp.where(seg == 0.0, jnp.exp(cum), 0.0)

    heads = head_rows(j)
    enter = ent[...]
    hi = enter.astype(BF16)
    lo = (enter - hi.astype(F32)).astype(BF16)
    ent_o[...] = dot(hi, heads) + dot(lo, heads)

    turned = pltpu.roll(cum_2[...], lax.rem(LANES - PER * j, LANES), 1)
    for pair in range(PER // 2):
        lanes = slice(pair * LANES, (pair + 1) * LANES)
        both = inner_r[:, lanes]
        ys = []
        for k in (2 * pair, 2 * pair + 1):
            head = PER * j + k
            before = cum_t[pl.ds(head, 1), :]
            step = step_t[pl.ds(head, 1), :]
            top = jnp.exp2(jnp.minimum(turned[:half, k : k + 1] - before[:, :half], 0.0))
            top = (top * scores[:half, :half] * step[:, :half]).astype(BF16)
            low = jnp.exp2(jnp.minimum(turned[half:, k : k + 1] - before, 0.0))
            low = (low * scores[half:, :] * step).astype(BF16)
            ys.append(jnp.concatenate([dot(top, both[:half]), dot(low, both)], 0))
        lane = lax.broadcasted_iota(jnp.int32, (GROUP, LANES), 1)
        y = jnp.where(lane < HEADDIM, ys[0], ys[1])
        out[:, lanes] = y + skip[:, lanes] * both.astype(F32)


def mix(inner, b, c, cum, step, skip):
    block = pl.BlockSpec((GROUP, TILE), lambda g, j: (g, j))
    small = pl.BlockSpec((GROUP, LANES), lambda g, j: (g, 0))
    return pl.pallas_call(
        mix_body,
        grid=(ROWS // GROUP, STEPS),
        in_specs=[block, small, small, small, small, pl.BlockSpec((1, TILE), lambda g, j: (0, j))],
        out_specs=[block, block],
        out_shape=[sds((ROWS, WIDTH), F32), sds((ROWS, WIDTH), F32)],
        scratch_shapes=[
            pltpu.VMEM((GROUP, GROUP), F32),
            pltpu.VMEM((LANES, GROUP), F32),
            pltpu.VMEM((LANES, GROUP), F32),
            pltpu.VMEM((GROUP, LANES), F32),
            pltpu.VMEM((GROUP, LANES), F32),
        ],
        compiler_params=params(16),
        cost_estimate=cost(3e9, 8e6, 3e6),
        name="mix",
    )(inner, b, c, cum, step, skip)


def squares_rows(total, out):
    hi, mid, lo = three(total)
    row = lax.broadcasted_iota(jnp.int32, (16, ROWS), 0)
    rows = jnp.where(
        row == 0,
        hi.astype(F32),
        jnp.where(row == 1, mid.astype(F32), jnp.where(row == 2, lo.astype(F32), 0.0)),
    ).astype(BF16)
    out[ROWS:, :] = jnp.concatenate([rows, jnp.zeros((16, FEAT - ROWS), BF16)], 1)


def gated_body(
    idx, h0, h1, h2, h3, first, thr, c_r, u_r, ent_r, zs_r, gain, w_out,
    rows_o, sums_o, out, state, acc, squares,
):
    j = pl.program_id(0)
    for d, part in enumerate((h0, h1, h2, h3)):
        start = pl.multiple_of(lax.rem(idx[1] + 4 - d, 4) * QUARTER, QUARTER)
        state[pl.ds(start, QUARTER), :] = part[...]
    enter = state[...]
    second = (first[...] + thr[0:1, :] * enter.astype(F32)).astype(BF16)
    carried = jnp.concatenate([dot(c_r[:GROUP], enter), dot(c_r[GROUP:], second)], 0)
    gated = (u_r[...] + ent_r[...] * carried) * zs_r[...]
    rows = (gated * gain[...]).astype(BF16)
    rows_o[...] = rows
    square = gated * gated
    hi = square.astype(BF16)
    lo = (square - hi.astype(F32)).astype(BF16)
    ones = jnp.ones((8, TILE), BF16)
    part_squares = dot_nt(ones, hi) + dot_nt(ones, lo)
    part = dot(rows, w_out[...])

    @pl.when(j == 0)
    def _():
        squares[...] = part_squares
        acc[...] = part

    @pl.when(j > 0)
    def _():
        squares[...] += part_squares
        acc[...] += part

    @pl.when(j == STEPS - 1)
    def _():
        sums_o[...] = squares[...]
        out[:ROWS, :] = acc[...].astype(BF16)
        squares_rows(squares[0:1, :], out)


def gated_rows(idx, parts, first, thr, c, u, ent, zs, gain, w_out):
    weight = pl.BlockSpec((TILE, FEAT), lambda j, s: (j, s[2]))
    return pl.pallas_call(
        gated_body,
        grid_spec=pltpu.PrefetchScalarGridSpec(
            num_scalar_prefetch=1,
            grid=(STEPS,),
            in_specs=[
                *[tile(QUARTER)] * 4, tile(NSTATE), tile(8), whole((ROWS, LANES)),
                tile(ROWS), tile(ROWS), tile(ROWS), tile(1), weight,
            ],
            out_specs=[tile(ROWS), whole((8, ROWS)), whole((OUTROWS, FEAT))],
            scratch_shapes=[
                pltpu.VMEM((NSTATE, TILE), BF16),
                pltpu.VMEM((ROWS, FEAT), F32),
                pltpu.VMEM((8, ROWS), F32),
            ],
        ),
        out_shape=[sds((ROWS, WIDTH), BF16), sds((8, ROWS), F32), sds((OUTROWS, FEAT), BF16)],
        compiler_params=params(24),
        cost_estimate=cost(2 * ROWS * WIDTH * FEAT * 1.3, 12e6),
        name="gated_rows",
    )(idx, *parts, first, thr, c, u, ent, zs, gain, w_out)


def block_body(send, idx, rows, sums, w_out, out):
    part = dot(rows[...], w_out[...])
    if send:
        out[:ROWS, :] = part.astype(BF16)
        squares_rows(sums[0:1, :], out)
    else:
        out[...] = part


def out_block(send, target, rows, sums, w_out):
    shape = sds((OUTROWS, FEAT), BF16) if send else sds((ROWS, FEAT), F32)
    return pl.pallas_call(
        functools.partial(block_body, send),
        grid_spec=pltpu.PrefetchScalarGridSpec(
            num_scalar_prefetch=1,
            grid=(1,),
            in_specs=[
                whole((ROWS, WIDTH)),
                whole((8, ROWS)),
                pl.BlockSpec((WIDTH, FEAT), lambda j, s: (0, s[0])),
            ],
            out_specs=whole(shape.shape),
        ),
        out_shape=shape,
        compiler_params=params(16),
        cost_estimate=cost(2 * ROWS * WIDTH * FEAT, 4e6),
        name="out_block",
    )(target, rows, sums, w_out)


def norm_body(own, sums, r1, r2, r3, out):
    parts = [*three(sums[0:1, :])]
    for arrived in (r1, r2, r3):
        tail = arrived[ROWS : ROWS + 3, :ROWS]
        parts += [tail[0:1], tail[1:2], tail[2:3]]
    row = lax.broadcasted_iota(jnp.int32, (16, ROWS), 0)
    stack = jnp.zeros((16, ROWS), F32)
    for k, part in enumerate(parts):
        stack = jnp.where(row == k, part.astype(F32), stack)
    squares = dot_tn(stack.astype(BF16), jnp.ones((16, LANES), BF16))
    factor = lax.rsqrt(squares / DI + 1e-05)
    for k in range(FEAT // LANES):
        lanes = slice(k * LANES, (k + 1) * LANES)
        total = own[:, lanes] + r1[:ROWS, lanes].astype(F32)
        total = total + (r2[:ROWS, lanes].astype(F32) + r3[:ROWS, lanes].astype(F32))
        out[:, lanes] = (total * factor).astype(BF16)


def norm(own, sums, arrived):
    return pl.pallas_call(
        norm_body,
        grid=(1,),
        in_specs=[whole((ROWS, FEAT)), whole((8, ROWS)), *[whole((OUTROWS, FEAT))] * 3],
        out_specs=whole((ROWS, FEAT)),
        out_shape=sds((ROWS, FEAT), BF16),
        compiler_params=params(24),
        cost_estimate=cost(2e6, 5e6),
        name="norm",
    )(own, sums, *arrived)


def on_device(tokens, resets, w_x, w_z, w_bc, w_dt, dt_bias, decay_rate, d_skip, norm_gain, w_out):
    me = lax.axis_index("head")
    y, z = lax.axis_index("seq_0"), lax.axis_index("seq_1")
    heads = w_dt.shape[1]
    arrived = {d: shifted(tokens, "head", d) for d in (1, 3, 2)}

    def owner(d):
        return ((me - d) % 4).reshape(1).astype(jnp.int32)

    w_bd = jnp.concatenate([w_bc, jnp.pad(w_dt, ((0, 0), (0, LANES - heads)))], 1)
    bias = jnp.pad(dt_bias, (0, LANES - heads)).reshape(1, LANES)
    rate = jnp.pad(decay_rate, (0, LANES - heads)).reshape(1, LANES)
    starts = jnp.broadcast_to(resets.astype(F32)[:, None], (ROWS, LANES))
    skip = jnp.repeat(d_skip, HEADDIM).reshape(1, WIDTH)
    gain = norm_gain.reshape(1, WIDTH)

    sums = project(owner(0), tokens, w_x, w_z, w_bd)
    sums = project(owner(1), arrived[1], w_x, w_z, w_bd, sums)
    acc_x, acc_z, acc_bd = project(owner(3), arrived[3], w_x, w_z, w_bd, sums)
    last = jnp.stack([(me - 2) % 4, z]).astype(jnp.int32)
    inner, b, c, cum, step, first, thr, *messages = device_state(
        last, arrived[2], w_x, w_bd, acc_x, acc_bd, starts, bias, rate
    )
    place = jnp.stack([y, z, (me + 2) % 4]).astype(jnp.int32)
    quarters = [messages[0], *(shifted(messages[d], "seq_1", d) for d in (1, 2, 3))]
    zs = gate(last, arrived[2], w_z, acc_z)
    u, ent = mix(inner, b, c, cum, step, skip)
    total = row_total(place, quarters)
    totals = [total, *(shifted(total, "seq_0", d) for d in (1, 2, 3))]
    parts = prefixes(place, quarters, totals)
    parts = [parts[0], *(shifted(parts[d], "seq_1", d) for d in (1, 2, 3))]
    rows, squares, far = gated_rows(place, parts, first, thr, c, u, ent, zs, gain, w_out)
    results = [shifted(far, "head", 2)]
    for d in (1, 3):
        target = ((me + d) % 4).reshape(1).astype(jnp.int32)
        results.append(shifted(out_block(True, target, rows, squares, w_out), "head", d))
    own = out_block(False, me.reshape(1).astype(jnp.int32), rows, squares, w_out)
    return norm(own, squares, results)


def solution(mesh):
    split = Mesh(
        mesh.devices.reshape(4, 4, mesh.shape["head"], mesh.shape["batch"]),
        ("seq_0", "seq_1", "head", "batch"),
    )
    placed = (
        P(BATCH_SEQ, "head"),
        P(BATCH_SEQ),
        P(None, "head"),
        P(None, "head"),
        P(),
        P(None, "head"),
        P("head"),
        P("head"),
        P("head"),
        P("head"),
        P("head", None),
    )
    return jax.shard_map(
        on_device, mesh=split, in_specs=placed, out_specs=P(BATCH_SEQ, "head"), check_vma=False
    )
```

```python
import functools

import jax
import jax.numpy as jnp
from jax import lax
from jax.experimental import pallas as pl
from jax.experimental.pallas import tpu as pltpu
from jax.sharding import Mesh
from jax.sharding import PartitionSpec as P

DI = 5120
HEADDIM = 64
NSTATE = 128
GROUP = 256
ROWS = 512
FEAT = 640
WIDTH = 1280
TILE = 256
STEPS = WIDTH // TILE
PER = TILE // HEADDIM
LANES = 128
BD = 384
QUARTER = NSTATE // 4
MSG = QUARTER + 16
OUTROWS = ROWS + 16
HALFROWS = GROUP + 16
LOG2E = 1.4426950408889634
BATCH_SEQ = ("batch", "seq_0", "seq_1")
F32 = jnp.float32
BF16 = jnp.bfloat16
MIB = 1 << 20


def dot(a, b):
    return lax.dot_general(a, b, (((1,), (0,)), ((), ())), preferred_element_type=F32)


def dot_nt(a, b):
    return lax.dot_general(a, b, (((1,), (1,)), ((), ())), preferred_element_type=F32)


def dot_tn(a, b):
    return lax.dot_general(a, b, (((0,), (0,)), ((), ())), preferred_element_type=F32)


def silu(v):
    return v / (1.0 + jnp.exp(-v))


def three(v):
    hi = v.astype(BF16)
    rest = v - hi.astype(F32)
    mid = rest.astype(BF16)
    return hi, mid, (rest - mid.astype(F32)).astype(BF16)


def shifted(array, axis, shift):
    return lax.ppermute(array, axis, [(i, (i + shift) % 4) for i in range(4)])


VMEM = pl.BlockSpec(memory_space=pltpu.VMEM)
HBM = pl.BlockSpec(memory_space=pltpu.HBM)
SMEM = pl.BlockSpec(memory_space=pltpu.SMEM)


def cost(flops, nbytes, trans=0):
    return pl.CostEstimate(flops=int(flops), bytes_accessed=int(nbytes), transcendentals=int(trans))


def call(body, name, idx, args, outs, scratch=(), mib=16, flops=1e8, aliases=None, kept=True):
    args = [pltpu.with_memory_space_constraint(a, pltpu.VMEM) for a in args]
    made = [pltpu.VMEM(*o) if kept else jax.ShapeDtypeStruct(*o) for o in outs]
    return pl.pallas_call(
        body,
        in_specs=[SMEM, *[VMEM] * len(args)],
        out_specs=[VMEM] * len(outs),
        out_shape=made,
        scratch_shapes=[pltpu.VMEM(*s) for s in scratch],
        input_output_aliases=aliases or {},
        compiler_params=pltpu.CompilerParams(vmem_limit_bytes=mib * MIB),
        cost_estimate=cost(flops, 1e6),
        name=name,
    )(idx, *args)


def span(j, size=TILE):
    return slice(j * size, (j + 1) * size)


def block_of(idx, shift):
    owner = lax.rem(idx[0] + 4 - shift, 4)
    return pl.ds(pl.multiple_of(owner * FEAT, FEAT), FEAT)


def add_parts(shift, idx, tokens, w_x, w_bc, w_dt, sums, outs):
    feats = block_of(idx, shift)
    parts = [dot(tokens, w_x[feats, span(j)]) for j in range(STEPS)]
    for j, part in enumerate(parts):
        outs[0][:, span(j)] = sums[0][:, span(j)] + part if sums else part
    part = dot(tokens, w_bc[feats, :])
    outs[1][:, : 2 * NSTATE] = sums[1][:, : 2 * NSTATE] + part if sums else part
    part = dot_nt(tokens, w_dt[:, feats])
    outs[1][:, 2 * NSTATE :] = sums[1][:, 2 * NSTATE :] + part if sums else part


def load_body(idx, tok, w_dt, w_x, w_z, w_bc, acc_x, acc_bd, v_x, v_z, v_bc, sems):
    copies = []
    for shift in range(4):
        feats = block_of(idx, shift)
        for source, target in ((w_x, v_x), (w_bc, v_bc)):
            sem = sems.at[len(copies)]
            copies.append(pltpu.make_async_copy(source.at[feats, :], target.at[feats, :], sem))
    copies.append(pltpu.make_async_copy(w_z, v_z, sems.at[len(copies)]))
    for copy in copies:
        copy.start()
    copies[0].wait()
    copies[1].wait()
    add_parts(0, idx, tok[...], v_x, v_bc, w_dt, (), (acc_x, acc_bd))
    for copy in copies[2:]:
        copy.wait()


def load_weights(idx, tok, w_dt, w_x, w_z, w_bc):
    tok, w_dt = (pltpu.with_memory_space_constraint(a, pltpu.VMEM) for a in (tok, w_dt))
    return pl.pallas_call(
        load_body,
        in_specs=[SMEM, VMEM, VMEM, HBM, HBM, HBM],
        out_specs=[VMEM] * 5,
        out_shape=[
            pltpu.VMEM((ROWS, WIDTH), F32),
            pltpu.VMEM((ROWS, BD), F32),
            pltpu.VMEM(w_x.shape, BF16),
            pltpu.VMEM(w_z.shape, BF16),
            pltpu.VMEM(w_bc.shape, BF16),
        ],
        scratch_shapes=[pltpu.SemaphoreType.DMA((9,))],
        compiler_params=pltpu.CompilerParams(vmem_limit_bytes=36 * MIB),
        cost_estimate=cost(2 * ROWS * FEAT * (WIDTH + BD), 15e6),
        name="load_weights",
    )(idx, tok, w_dt, w_x, w_z, w_bc)


def project_body(shift, idx, tok, w_x, w_bc, w_dt, acc_x, acc_bd, out_x, out_bd):
    add_parts(shift, idx, tok[...], w_x, w_bc, w_dt, (acc_x, acc_bd), (out_x, out_bd))


def project(shift, idx, tok, w_x, w_bc, w_dt, sums):
    return call(
        functools.partial(project_body, shift),
        "project",
        idx,
        [tok, w_x, w_bc, w_dt, *sums],
        [((ROWS, WIDTH), F32), ((ROWS, BD), F32)],
        flops=2 * ROWS * FEAT * (WIDTH + BD),
        aliases={5: 0, 6: 1},
    )


def head_rows(j):
    head = lax.broadcasted_iota(jnp.int32, (LANES, TILE), 0)
    channel = lax.broadcasted_iota(jnp.int32, (LANES, TILE), 1)
    return (head == PER * j + channel // HEADDIM).astype(BF16)


def terms(v, rows, width):
    hi, mid, lo = (part.astype(F32) for part in three(v))
    row = lax.broadcasted_iota(jnp.int32, (rows, width), 0)
    return jnp.where(row == 0, hi, jnp.where(row == 1, mid, jnp.where(row == 2, lo, 0.0)))


def state_body(
    idx, tok_0, tok_1, w_x, w_bc, w_dt, acc_x, acc_bd, resets, bias, rate,
    inner_o, b_o, c_o, cum_o, step_o, first_o, thr_o, m0, m1, m2, m3, state_s,
):
    tokens = jnp.concatenate([tok_0[...], tok_1[...]], 0)
    feats = block_of(idx, 2)
    mapped = silu(acc_bd[:, : 2 * NSTATE] + dot(tokens, w_bc[feats, :]))
    b_t = mapped[:, :NSTATE].T.astype(BF16)
    b_o[...] = mapped[:, :NSTATE].astype(BF16)
    c_o[...] = mapped[:, NSTATE:].astype(BF16)
    logits = acc_bd[:, 2 * NSTATE :] + dot_nt(tokens, w_dt[:, feats]) + bias[...]
    step = jnp.maximum(logits, 0.0) + jnp.log1p(jnp.exp(-jnp.abs(logits)))
    step_o[...] = step
    lane = lax.broadcasted_iota(jnp.int32, (ROWS, LANES), 1)
    decay = jnp.where(lane == LANES - 1, resets[...], -step * rate[...])
    row = lax.broadcasted_iota(jnp.int32, (GROUP, GROUP), 0)
    col = lax.broadcasted_iota(jnp.int32, (GROUP, GROUP), 1)
    lower = (row >= col).astype(BF16)
    keeps, throughs = [], []
    for g in range(2):
        hi, mid, lo = three(decay[span(g, GROUP)])
        cum = dot(lower, hi) + (dot(lower, mid) + dot(lower, lo))
        cum_o[span(g, GROUP), :] = cum
        last = cum[GROUP - 1 :, :]
        seg, closing = cum[:, LANES - 1 :], last[:, LANES - 1 :]
        keeps.append(jnp.where(seg == closing, jnp.exp(last - cum), 0.0) * step[span(g, GROUP)])
        throughs.append(jnp.where(closing == 0.0, jnp.exp(last), 0.0))
    keep = jnp.concatenate(keeps, 0)
    keep_hi = keep.astype(BF16)
    keep_lo = (keep - keep_hi.astype(F32)).astype(BF16)
    through = jnp.concatenate([terms(t, 8, LANES) for t in throughs], 0).astype(BF16)
    for j in range(STEPS):
        inner = silu(acc_x[:, span(j)] + dot(tokens, w_x[feats, span(j)])).astype(BF16)
        inner_o[:, span(j)] = inner
        heads = head_rows(j)
        wide = dot(keep_hi, heads) + dot(keep_lo, heads)
        scaled = (wide * inner.astype(F32)).astype(BF16)
        state0 = dot(b_t[:, :GROUP], scaled[:GROUP])
        state1 = dot(b_t[:, GROUP:], scaled[GROUP:])
        thr = dot(through, heads)
        thr0 = thr[0:1] + thr[1:2] + thr[2:3]
        thr1 = thr[8:9] + thr[9:10] + thr[10:11]
        first_o[:, span(j)] = state0
        thr_o[:, span(j)] = jnp.broadcast_to(thr0, (8, TILE))
        state_s[:, span(j)] = thr1 * state0 + state1
        last_rows = terms(thr0 * thr1, 16, TILE).astype(BF16)
        for message in (m0, m1, m2, m3):
            message[QUARTER:, span(j)] = last_rows
    for d, message in enumerate((m0, m1, m2, m3)):
        start = pl.multiple_of(lax.rem(idx[2] + d, 4) * QUARTER, QUARTER)
        message[:QUARTER, :] = state_s[pl.ds(start, QUARTER), :].astype(BF16)


def device_state(idx, far, w_x, w_bc, w_dt, sums, resets, bias, rate):
    small = (ROWS, LANES)
    return call(
        state_body,
        "device_state",
        idx,
        [*far, w_x, w_bc, w_dt, *sums, resets, bias, rate],
        [
            ((ROWS, WIDTH), BF16), (small, BF16), (small, BF16), (small, F32), (small, F32),
            ((NSTATE, WIDTH), F32), ((8, WIDTH), F32), *[((MSG, WIDTH), BF16)] * 4,
        ],
        [((NSTATE, WIDTH), F32)],
        flops=2 * ROWS * FEAT * (WIDTH + BD),
    )


def decay_of(message):
    tail = message[QUARTER : QUARTER + 3, :].astype(F32)
    return tail[0:1] + tail[1:2] + tail[2:3]


def total_body(idx, m0, m1, m2, m3, out, held):
    for d, message in enumerate((m0, m1, m2, m3)):
        held[lax.rem(idx[2] + 4 - d, 4)] = message[...]
    state = held[0][:QUARTER].astype(F32)
    through = decay_of(held[0])
    for k in range(1, 4):
        decay = decay_of(held[k])
        state = decay * state + held[k][:QUARTER].astype(F32)
        through = through * decay
    out[:QUARTER, :] = state.astype(BF16)
    out[QUARTER:, :] = terms(through, 16, WIDTH).astype(BF16)


def prefix_body(idx, m0, m1, m2, m3, t0, t1, t2, t3, h0, h1, h2, h3, held, rows, found):
    for d, message in enumerate((m0, m1, m2, m3)):
        held[lax.rem(idx[2] + 4 - d, 4)] = message[...]
    for d, message in enumerate((t0, t1, t2, t3)):
        rows[lax.rem(idx[1] + 4 - d, 4)] = message[...]
    state = jnp.zeros((QUARTER, WIDTH), F32)
    for k in range(3):
        after = decay_of(rows[k]) * state + rows[k][:QUARTER].astype(F32)
        state = jnp.where(k < idx[1], after, state)
    for k in range(4):
        found[k] = state.astype(BF16)
        if k < 3:
            state = decay_of(held[k]) * state + held[k][:QUARTER].astype(F32)
    for d, out in enumerate((h0, h1, h2, h3)):
        out[...] = found[lax.rem(idx[2] + d, 4)]


def row_total(idx, messages):
    return call(
        total_body,
        "row_total",
        idx,
        messages,
        [((MSG, WIDTH), BF16)],
        [((4, MSG, WIDTH), BF16)],
        mib=8,
    )[0]


def prefixes(idx, messages, totals):
    return call(
        prefix_body,
        "prefixes",
        idx,
        [*messages, *totals],
        [((QUARTER, WIDTH), BF16)] * 4,
        [((4, MSG, WIDTH), BF16), ((4, MSG, WIDTH), BF16), ((4, QUARTER, WIDTH), BF16)],
        mib=8,
    )


def gate_part_body(idx, t0, t1, t3, w_z, out):
    for j in range(STEPS):
        part = dot(t0[...], w_z[block_of(idx, 0), span(j)])
        for shift, tokens in ((1, t1), (3, t3)):
            part = part + dot(tokens[...], w_z[block_of(idx, shift), span(j)])
        out[:, span(j)] = part


def gate_part(idx, tokens, w_z):
    return call(
        gate_part_body,
        "gate_part",
        idx,
        [*tokens, w_z],
        [((ROWS, WIDTH), F32)],
        flops=6 * ROWS * FEAT * WIDTH,
    )[0]


def gate_body(idx, t_0, t_1, w_z, acc_z, out):
    tokens = jnp.concatenate([t_0[...], t_1[...]], 0)
    feats = block_of(idx, 2)
    for j in range(STEPS):
        gating = acc_z[:, span(j)] + dot(tokens, w_z[feats, span(j)])
        out[:, span(j)] = silu(gating.astype(BF16).astype(F32))


def gate(idx, far, w_z, acc_z):
    return call(
        gate_body,
        "gate",
        idx,
        [*far, w_z, acc_z],
        [((ROWS, WIDTH), F32)],
        flops=2 * ROWS * FEAT * WIDTH,
        aliases={4: 0},
    )[0]


def mix_body(g, idx, inner_r, b_r, c_r, cum_r, step_r, skip, out, ent_o, scores, cum_t, step_t):
    half = GROUP // 2
    rows = span(g, GROUP)
    cum = cum_r[rows, :]
    across = cum.T
    cum_2 = cum * LOG2E
    cum_t[...] = across * LOG2E
    step_t[...] = step_r[rows, :].T
    row = lax.broadcasted_iota(jnp.int32, (GROUP, GROUP), 0)
    col = lax.broadcasted_iota(jnp.int32, (GROUP, GROUP), 1)
    seg = cum[:, LANES - 1 :]
    same = (seg == across[LANES - 1 :, :]) & (row >= col)
    scores[...] = jnp.where(same, dot_nt(c_r[rows, :], b_r[rows, :]), 0.0)
    enter = jnp.where(seg == 0.0, jnp.exp(cum), 0.0)
    hi = enter.astype(BF16)
    lo = (enter - hi.astype(F32)).astype(BF16)
    lane = lax.broadcasted_iota(jnp.int32, (GROUP, LANES), 1)
    for j in range(STEPS):
        heads = head_rows(j)
        ent_o[:, span(j)] = dot(hi, heads) + dot(lo, heads)
    for pair in range(WIDTH // LANES):
        both = inner_r[rows, span(pair, LANES)]
        ys = []
        for head in (2 * pair, 2 * pair + 1):
            before = cum_t[head : head + 1, :]
            step = step_t[head : head + 1, :]
            top = jnp.exp2(jnp.minimum(cum_2[:half, head : head + 1] - before[:, :half], 0.0))
            top = (top * scores[:half, :half] * step[:, :half]).astype(BF16)
            low = jnp.exp2(jnp.minimum(cum_2[half:, head : head + 1] - before, 0.0))
            low = (low * scores[half:, :] * step).astype(BF16)
            ys.append(jnp.concatenate([dot(top, both[:half]), dot(low, both)], 0))
        y = jnp.where(lane < HEADDIM, ys[0], ys[1])
        out[:, span(pair, LANES)] = y + skip[:, span(pair, LANES)] * both.astype(F32)


def mix(g, idx, inner, b, c, cum, step, skip):
    return call(
        functools.partial(mix_body, g),
        "mix",
        idx,
        [inner, b, c, cum, step, skip],
        [((GROUP, WIDTH), F32), ((GROUP, WIDTH), F32)],
        [((GROUP, GROUP), F32), ((LANES, GROUP), F32), ((LANES, GROUP), F32)],
        flops=2e9,
    )


def block_cols(idx, shift):
    target = lax.rem(idx[0] + shift, 4)
    return pl.ds(pl.multiple_of(target * FEAT, FEAT), FEAT)


def squares_rows(total):
    width = total.shape[1]
    rows = terms(total, 16, width).astype(BF16)
    return jnp.concatenate([rows, jnp.zeros((16, FEAT - width), BF16)], 1)


def row_of(message, start, width):
    tail = message[start : start + 3, :width].astype(F32)
    return tail[0:1] + (tail[1:2] + tail[2:3])


def gated_body(
    g, idx, h0, h1, h2, h3, first, thr, c_r, u, ent, zs_r, gain, w_out, rows_o, sums_o, out, state
):
    for d, part in enumerate((h0, h1, h2, h3)):
        start = pl.multiple_of(lax.rem(idx[2] + 4 - d, 4) * QUARTER, QUARTER)
        state[pl.ds(start, QUARTER), :] = part[...]
    ones = jnp.ones((8, LANES), BF16)
    rows = span(g, GROUP)
    squares = jnp.zeros((GROUP, LANES), F32)
    for j in range(STEPS):
        enter = state[:, span(j)]
        if g:
            enter = first[:, span(j)] + thr[0:1, span(j)] * enter.astype(F32)
            enter = enter.astype(BF16)
        carried = dot(c_r[rows, :], enter)
        gated = (u[:, span(j)] + ent[:, span(j)] * carried) * zs_r[rows, span(j)]
        rows_o[:, span(j)] = (gated * gain[:, span(j)]).astype(BF16)
        square = gated * gated
        squares = squares + (square[:, :LANES] + square[:, LANES:])
    hi, mid, lo = three(squares)
    sums = dot_nt(ones, hi) + (dot_nt(ones, mid) + dot_nt(ones, lo))
    sums_o[...] = sums
    out[:GROUP, :] = dot(rows_o[...], w_out[:, block_cols(idx, 2)]).astype(BF16)
    out[GROUP:, :] = squares_rows(sums[0:1, :])


def gated_rows(g, idx, parts, first, thr, c, u, ent, zs, gain, w_out):
    return call(
        functools.partial(gated_body, g),
        "gated_rows",
        idx,
        [*parts, first, thr, c, u, ent, zs, gain, w_out],
        [((GROUP, WIDTH), BF16), ((8, GROUP), F32), ((HALFROWS, FEAT), BF16)],
        [((NSTATE, WIDTH), BF16)],
        flops=1.3 * ROWS * WIDTH * FEAT,
    )


def part_body(shift, idx, rows, w_out, out):
    out[...] = dot(rows[...], w_out[:, block_cols(idx, shift)])


def out_part(shift, idx, rows, w_out):
    return call(
        functools.partial(part_body, shift),
        "out_part",
        idx,
        [rows, w_out],
        [((GROUP, FEAT), F32)],
        flops=ROWS * WIDTH * FEAT,
    )[0]


def send_body(shift, idx, rows, sums, w_out, out):
    out[:GROUP, :] = dot(rows[...], w_out[:, block_cols(idx, shift)]).astype(BF16)
    out[GROUP:, :] = squares_rows(sums[0:1, :])


def out_send(shift, idx, rows, sums, w_out):
    return call(
        functools.partial(send_body, shift),
        "out_send",
        idx,
        [rows, sums, w_out],
        [((HALFROWS, FEAT), BF16)],
        flops=ROWS * WIDTH * FEAT,
    )[0]


def join_body(idx, part, sums, half, out):
    out[:GROUP, :] = (part[...] + half[:GROUP, :].astype(F32)).astype(BF16)
    out[GROUP:, :] = squares_rows(sums[0:1, :] + row_of(half, GROUP, GROUP))


def join(idx, part, sums, half):
    return call(
        join_body,
        "join",
        idx,
        [part, sums, half],
        [((HALFROWS, FEAT), BF16)],
        mib=8,
    )[0]


def norm_body(idx, own_0, own_1, sums_0, sums_1, left_0, left_1, right_0, right_1, out):
    halves = ((own_0, sums_0, left_0, right_0), (own_1, sums_1, left_1, right_1))
    for g, (own, sums, left, right) in enumerate(halves):
        total = sums[0:1, :] + (row_of(left, GROUP, GROUP) + row_of(right, GROUP, GROUP))
        stack = terms(total, 16, GROUP).astype(BF16)
        squares = dot_tn(stack, jnp.ones((16, LANES), BF16))
        factor = lax.rsqrt(squares / DI + 1e-05)
        for k in range(FEAT // LANES):
            lanes = span(k, LANES)
            value = left[:GROUP, lanes].astype(F32) + right[:GROUP, lanes].astype(F32)
            out[span(g, GROUP), lanes] = ((own[:, lanes] + value) * factor).astype(BF16)


def norm(idx, owns, sums, left, right):
    return call(
        norm_body,
        "norm",
        idx,
        [*owns, *sums, *left, *right],
        [((ROWS, FEAT), BF16)],
        kept=False,
    )[0]


def on_device(tokens, resets, w_x, w_z, w_bc, w_dt, dt_bias, decay_rate, d_skip, norm_gain, w_out):
    places = ("head", "seq_0", "seq_1")
    idx = jnp.stack([lax.axis_index(axis) for axis in places]).astype(jnp.int32)
    heads = w_dt.shape[1]
    left, right = shifted(tokens, "head", 1), shifted(tokens, "head", 3)
    w_dt = jnp.pad(w_dt.T, ((0, LANES - heads), (0, 0)))
    bias = jnp.pad(dt_bias, (0, LANES - heads)).reshape(1, LANES)
    rate = jnp.pad(decay_rate, (0, LANES - heads)).reshape(1, LANES)
    starts = jnp.broadcast_to(resets.astype(F32)[:, None], (ROWS, LANES))
    skip = jnp.repeat(d_skip, HEADDIM).reshape(1, WIDTH)
    gain = norm_gain.reshape(1, WIDTH)

    acc_x, acc_bd, w_x, w_z, w_bc = load_weights(idx, tokens, w_dt, w_x, w_z, w_bc)
    left, right, acc_x = lax.optimization_barrier((left, right, acc_x))
    far = [shifted(left[:GROUP], "head", 1), shifted(right[GROUP:], "head", 3)]
    sums = project(1, idx, left, w_x, w_bc, w_dt, (acc_x, acc_bd))
    sums = project(3, idx, right, w_x, w_bc, w_dt, sums)
    acc_z = gate_part(idx, (tokens, left, right), w_z)
    far, acc_z, sums = lax.optimization_barrier((far, acc_z, sums))
    inner, b, c, cum, step, first, thr, *messages = device_state(
        idx, far, w_x, w_bc, w_dt, sums, starts, bias, rate
    )
    quarters = [messages[0], *(shifted(messages[d], "seq_1", d) for d in (1, 2, 3))]
    u0, e0 = mix(0, idx, inner, b, c, cum, step, skip)
    quarters, u0, e0, cum = lax.optimization_barrier((quarters, u0, e0, cum))
    total = row_total(idx, quarters)
    totals = [total, *(shifted(total, "seq_0", d) for d in (1, 2, 3))]
    u1, e1 = mix(1, idx, inner, b, c, cum, step, skip)
    totals, u1, e1, w_z = lax.optimization_barrier((totals, u1, e1, w_z))
    parts = prefixes(idx, quarters, totals)
    parts = [parts[0], *(shifted(parts[d], "seq_1", d) for d in (1, 2, 3))]
    zs = gate(idx, far, w_z, acc_z)
    block_0, sums_0, half_0 = gated_rows(0, idx, parts, first, thr, c, u0, e0, zs, gain, w_out)
    half_0 = shifted(half_0, "head", 1)
    block_1, sums_1, half_1 = gated_rows(1, idx, parts, first, thr, c, u1, e1, zs, gain, w_out)
    half_1 = shifted(half_1, "head", 3)
    right_0 = shifted(out_send(3, idx, block_0, sums_0, w_out), "head", 3)
    left_1 = shifted(out_send(1, idx, block_1, sums_1, w_out), "head", 1)
    near_0, near_1 = out_part(1, idx, block_0, w_out), out_part(3, idx, block_1, w_out)
    left_0 = shifted(join(idx, near_0, sums_0, half_0), "head", 1)
    right_1 = shifted(join(idx, near_1, sums_1, half_1), "head", 3)
    owns = [out_part(0, idx, block, w_out) for block in (block_0, block_1)]
    return norm(idx, owns, (sums_0, sums_1), (left_0, left_1), (right_0, right_1))


def solution(mesh):
    split = Mesh(
        mesh.devices.reshape(4, 4, mesh.shape["head"], mesh.shape["batch"]),
        ("seq_0", "seq_1", "head", "batch"),
    )
    placed = (
        P(BATCH_SEQ, "head"),
        P(BATCH_SEQ),
        P(None, "head"),
        P(None, "head"),
        P(),
        P(None, "head"),
        P("head"),
        P("head"),
        P("head"),
        P("head"),
        P("head", None),
    )
    return jax.shard_map(
        on_device, mesh=split, in_specs=placed, out_specs=P(BATCH_SEQ, "head"), check_vma=False
    )
```

```python
import functools

import jax
import jax.numpy as jnp
from jax import lax
from jax.experimental import pallas as pl
from jax.experimental.pallas import tpu as pltpu
from jax.sharding import Mesh
from jax.sharding import PartitionSpec as P

DI = 5120
HEADDIM = 64
NSTATE = 128
GROUP = 256
ROWS = 512
FEAT = 640
WIDTH = 1280
TILE = 256
STEPS = WIDTH // TILE
PER = TILE // HEADDIM
LANES = 128
BD = 384
QUARTER = NSTATE // 4
MSG = WIDTH + LANES
HALFROWS = GROUP + 16
LOG2E = 1.4426950408889634
BATCH_SEQ = ("batch", "seq_0", "seq_1")
F32 = jnp.float32
BF16 = jnp.bfloat16
MIB = 1 << 20


def dot(a, b):
    return lax.dot_general(a, b, (((1,), (0,)), ((), ())), preferred_element_type=F32)


def dot_nt(a, b):
    return lax.dot_general(a, b, (((1,), (1,)), ((), ())), preferred_element_type=F32)


def dot_tn(a, b):
    return lax.dot_general(a, b, (((0,), (0,)), ((), ())), preferred_element_type=F32)


def silu(v):
    return v / (1.0 + jnp.exp(-v))


def three(v):
    hi = v.astype(BF16)
    rest = v - hi.astype(F32)
    mid = rest.astype(BF16)
    return hi, mid, (rest - mid.astype(F32)).astype(BF16)


def swapped(array, axis, bits):
    return lax.ppermute(array, axis, [(i, i ^ bits) for i in range(4)])


VMEM = pl.BlockSpec(memory_space=pltpu.VMEM)
HBM = pl.BlockSpec(memory_space=pltpu.HBM)
SMEM = pl.BlockSpec(memory_space=pltpu.SMEM)


def cost(flops, nbytes, trans=0):
    return pl.CostEstimate(flops=int(flops), bytes_accessed=int(nbytes), transcendentals=int(trans))


def call(body, name, idx, args, outs, scratch=(), mib=16, flops=1e8, aliases=None, kept=True):
    args = [pltpu.with_memory_space_constraint(a, pltpu.VMEM) for a in args]
    made = [pltpu.VMEM(*o) if kept else jax.ShapeDtypeStruct(*o) for o in outs]
    return pl.pallas_call(
        body,
        in_specs=[SMEM, *[VMEM] * len(args)],
        out_specs=[VMEM] * len(outs),
        out_shape=made,
        scratch_shapes=[pltpu.VMEM(*s) for s in scratch],
        input_output_aliases=aliases or {},
        compiler_params=pltpu.CompilerParams(vmem_limit_bytes=mib * MIB),
        cost_estimate=cost(flops, 1e6),
        name=name,
    )(idx, *args)


def span(j, size=TILE):
    return slice(j * size, (j + 1) * size)


def block_of(idx, bits):
    owner = idx[0] ^ bits
    return pl.ds(pl.multiple_of(owner * FEAT, FEAT), FEAT)


def own_parts(idx, tokens, w_x, w_bc, w_dt, out_x, out_bd):
    feats = block_of(idx, 0)
    for j in range(STEPS):
        out_x[:, span(j)] = dot(tokens, w_x[feats, span(j)])
    out_bd[:, : 2 * NSTATE] = dot(tokens, w_bc[feats, :])
    out_bd[:, 2 * NSTATE :] = dot_nt(tokens, w_dt[:, feats])


def load_body(idx, tok, w_dt, w_x, w_z, w_bc, acc_x, acc_bd, v_x, v_z, v_bc, sems):
    copies = []
    for bits in range(4):
        feats = block_of(idx, bits)
        for source, target in ((w_x, v_x), (w_bc, v_bc)):
            sem = sems.at[len(copies)]
            copies.append(pltpu.make_async_copy(source.at[feats, :], target.at[feats, :], sem))
    copies.append(pltpu.make_async_copy(w_z, v_z, sems.at[len(copies)]))
    for copy in copies:
        copy.start()
    copies[0].wait()
    copies[1].wait()
    own_parts(idx, tok[...], v_x, v_bc, w_dt, acc_x, acc_bd)
    for copy in copies[2:]:
        copy.wait()


def load_weights(idx, tok, w_dt, w_x, w_z, w_bc):
    tok, w_dt = (pltpu.with_memory_space_constraint(a, pltpu.VMEM) for a in (tok, w_dt))
    return pl.pallas_call(
        load_body,
        in_specs=[SMEM, VMEM, VMEM, HBM, HBM, HBM],
        out_specs=[VMEM] * 5,
        out_shape=[
            pltpu.VMEM((ROWS, WIDTH), F32),
            pltpu.VMEM((ROWS, BD), F32),
            pltpu.VMEM(w_x.shape, BF16),
            pltpu.VMEM(w_z.shape, BF16),
            pltpu.VMEM(w_bc.shape, BF16),
        ],
        scratch_shapes=[pltpu.SemaphoreType.DMA((9,))],
        compiler_params=pltpu.CompilerParams(vmem_limit_bytes=36 * MIB),
        cost_estimate=cost(2 * ROWS * FEAT * (WIDTH + BD), 15e6),
        name="load_weights",
    )(idx, tok, w_dt, w_x, w_z, w_bc)


def project_body(idx, left, right, w_x, w_bc, w_dt, acc_x, acc_bd, out_x, out_bd):
    tokens = jnp.concatenate([left[...], right[...]], 1)
    one, other = block_of(idx, 1), block_of(idx, 3)
    for j in range(STEPS):
        weight = jnp.concatenate([w_x[one, span(j)], w_x[other, span(j)]], 0)
        out_x[:, span(j)] = acc_x[:, span(j)] + dot(tokens, weight)
    weight = jnp.concatenate([w_bc[one, :], w_bc[other, :]], 0)
    out_bd[:, : 2 * NSTATE] = acc_bd[:, : 2 * NSTATE] + dot(tokens, weight)
    weight = jnp.concatenate([w_dt[:, one], w_dt[:, other]], 1)
    out_bd[:, 2 * NSTATE :] = acc_bd[:, 2 * NSTATE :] + dot_nt(tokens, weight)


def project(idx, left, right, w_x, w_bc, w_dt, sums):
    return call(
        project_body,
        "project",
        idx,
        [left, right, w_x, w_bc, w_dt, *sums],
        [((ROWS, WIDTH), F32), ((ROWS, BD), F32)],
        flops=4 * ROWS * FEAT * (WIDTH + BD),
        aliases={6: 0, 7: 1},
    )


def head_rows(j):
    head = lax.broadcasted_iota(jnp.int32, (LANES, TILE), 0)
    channel = lax.broadcasted_iota(jnp.int32, (LANES, TILE), 1)
    return (head == PER * j + channel // HEADDIM).astype(BF16)


def terms(v, rows, width):
    hi, mid, lo = (part.astype(F32) for part in three(v))
    row = lax.broadcasted_iota(jnp.int32, (rows, width), 0)
    return jnp.where(row == 0, hi, jnp.where(row == 1, mid, jnp.where(row == 2, lo, 0.0)))


def state_body(
    idx, tok_0, tok_1, w_x, w_bc, w_dt, acc_x, acc_bd, resets, bias, rate,
    inner_o, b_o, c_o, cum_o, step_o, first_o, thr_o, m0, m1, m2, m3, state_s,
):
    tokens = jnp.concatenate([tok_0[...], tok_1[...]], 0)
    feats = block_of(idx, 2)
    mapped = silu(acc_bd[:, : 2 * NSTATE] + dot(tokens, w_bc[feats, :]))
    b_t = mapped[:, :NSTATE].T.astype(BF16)
    b_o[...] = mapped[:, :NSTATE].astype(BF16)
    c_o[...] = mapped[:, NSTATE:].astype(BF16)
    logits = acc_bd[:, 2 * NSTATE :] + dot_nt(tokens, w_dt[:, feats]) + bias[...]
    step = jnp.maximum(logits, 0.0) + jnp.log1p(jnp.exp(-jnp.abs(logits)))
    step_o[...] = step
    lane = lax.broadcasted_iota(jnp.int32, (ROWS, LANES), 1)
    decay = jnp.where(lane == LANES - 1, resets[...], -step * rate[...])
    row = lax.broadcasted_iota(jnp.int32, (GROUP, GROUP), 0)
    col = lax.broadcasted_iota(jnp.int32, (GROUP, GROUP), 1)
    lower = (row >= col).astype(BF16)
    keeps, throughs = [], []
    for g in range(2):
        hi, mid, lo = three(decay[span(g, GROUP)])
        cum = dot(lower, hi) + (dot(lower, mid) + dot(lower, lo))
        cum_o[span(g, GROUP), :] = cum
        last = cum[GROUP - 1 :, :]
        seg, closing = cum[:, LANES - 1 :], last[:, LANES - 1 :]
        keeps.append(jnp.where(seg == closing, jnp.exp(last - cum), 0.0) * step[span(g, GROUP)])
        throughs.append(jnp.where(closing == 0.0, jnp.exp(last), 0.0))
    keep = jnp.concatenate(keeps, 0)
    keep_hi = keep.astype(BF16)
    keep_lo = (keep - keep_hi.astype(F32)).astype(BF16)
    through = jnp.concatenate([terms(t, 8, LANES) for t in throughs], 0).astype(BF16)
    tail = terms(throughs[0] * throughs[1], QUARTER, LANES).astype(BF16)
    for j in range(STEPS):
        inner = silu(acc_x[:, span(j)] + dot(tokens, w_x[feats, span(j)])).astype(BF16)
        inner_o[:, span(j)] = inner
        heads = head_rows(j)
        wide = dot(keep_hi, heads) + dot(keep_lo, heads)
        scaled = (wide * inner.astype(F32)).astype(BF16)
        state0 = dot(b_t[:, :GROUP], scaled[:GROUP])
        state1 = dot(b_t[:, GROUP:], scaled[GROUP:])
        thr = dot(through, heads)
        thr0 = thr[0:1] + thr[1:2] + thr[2:3]
        thr1 = thr[8:9] + thr[9:10] + thr[10:11]
        first_o[:, span(j)] = state0
        thr_o[:, span(j)] = jnp.broadcast_to(thr0, (8, TILE))
        state_s[:, span(j)] = thr1 * state0 + state1
    for d, message in enumerate((m0, m1, m2, m3)):
        start = pl.multiple_of((idx[2] ^ d) * QUARTER, QUARTER)
        message[:, :WIDTH] = state_s[pl.ds(start, QUARTER), :].astype(BF16)
        message[:, WIDTH:] = tail


def device_state(idx, far, w_x, w_bc, w_dt, sums, resets, bias, rate):
    small = (ROWS, LANES)
    return call(
        state_body,
        "device_state",
        idx,
        [*far, w_x, w_bc, w_dt, *sums, resets, bias, rate],
        [
            ((ROWS, WIDTH), BF16), (small, BF16), (small, BF16), (small, F32), (small, F32),
            ((NSTATE, WIDTH), F32), ((8, WIDTH), F32), *[((QUARTER, MSG), BF16)] * 4,
        ],
        [((NSTATE, WIDTH), F32)],
        flops=2 * ROWS * FEAT * (WIDTH + BD),
    )


def tail_of(message):
    tail = message[:, WIDTH:].astype(F32)
    return tail[0:1] + tail[1:2] + tail[2:3]


def decays_of(messages, j):
    tails = jnp.concatenate([m[:16, WIDTH:] for m in messages], 0)
    wide = dot(tails, head_rows(j))
    rows = range(0, 16 * len(messages), 16)
    return [wide[k : k + 1] + wide[k + 1 : k + 2] + wide[k + 2 : k + 3] for k in rows]


def total_body(idx, m0, m1, m2, m3, out, held):
    for d, message in enumerate((m0, m1, m2, m3)):
        held[idx[2] ^ d] = message[...]
    messages = [held.at[k] for k in range(4)]
    through = tail_of(messages[0])
    for message in messages[1:]:
        through = through * tail_of(message)
    out[:, WIDTH:] = terms(through, QUARTER, LANES).astype(BF16)
    for j in range(STEPS):
        decays = decays_of(messages, j)
        state = messages[0][:, span(j)].astype(F32)
        for k in range(1, 4):
            state = decays[k] * state + messages[k][:, span(j)].astype(F32)
        out[:, span(j)] = state.astype(BF16)


def prefix_body(idx, m0, m1, m2, m3, t0, t1, t2, t3, h0, h1, h2, h3, held, rows, found):
    for d, message in enumerate((m0, m1, m2, m3)):
        held[idx[2] ^ d] = message[...]
    for d, message in enumerate((t0, t1, t2, t3)):
        rows[idx[1] ^ d] = message[...]
    messages = [held.at[k] for k in range(4)]
    totals = [rows.at[k] for k in range(4)]
    for j in range(STEPS):
        decays = decays_of([*messages, *totals], j)
        state = jnp.zeros((QUARTER, TILE), F32)
        for k in range(3):
            after = decays[4 + k] * state + totals[k][:, span(j)].astype(F32)
            state = jnp.where(k < idx[1], after, state)
        for k in range(4):
            found[k, :, span(j)] = state.astype(BF16)
            if k < 3:
                state = decays[k] * state + messages[k][:, span(j)].astype(F32)
    for d, out in enumerate((h0, h1, h2, h3)):
        out[...] = found[idx[2] ^ d]


def row_total(idx, messages):
    return call(
        total_body,
        "row_total",
        idx,
        messages,
        [((QUARTER, MSG), BF16)],
        [((4, QUARTER, MSG), BF16)],
        mib=8,
    )[0]


def prefixes(idx, messages, totals):
    return call(
        prefix_body,
        "prefixes",
        idx,
        [*messages, *totals],
        [((QUARTER, WIDTH), BF16)] * 4,
        [((4, QUARTER, MSG), BF16), ((4, QUARTER, MSG), BF16), ((4, QUARTER, WIDTH), BF16)],
        mib=8,
    )


def gate_part_body(idx, t0, t1, t3, w_z, out):
    for j in range(STEPS):
        part = dot(t0[...], w_z[block_of(idx, 0), span(j)])
        for bits, tokens in ((1, t1), (3, t3)):
            part = part + dot(tokens[...], w_z[block_of(idx, bits), span(j)])
        out[:, span(j)] = part


def gate_part(idx, tokens, w_z):
    return call(
        gate_part_body,
        "gate_part",
        idx,
        [*tokens, w_z],
        [((ROWS, WIDTH), F32)],
        flops=6 * ROWS * FEAT * WIDTH,
    )[0]


def gate_body(idx, t_0, t_1, w_z, acc_z, out):
    tokens = jnp.concatenate([t_0[...], t_1[...]], 0)
    feats = block_of(idx, 2)
    for j in range(STEPS):
        gating = acc_z[:, span(j)] + dot(tokens, w_z[feats, span(j)])
        out[:, span(j)] = silu(gating.astype(BF16).astype(F32))


def gate(idx, far, w_z, acc_z):
    return call(
        gate_body,
        "gate",
        idx,
        [*far, w_z, acc_z],
        [((ROWS, WIDTH), F32)],
        flops=2 * ROWS * FEAT * WIDTH,
        aliases={4: 0},
    )[0]


def mix_body(g, idx, inner_r, b_r, c_r, cum_r, step_r, skip, out, ent_o, scores, cum_t, step_t):
    half = GROUP // 2
    rows = span(g, GROUP)
    cum = cum_r[rows, :]
    across = cum.T
    cum_2 = cum * LOG2E
    cum_t[...] = across * LOG2E
    step_t[...] = step_r[rows, :].T
    row = lax.broadcasted_iota(jnp.int32, (GROUP, GROUP), 0)
    col = lax.broadcasted_iota(jnp.int32, (GROUP, GROUP), 1)
    seg = cum[:, LANES - 1 :]
    same = (seg == across[LANES - 1 :, :]) & (row >= col)
    scores[...] = jnp.where(same, dot_nt(c_r[rows, :], b_r[rows, :]), 0.0)
    enter = jnp.where(seg == 0.0, jnp.exp(cum), 0.0)
    hi = enter.astype(BF16)
    lo = (enter - hi.astype(F32)).astype(BF16)
    lane = lax.broadcasted_iota(jnp.int32, (GROUP, LANES), 1)
    for j in range(STEPS):
        heads = head_rows(j)
        ent_o[:, span(j)] = dot(hi, heads) + dot(lo, heads)
    for pair in range(WIDTH // LANES):
        both = inner_r[rows, span(pair, LANES)]
        ys = []
        for head in (2 * pair, 2 * pair + 1):
            before = cum_t[head : head + 1, :]
            step = step_t[head : head + 1, :]
            top = jnp.exp2(jnp.minimum(cum_2[:half, head : head + 1] - before[:, :half], 0.0))
            top = (top * scores[:half, :half] * step[:, :half]).astype(BF16)
            low = jnp.exp2(jnp.minimum(cum_2[half:, head : head + 1] - before, 0.0))
            low = (low * scores[half:, :] * step).astype(BF16)
            ys.append(jnp.concatenate([dot(top, both[:half]), dot(low, both)], 0))
        y = jnp.where(lane < HEADDIM, ys[0], ys[1])
        out[:, span(pair, LANES)] = y + skip[:, span(pair, LANES)] * both.astype(F32)


def mix(g, idx, inner, b, c, cum, step, skip):
    return call(
        functools.partial(mix_body, g),
        "mix",
        idx,
        [inner, b, c, cum, step, skip],
        [((GROUP, WIDTH), F32), ((GROUP, WIDTH), F32)],
        [((GROUP, GROUP), F32), ((LANES, GROUP), F32), ((LANES, GROUP), F32)],
        flops=2e9,
    )


def block_cols(idx, bits):
    target = idx[0] ^ bits
    return pl.ds(pl.multiple_of(target * FEAT, FEAT), FEAT)


def squares_rows(total):
    width = total.shape[1]
    rows = terms(total, 16, width).astype(BF16)
    return jnp.concatenate([rows, jnp.zeros((16, FEAT - width), BF16)], 1)


def row_of(message, start, width):
    tail = message[start : start + 3, :width].astype(F32)
    return tail[0:1] + (tail[1:2] + tail[2:3])


def gated_body(
    idx, h0, h1, h2, h3, first, thr, c_r, u0, u1, e0, e1, zs_r, gain, w_out,
    rows_o, sums_o, top, low, state,
):
    for d, part in enumerate((h0, h1, h2, h3)):
        start = pl.multiple_of((idx[2] ^ d) * QUARTER, QUARTER)
        state[pl.ds(start, QUARTER), :] = part[...]
    ones = jnp.ones((8, LANES), BF16)
    for g, (u, ent) in enumerate(((u0, e0), (u1, e1))):
        rows = span(g, GROUP)
        squares = jnp.zeros((GROUP, LANES), F32)
        for j in range(STEPS):
            enter = state[:, span(j)]
            if g:
                enter = first[:, span(j)] + thr[0:1, span(j)] * enter.astype(F32)
                enter = enter.astype(BF16)
            carried = dot(c_r[rows, :], enter)
            gated = (u[:, span(j)] + ent[:, span(j)] * carried) * zs_r[rows, span(j)]
            rows_o[rows, span(j)] = (gated * gain[:, span(j)]).astype(BF16)
            square = gated * gated
            squares = squares + (square[:, :LANES] + square[:, LANES:])
        hi, mid, lo = three(squares)
        sums_o[:, rows] = dot_nt(ones, hi) + (dot_nt(ones, mid) + dot_nt(ones, lo))
    part = dot(rows_o[...], w_out[:, block_cols(idx, 2)]).astype(BF16)
    for g, out in enumerate((top, low)):
        out[:GROUP, :] = part[span(g, GROUP)]
        out[GROUP:, :] = squares_rows(sums_o[0:1, span(g, GROUP)])


def gated_rows(idx, parts, first, thr, c, us, ents, zs, gain, w_out):
    return call(
        gated_body,
        "gated_rows",
        idx,
        [*parts, first, thr, c, *us, *ents, zs, gain, w_out],
        [((ROWS, WIDTH), BF16), ((8, ROWS), F32), *[((HALFROWS, FEAT), BF16)] * 2],
        [((NSTATE, WIDTH), BF16)],
        flops=2.6 * ROWS * WIDTH * FEAT,
    )


def near_body(bits, g, idx, rows, sums, w_out, message, part):
    value = dot(rows[...], w_out[:, block_cols(idx, bits)])
    part[...] = value[span(g, GROUP)]
    message[:GROUP, :] = value[span(1 - g, GROUP)].astype(BF16)
    message[GROUP:, :] = squares_rows(sums[0:1, span(1 - g, GROUP)])


def near_block(bits, g, idx, rows, sums, w_out):
    return call(
        functools.partial(near_body, bits, g),
        "near_block",
        idx,
        [rows, sums, w_out],
        [((HALFROWS, FEAT), BF16), ((GROUP, FEAT), F32)],
        flops=2 * ROWS * WIDTH * FEAT,
    )


def own_body(idx, rows, w_out, out):
    out[...] = dot(rows[...], w_out[:, block_cols(idx, 0)])


def own_block(idx, rows, w_out):
    return call(
        own_body,
        "own_block",
        idx,
        [rows, w_out],
        [((ROWS, FEAT), F32)],
        flops=2 * ROWS * WIDTH * FEAT,
    )[0]


def join_body(g, idx, part, sums, half, out):
    out[:GROUP, :] = (part[...] + half[:GROUP, :].astype(F32)).astype(BF16)
    out[GROUP:, :] = squares_rows(sums[0:1, span(g, GROUP)] + row_of(half, GROUP, GROUP))


def join(g, idx, part, sums, half):
    return call(
        functools.partial(join_body, g),
        "join",
        idx,
        [part, sums, half],
        [((HALFROWS, FEAT), BF16)],
        mib=8,
    )[0]


def norm_body(idx, own, sums, left_0, left_1, right_0, right_1, out):
    for g, (left, right) in enumerate(((left_0, right_0), (left_1, right_1))):
        rows = span(g, GROUP)
        total = sums[0:1, rows] + (row_of(left, GROUP, GROUP) + row_of(right, GROUP, GROUP))
        stack = terms(total, 16, GROUP).astype(BF16)
        squares = dot_tn(stack, jnp.ones((16, LANES), BF16))
        factor = lax.rsqrt(squares / DI + 1e-05)
        for k in range(FEAT // LANES):
            lanes = span(k, LANES)
            value = left[:GROUP, lanes].astype(F32) + right[:GROUP, lanes].astype(F32)
            out[rows, lanes] = ((own[rows, lanes] + value) * factor).astype(BF16)


def norm(idx, own, sums, left, right):
    return call(
        norm_body,
        "norm",
        idx,
        [own, sums, *left, *right],
        [((ROWS, FEAT), BF16)],
        kept=False,
    )[0]


def on_device(tokens, resets, w_x, w_z, w_bc, w_dt, dt_bias, decay_rate, d_skip, norm_gain, w_out):
    places = ("head", "seq_0", "seq_1")
    idx = jnp.stack([lax.axis_index(axis) for axis in places]).astype(jnp.int32)
    heads = w_dt.shape[1]
    left, right = swapped(tokens, "head", 1), swapped(tokens, "head", 3)
    w_dt = jnp.pad(w_dt.T, ((0, LANES - heads), (0, 0)))
    bias = jnp.pad(dt_bias, (0, LANES - heads)).reshape(1, LANES)
    rate = jnp.pad(decay_rate, (0, LANES - heads)).reshape(1, LANES)
    starts = jnp.broadcast_to(resets.astype(F32)[:, None], (ROWS, LANES))
    skip = jnp.repeat(d_skip, HEADDIM).reshape(1, WIDTH)
    gain = norm_gain.reshape(1, WIDTH)

    acc_x, acc_bd, w_x, w_z, w_bc = load_weights(idx, tokens, w_dt, w_x, w_z, w_bc)
    left, right, acc_x = lax.optimization_barrier((left, right, acc_x))
    far = [swapped(left[:GROUP], "head", 3), swapped(right[GROUP:], "head", 1)]
    sums = project(idx, left, right, w_x, w_bc, w_dt, (acc_x, acc_bd))
    acc_z = gate_part(idx, (tokens, left, right), w_z)
    far, acc_z, sums = lax.optimization_barrier((far, acc_z, sums))
    inner, b, c, cum, step, first, thr, *messages = device_state(
        idx, far, w_x, w_bc, w_dt, sums, starts, bias, rate
    )
    quarters = [messages[0], *(swapped(messages[d], "seq_1", d) for d in (1, 2, 3))]
    u0, e0 = mix(0, idx, inner, b, c, cum, step, skip)
    quarters, u0, e0, cum = lax.optimization_barrier((quarters, u0, e0, cum))
    total = row_total(idx, quarters)
    totals = [total, *(swapped(total, "seq_0", d) for d in (1, 2, 3))]
    u1, e1 = mix(1, idx, inner, b, c, cum, step, skip)
    totals, u1, e1, w_z = lax.optimization_barrier((totals, u1, e1, w_z))
    parts = prefixes(idx, quarters, totals)
    parts = [parts[0], *(swapped(parts[d], "seq_1", d) for d in (1, 2, 3))]
    zs = gate(idx, far, w_z, acc_z)
    rows, sums, top, low = gated_rows(
        idx, parts, first, thr, c, (u0, u1), (e0, e1), zs, gain, w_out
    )
    top, low = swapped(top, "head", 1), swapped(low, "head", 3)
    left_0, part_1 = near_block(1, 1, idx, rows, sums, w_out)
    left_0 = swapped(left_0, "head", 1)
    right_1, part_0 = near_block(3, 0, idx, rows, sums, w_out)
    right_1 = swapped(right_1, "head", 3)
    own = own_block(idx, rows, w_out)
    right_0 = swapped(join(0, idx, part_0, sums, top), "head", 3)
    left_1 = swapped(join(1, idx, part_1, sums, low), "head", 1)
    return norm(idx, own, sums, (left_0, left_1), (right_0, right_1))


def solution(mesh):
    split = Mesh(
        mesh.devices.reshape(4, 4, mesh.shape["head"], mesh.shape["batch"]),
        ("seq_0", "seq_1", "head", "batch"),
    )
    placed = (
        P(BATCH_SEQ, "head"),
        P(BATCH_SEQ),
        P(None, "head"),
        P(None, "head"),
        P(),
        P(None, "head"),
        P("head"),
        P("head"),
        P("head"),
        P("head"),
        P("head", None),
    )
    return jax.shard_map(
        on_device, mesh=split, in_specs=placed, out_specs=P(BATCH_SEQ, "head"), check_vma=False
    )
```

```python
import functools

import jax
import jax.numpy as jnp
from jax import lax
from jax.experimental import pallas as pl
from jax.experimental.pallas import tpu as pltpu
from jax.sharding import Mesh
from jax.sharding import PartitionSpec as P

DI = 5120
HEADDIM = 64
NSTATE = 128
GROUP = 256
ROWS = 512
FEAT = 640
WIDTH = 1280
TILE = 256
STEPS = WIDTH // TILE
PER = TILE // HEADDIM
LANES = 128
BD = 384
TAILED = GROUP + 8
QUARTER = NSTATE // 4
MSG = WIDTH + LANES
LOG2E = 1.4426950408889634
BATCH_SEQ = ("batch", "seq_0", "seq_1")
F32 = jnp.float32
BF16 = jnp.bfloat16
MIB = 1 << 20


def dot(a, b):
    return lax.dot_general(a, b, (((1,), (0,)), ((), ())), preferred_element_type=F32)


def dot_nt(a, b):
    return lax.dot_general(a, b, (((1,), (1,)), ((), ())), preferred_element_type=F32)


def dot_tn(a, b):
    return lax.dot_general(a, b, (((0,), (0,)), ((), ())), preferred_element_type=F32)


def silu(v):
    return v / (1.0 + jnp.exp(-v))


def three(v):
    hi = v.astype(BF16)
    rest = v - hi.astype(F32)
    mid = rest.astype(BF16)
    return hi, mid, (rest - mid.astype(F32)).astype(BF16)


def swapped(array, axis, bits):
    return lax.ppermute(array, axis, [(i, i ^ bits) for i in range(4)])


VMEM = pl.BlockSpec(memory_space=pltpu.VMEM)
HBM = pl.BlockSpec(memory_space=pltpu.HBM)
SMEM = pl.BlockSpec(memory_space=pltpu.SMEM)


def cost(flops, nbytes, trans=0):
    return pl.CostEstimate(flops=int(flops), bytes_accessed=int(nbytes), transcendentals=int(trans))


def call(body, name, idx, args, outs, scratch=(), mib=16, flops=1e8, aliases=None, kept=True):
    args = [pltpu.with_memory_space_constraint(a, pltpu.VMEM) for a in args]
    made = [pltpu.VMEM(*o) if kept else jax.ShapeDtypeStruct(*o) for o in outs]
    return pl.pallas_call(
        body,
        in_specs=[SMEM, *[VMEM] * len(args)],
        out_specs=[VMEM] * len(outs),
        out_shape=made,
        scratch_shapes=[pltpu.VMEM(*s) for s in scratch],
        input_output_aliases=aliases or {},
        compiler_params=pltpu.CompilerParams(vmem_limit_bytes=mib * MIB),
        cost_estimate=cost(flops, 1e6),
        name=name,
    )(idx, *args)


def span(j, size=TILE):
    return slice(j * size, (j + 1) * size)


def block_of(idx, bits):
    owner = idx[0] ^ bits
    return pl.ds(pl.multiple_of(owner * FEAT, FEAT), FEAT)


def own_parts(idx, tokens, w_x, w_bc, w_dt, out_x, out_bd):
    feats = block_of(idx, 0)
    for j in range(STEPS):
        out_x[:, span(j)] = dot(tokens, w_x[feats, span(j)])
    out_bd[:, : 2 * NSTATE] = dot(tokens, w_bc[feats, :])
    out_bd[:, 2 * NSTATE :] = dot_nt(tokens, w_dt[:, feats])


def load_body(idx, w_dt, tok, w_x, w_z, w_bc, acc_x, acc_bd, v_tok, v_dt, v_x, v_z, v_bc, sems):
    copies = [pltpu.make_async_copy(tok, v_tok, sems.at[0])]
    for bits in range(4):
        feats = block_of(idx, bits)
        for source, target in ((w_x, v_x), (w_bc, v_bc)):
            sem = sems.at[len(copies)]
            copies.append(pltpu.make_async_copy(source.at[feats, :], target.at[feats, :], sem))
    copies.append(pltpu.make_async_copy(w_z, v_z, sems.at[len(copies)]))
    for copy in copies:
        copy.start()
    v_dt[...] = jnp.zeros_like(v_dt)
    v_dt[: w_dt.shape[0], :] = w_dt[...]
    for copy in copies[:3]:
        copy.wait()
    own_parts(idx, v_tok[...], v_x, v_bc, v_dt, acc_x, acc_bd)
    for copy in copies[3:]:
        copy.wait()


def load_weights(idx, tok, w_dt, w_x, w_z, w_bc):
    w_dt = pltpu.with_memory_space_constraint(w_dt, pltpu.VMEM)
    return pl.pallas_call(
        load_body,
        in_specs=[SMEM, VMEM, HBM, HBM, HBM, HBM],
        out_specs=[VMEM] * 7,
        out_shape=[
            pltpu.VMEM((ROWS, WIDTH), F32),
            pltpu.VMEM((ROWS, BD), F32),
            pltpu.VMEM(tok.shape, BF16),
            pltpu.VMEM((LANES, w_dt.shape[1]), BF16),
            pltpu.VMEM(w_x.shape, BF16),
            pltpu.VMEM(w_z.shape, BF16),
            pltpu.VMEM(w_bc.shape, BF16),
        ],
        scratch_shapes=[pltpu.SemaphoreType.DMA((10,))],
        compiler_params=pltpu.CompilerParams(vmem_limit_bytes=36 * MIB),
        cost_estimate=cost(2 * ROWS * FEAT * (WIDTH + BD), 15e6),
        name="load_weights",
    )(idx, w_dt, tok, w_x, w_z, w_bc)


def near_tokens(l_0, l_1, r_0, r_1):
    left = jnp.concatenate([l_0[...], l_1[...]], 0)
    return jnp.concatenate([left, jnp.concatenate([r_0[...], r_1[...]], 0)], 1)


def project_body(idx, l_0, l_1, r_0, r_1, w_x, w_bc, w_dt, acc_x, acc_bd, out_x, out_bd):
    tokens = near_tokens(l_0, l_1, r_0, r_1)
    one, other = block_of(idx, 1), block_of(idx, 3)
    for j in range(STEPS):
        weight = jnp.concatenate([w_x[one, span(j)], w_x[other, span(j)]], 0)
        out_x[:, span(j)] = acc_x[:, span(j)] + dot(tokens, weight)
    weight = jnp.concatenate([w_bc[one, :], w_bc[other, :]], 0)
    out_bd[:, : 2 * NSTATE] = acc_bd[:, : 2 * NSTATE] + dot(tokens, weight)
    weight = jnp.concatenate([w_dt[:, one], w_dt[:, other]], 1)
    out_bd[:, 2 * NSTATE :] = acc_bd[:, 2 * NSTATE :] + dot_nt(tokens, weight)


def project(idx, near, w_x, w_bc, w_dt, sums):
    return call(
        project_body,
        "project",
        idx,
        [*near, w_x, w_bc, w_dt, *sums],
        [((ROWS, WIDTH), F32), ((ROWS, BD), F32)],
        flops=4 * ROWS * FEAT * (WIDTH + BD),
        aliases={8: 0, 9: 1},
    )


def head_rows(j):
    head = lax.broadcasted_iota(jnp.int32, (LANES, TILE), 0)
    channel = lax.broadcasted_iota(jnp.int32, (LANES, TILE), 1)
    return (head == PER * j + channel // HEADDIM).astype(BF16)


def terms(v, rows, width):
    hi, mid, lo = (part.astype(F32) for part in three(v))
    row = lax.broadcasted_iota(jnp.int32, (rows, width), 0)
    return jnp.where(row == 0, hi, jnp.where(row == 1, mid, jnp.where(row == 2, lo, 0.0)))


def state_body(
    idx, tok_0, tok_1, w_x, w_bc, w_dt, acc_x, acc_bd, resets, bias, rate,
    inner_o, b_o, c_o, cum_o, step_o, first_o, thr_o, m0, m1, m2, m3, state_s,
):
    tokens = jnp.concatenate([tok_0[...], tok_1[...]], 0)
    feats = block_of(idx, 2)
    mapped = silu(acc_bd[:, : 2 * NSTATE] + dot(tokens, w_bc[feats, :]))
    b_t = mapped[:, :NSTATE].T.astype(BF16)
    b_o[...] = mapped[:, :NSTATE].astype(BF16)
    c_o[...] = mapped[:, NSTATE:].astype(BF16)
    logits = acc_bd[:, 2 * NSTATE :] + dot_nt(tokens, w_dt[:, feats]) + bias[...]
    step = jnp.maximum(logits, 0.0) + jnp.log1p(jnp.exp(-jnp.abs(logits)))
    step_o[...] = step
    lane = lax.broadcasted_iota(jnp.int32, (ROWS, LANES), 1)
    first_row = lax.broadcasted_iota(jnp.int32, (16, ROWS), 0) == 0
    marks = jnp.where(first_row, resets[...].astype(F32), 0.0).astype(BF16)
    marks = dot_tn(marks, jnp.ones((16, LANES), BF16))
    decay = jnp.where(lane == LANES - 1, marks, -step * rate[...])
    row = lax.broadcasted_iota(jnp.int32, (GROUP, GROUP), 0)
    col = lax.broadcasted_iota(jnp.int32, (GROUP, GROUP), 1)
    lower = (row >= col).astype(BF16)
    keeps, throughs = [], []
    for g in range(2):
        hi, mid, lo = three(decay[span(g, GROUP)])
        cum = dot(lower, hi) + (dot(lower, mid) + dot(lower, lo))
        cum_o[span(g, GROUP), :] = cum
        last = cum[GROUP - 1 :, :]
        seg, closing = cum[:, LANES - 1 :], last[:, LANES - 1 :]
        keeps.append(jnp.where(seg == closing, jnp.exp(last - cum), 0.0) * step[span(g, GROUP)])
        throughs.append(jnp.where(closing == 0.0, jnp.exp(last), 0.0))
    keep = jnp.concatenate(keeps, 0)
    keep_hi = keep.astype(BF16)
    keep_lo = (keep - keep_hi.astype(F32)).astype(BF16)
    through = jnp.concatenate([terms(t, 8, LANES) for t in throughs], 0).astype(BF16)
    tail = terms(throughs[0] * throughs[1], QUARTER, LANES).astype(BF16)
    for j in range(STEPS):
        inner = silu(acc_x[:, span(j)] + dot(tokens, w_x[feats, span(j)])).astype(BF16)
        inner_o[:, span(j)] = inner
        heads = head_rows(j)
        wide = dot(keep_hi, heads) + dot(keep_lo, heads)
        scaled = (wide * inner.astype(F32)).astype(BF16)
        state0 = dot(b_t[:, :GROUP], scaled[:GROUP])
        state1 = dot(b_t[:, GROUP:], scaled[GROUP:])
        thr = dot(through, heads)
        thr0 = thr[0:1] + thr[1:2] + thr[2:3]
        thr1 = thr[8:9] + thr[9:10] + thr[10:11]
        first_o[:, span(j)] = state0
        thr_o[:, span(j)] = jnp.broadcast_to(thr0, (8, TILE))
        state_s[:, span(j)] = thr1 * state0 + state1
    for d, message in enumerate((m0, m1, m2, m3)):
        start = pl.multiple_of((idx[2] ^ d) * QUARTER, QUARTER)
        message[:, :WIDTH] = state_s[pl.ds(start, QUARTER), :].astype(BF16)
        message[:, WIDTH:] = tail


def device_state(idx, far, w_x, w_bc, w_dt, sums, resets, bias, rate):
    small = (ROWS, LANES)
    return call(
        state_body,
        "device_state",
        idx,
        [*far, w_x, w_bc, w_dt, *sums, resets, bias, rate],
        [
            ((ROWS, WIDTH), BF16), (small, BF16), (small, BF16), (small, F32), (small, F32),
            ((NSTATE, WIDTH), F32), ((8, WIDTH), F32), *[((QUARTER, MSG), BF16)] * 4,
        ],
        [((NSTATE, WIDTH), F32)],
        flops=2 * ROWS * FEAT * (WIDTH + BD),
    )


def tail_of(message):
    tail = message[:, WIDTH:].astype(F32)
    return tail[0:1] + tail[1:2] + tail[2:3]


def decays_of(messages, j):
    tails = jnp.concatenate([m[:16, WIDTH:] for m in messages], 0)
    wide = dot(tails, head_rows(j))
    rows = range(0, 16 * len(messages), 16)
    return [wide[k : k + 1] + wide[k + 1 : k + 2] + wide[k + 2 : k + 3] for k in rows]


def total_body(idx, m0, m1, m2, m3, out, held):
    for d, message in enumerate((m0, m1, m2, m3)):
        held[idx[2] ^ d] = message[...]
    messages = [held.at[k] for k in range(4)]
    through = tail_of(messages[0])
    for message in messages[1:]:
        through = through * tail_of(message)
    out[:, WIDTH:] = terms(through, QUARTER, LANES).astype(BF16)
    for j in range(STEPS):
        decays = decays_of(messages, j)
        state = messages[0][:, span(j)].astype(F32)
        for k in range(1, 4):
            state = decays[k] * state + messages[k][:, span(j)].astype(F32)
        out[:, span(j)] = state.astype(BF16)


def prefix_body(idx, m0, m1, m2, m3, t0, t1, t2, t3, h0, h1, h2, h3, held, rows, found):
    for d, message in enumerate((m0, m1, m2, m3)):
        held[idx[2] ^ d] = message[...]
    for d, message in enumerate((t0, t1, t2, t3)):
        rows[idx[1] ^ d] = message[...]
    messages = [held.at[k] for k in range(4)]
    totals = [rows.at[k] for k in range(4)]
    for j in range(STEPS):
        decays = decays_of([*messages, *totals], j)
        state = jnp.zeros((QUARTER, TILE), F32)
        for k in range(3):
            after = decays[4 + k] * state + totals[k][:, span(j)].astype(F32)
            state = jnp.where(k < idx[1], after, state)
        for k in range(4):
            found[k, :, span(j)] = state.astype(BF16)
            if k < 3:
                state = decays[k] * state + messages[k][:, span(j)].astype(F32)
    for d, out in enumerate((h0, h1, h2, h3)):
        out[...] = found[idx[2] ^ d]


def row_total(idx, messages):
    return call(
        total_body,
        "row_total",
        idx,
        messages,
        [((QUARTER, MSG), BF16)],
        [((4, QUARTER, MSG), BF16)],
        mib=8,
    )[0]


def prefixes(idx, messages, totals):
    return call(
        prefix_body,
        "prefixes",
        idx,
        [*messages, *totals],
        [((QUARTER, WIDTH), BF16)] * 4,
        [((4, QUARTER, MSG), BF16), ((4, QUARTER, MSG), BF16), ((4, QUARTER, WIDTH), BF16)],
        mib=8,
    )


def gate_first_body(idx, tok, l_0, r_1, w_z, out):
    own, one, other = (block_of(idx, bits) for bits in (0, 1, 3))
    for j in range(STEPS):
        part = dot(tok[...], w_z[own, span(j)])
        out[:GROUP, span(j)] = part[:GROUP] + dot(l_0[...], w_z[one, span(j)])
        out[GROUP:, span(j)] = part[GROUP:] + dot(r_1[...], w_z[other, span(j)])


def gate_first(idx, tok, l_0, r_1, w_z):
    return call(
        gate_first_body,
        "gate_first",
        idx,
        [tok, l_0, r_1, w_z],
        [((ROWS, WIDTH), F32)],
        flops=4 * ROWS * FEAT * WIDTH,
    )[0]


def gate_second_body(idx, l_1, r_0, w_z, acc_z, out):
    one, other = block_of(idx, 1), block_of(idx, 3)
    for j in range(STEPS):
        out[:GROUP, span(j)] = acc_z[:GROUP, span(j)] + dot(r_0[...], w_z[other, span(j)])
        out[GROUP:, span(j)] = acc_z[GROUP:, span(j)] + dot(l_1[...], w_z[one, span(j)])


def gate_second(idx, l_1, r_0, w_z, acc_z):
    return call(
        gate_second_body,
        "gate_second",
        idx,
        [l_1, r_0, w_z, acc_z],
        [((ROWS, WIDTH), F32)],
        flops=2 * ROWS * FEAT * WIDTH,
        aliases={4: 0},
    )[0]


def gate_body(idx, t_0, t_1, w_z, acc_z, out):
    tokens = jnp.concatenate([t_0[...], t_1[...]], 0)
    feats = block_of(idx, 2)
    for j in range(STEPS):
        gating = acc_z[:, span(j)] + dot(tokens, w_z[feats, span(j)])
        out[:, span(j)] = silu(gating.astype(BF16).astype(F32))


def gate(idx, far, w_z, acc_z):
    return call(
        gate_body,
        "gate",
        idx,
        [*far, w_z, acc_z],
        [((ROWS, WIDTH), F32)],
        flops=2 * ROWS * FEAT * WIDTH,
        aliases={4: 0},
    )[0]


def mix_body(g, idx, inner_r, b_r, c_r, cum_r, step_r, skip, out, ent_o, scores, cum_t, step_t):
    half = GROUP // 2
    rows = span(g, GROUP)
    cum = cum_r[rows, :]
    across = cum.T
    cum_2 = cum * LOG2E
    cum_t[...] = across * LOG2E
    step_t[...] = step_r[rows, :].T
    row = lax.broadcasted_iota(jnp.int32, (GROUP, GROUP), 0)
    col = lax.broadcasted_iota(jnp.int32, (GROUP, GROUP), 1)
    seg = cum[:, LANES - 1 :]
    same = (seg == across[LANES - 1 :, :]) & (row >= col)
    scores[...] = jnp.where(same, dot_nt(c_r[rows, :], b_r[rows, :]), 0.0)
    enter = jnp.where(seg == 0.0, jnp.exp(cum), 0.0)
    hi = enter.astype(BF16)
    lo = (enter - hi.astype(F32)).astype(BF16)
    lane = lax.broadcasted_iota(jnp.int32, (GROUP, LANES), 1)
    for j in range(STEPS):
        heads = head_rows(j)
        ent_o[:, span(j)] = dot(hi, heads) + dot(lo, heads)
    for pair in range(WIDTH // LANES):
        both = inner_r[rows, span(pair, LANES)]
        ys = []
        for head in (2 * pair, 2 * pair + 1):
            before = cum_t[head : head + 1, :]
            step = step_t[head : head + 1, :]
            top = jnp.exp2(jnp.minimum(cum_2[:half, head : head + 1] - before[:, :half], 0.0))
            top = (top * scores[:half, :half] * step[:, :half]).astype(BF16)
            low = jnp.exp2(jnp.minimum(cum_2[half:, head : head + 1] - before, 0.0))
            low = (low * scores[half:, :] * step).astype(BF16)
            ys.append(jnp.concatenate([dot(top, both[:half]), dot(low, both)], 0))
        y = jnp.where(lane < HEADDIM, ys[0], ys[1])
        out[:, span(pair, LANES)] = y + skip[:, span(pair, LANES)] * both.astype(F32)


def mix(g, idx, inner, b, c, cum, step, skip):
    return call(
        functools.partial(mix_body, g),
        "mix",
        idx,
        [inner, b, c, cum, step, skip],
        [((GROUP, WIDTH), F32), ((GROUP, WIDTH), F32)],
        [((GROUP, GROUP), F32), ((LANES, GROUP), F32), ((LANES, GROUP), F32)],
        flops=2e9,
    )


def block_cols(idx, bits):
    target = idx[0] ^ bits
    return pl.ds(pl.multiple_of(target * FEAT, FEAT), FEAT)


def tail_rows(squares):
    zeros = jnp.zeros((8, FEAT - ROWS), F32)
    return jnp.concatenate([terms(squares, 8, ROWS), zeros], 1).astype(BF16)


def squares_of(message):
    tail = message[GROUP:, :ROWS].astype(F32)
    return tail[0:1] + (tail[1:2] + tail[2:3])


def gated_body(
    idx, h0, h1, h2, h3, first, thr, c_r, u0, u1, e0, e1, zs_r, gain, w_out,
    rows_o, sums_o, top, low, state,
):
    for d, part in enumerate((h0, h1, h2, h3)):
        start = pl.multiple_of((idx[2] ^ d) * QUARTER, QUARTER)
        state[pl.ds(start, QUARTER), :] = part[...]
    ones = jnp.ones((8, LANES), BF16)
    for g, (u, ent) in enumerate(((u0, e0), (u1, e1))):
        rows = span(g, GROUP)
        squares = jnp.zeros((GROUP, LANES), F32)
        for j in range(STEPS):
            enter = state[:, span(j)]
            if g:
                enter = first[:, span(j)] + thr[0:1, span(j)] * enter.astype(F32)
                enter = enter.astype(BF16)
            carried = dot(c_r[rows, :], enter)
            gated = (u[:, span(j)] + ent[:, span(j)] * carried) * zs_r[rows, span(j)]
            rows_o[rows, span(j)] = (gated * gain[:, span(j)]).astype(BF16)
            square = gated * gated
            squares = squares + (square[:, :LANES] + square[:, LANES:])
        hi, mid, lo = three(squares)
        sums_o[:, rows] = dot_nt(ones, hi) + (dot_nt(ones, mid) + dot_nt(ones, lo))
    part = dot(rows_o[...], w_out[:, block_cols(idx, 2)]).astype(BF16)
    tail = tail_rows(sums_o[0:1, :])
    for g, out in enumerate((top, low)):
        out[:GROUP, :] = part[span(g, GROUP)]
        out[GROUP:, :] = tail


def gated_rows(idx, parts, first, thr, c, us, ents, zs, gain, w_out):
    return call(
        gated_body,
        "gated_rows",
        idx,
        [*parts, first, thr, c, *us, *ents, zs, gain, w_out],
        [((ROWS, WIDTH), BF16), ((8, ROWS), F32), *[((TAILED, FEAT), BF16)] * 2],
        [((NSTATE, WIDTH), BF16)],
        flops=2.6 * ROWS * WIDTH * FEAT,
    )


def near_body(bits, g, idx, rows, w_out, message, part):
    value = dot(rows[...], w_out[:, block_cols(idx, bits)])
    part[...] = value[span(g, GROUP)]
    message[...] = value[span(1 - g, GROUP)].astype(BF16)


def near_block(bits, g, idx, rows, w_out):
    return call(
        functools.partial(near_body, bits, g),
        "near_block",
        idx,
        [rows, w_out],
        [((GROUP, FEAT), BF16), ((GROUP, FEAT), F32)],
        flops=1e6,
    )


def own_body(idx, rows, w_out, out):
    out[...] = dot(rows[...], w_out[:, block_cols(idx, 0)])


def own_block(idx, rows, w_out):
    return call(
        own_body,
        "own_block",
        idx,
        [rows, w_out],
        [((ROWS, FEAT), F32)],
        flops=1e6,
    )[0]


def join_body(idx, part, half, out):
    out[:GROUP, :] = (part[...] + half[:GROUP, :].astype(F32)).astype(BF16)
    out[GROUP:, :] = half[GROUP:, :]


def join(idx, part, half):
    return call(join_body, "join", idx, [part, half], [((TAILED, FEAT), BF16)], mib=8)[0]


def add_body(idx, own, left_0, right_1, out):
    out[:GROUP, :] = own[:GROUP, :] + left_0[...].astype(F32)
    out[GROUP:, :] = own[GROUP:, :] + right_1[...].astype(F32)


def add_near(idx, own, left_0, right_1):
    return call(
        add_body,
        "add_near",
        idx,
        [own, left_0, right_1],
        [((ROWS, FEAT), F32)],
        mib=8,
        flops=5e9,
        aliases={1: 0},
    )[0]


def norm_body(idx, own, sums, near, other, right_0, left_1, out, made, sems):
    squares = sums[0:1, :] + squares_of(right_0)
    squares = squares + (squares_of(near) + squares_of(other))
    stack = terms(squares, 16, ROWS).astype(BF16)
    factor = lax.rsqrt(dot_tn(stack, jnp.ones((16, LANES), BF16)) / DI + 1e-05)
    copies = []
    for g, last in enumerate((right_0, left_1)):
        rows = span(g, GROUP)
        for k in range(FEAT // LANES):
            lanes = span(k, LANES)
            value = own[rows, lanes] + last[:GROUP, lanes].astype(F32)
            made[rows, lanes] = (value * factor[rows]).astype(BF16)
        copies.append(pltpu.make_async_copy(made.at[rows, :], out.at[rows, :], sems.at[g]))
        copies[-1].start()
    for copy in copies:
        copy.wait()


def norm(idx, *args):
    args = [pltpu.with_memory_space_constraint(a, pltpu.VMEM) for a in args]
    return pl.pallas_call(
        norm_body,
        in_specs=[SMEM, *[VMEM] * len(args)],
        out_specs=HBM,
        out_shape=jax.ShapeDtypeStruct((ROWS, FEAT), BF16),
        scratch_shapes=[pltpu.VMEM((ROWS, FEAT), BF16), pltpu.SemaphoreType.DMA((2,))],
        compiler_params=pltpu.CompilerParams(vmem_limit_bytes=8 * MIB),
        cost_estimate=cost(1e6, 1e6),
        name="norm",
    )(idx, *args)


def on_device(tokens, resets, w_x, w_z, w_bc, w_dt, dt_bias, decay_rate, d_skip, norm_gain, w_out):
    places = ("head", "seq_0", "seq_1")
    idx = jnp.stack([lax.axis_index(axis) for axis in places]).astype(jnp.int32)
    heads = w_dt.shape[1]
    top, low = tokens[:GROUP], tokens[GROUP:]
    l_0, r_1 = swapped(top, "head", 1), swapped(low, "head", 3)
    l_1, r_0 = swapped(low, "head", 1), swapped(top, "head", 3)
    bias = jnp.pad(dt_bias, (0, LANES - heads)).reshape(1, LANES)
    rate = jnp.pad(decay_rate, (0, LANES - heads)).reshape(1, LANES)
    starts = resets.reshape(1, ROWS)
    skip = jnp.repeat(d_skip, HEADDIM).reshape(1, WIDTH)
    gain = norm_gain.reshape(1, WIDTH)

    acc_x, acc_bd, tokens, w_dt, w_x, w_z, w_bc = load_weights(
        idx, tokens, w_dt.T, w_x, w_z, w_bc
    )
    far = [swapped(l_0, "head", 3), swapped(r_1, "head", 1)]
    acc_z = gate_first(idx, tokens, l_0, r_1, w_z)
    near = (l_0, l_1, r_0, r_1)
    sums = project(idx, near, w_x, w_bc, w_dt, (acc_x, acc_bd))
    acc_z = gate_second(idx, l_1, r_0, w_z, acc_z)
    far, acc_z, sums = lax.optimization_barrier((far, acc_z, sums))
    inner, b, c, cum, step, first, thr, *messages = device_state(
        idx, far, w_x, w_bc, w_dt, sums, starts, bias, rate
    )
    quarters = [messages[0], *(swapped(messages[d], "seq_1", d) for d in (1, 2, 3))]
    u0, e0 = mix(0, idx, inner, b, c, cum, step, skip)
    quarters, u0, e0, cum = lax.optimization_barrier((quarters, u0, e0, cum))
    total = row_total(idx, quarters)
    totals = [total, *(swapped(total, "seq_0", d) for d in (1, 2, 3))]
    u1, e1 = mix(1, idx, inner, b, c, cum, step, skip)
    totals, u1, e1, w_z = lax.optimization_barrier((totals, u1, e1, w_z))
    parts = prefixes(idx, quarters, totals)
    parts = [parts[0], *(swapped(parts[d], "seq_1", d) for d in (1, 2, 3))]
    zs = gate(idx, far, w_z, acc_z)
    rows, sums, top, low = gated_rows(
        idx, parts, first, thr, c, (u0, u1), (e0, e1), zs, gain, w_out
    )
    top, low = swapped(top, "head", 1), swapped(low, "head", 3)
    left_0, part_1 = near_block(1, 1, idx, rows, w_out)
    left_0 = swapped(left_0, "head", 1)
    right_1, part_0 = near_block(3, 0, idx, rows, w_out)
    right_1 = swapped(right_1, "head", 3)
    own = own_block(idx, rows, w_out)
    right_0 = swapped(join(idx, part_0, top), "head", 3)
    left_1 = swapped(join(idx, part_1, low), "head", 1)
    own = add_near(idx, own, left_0, right_1)
    return norm(idx, own, sums, top, low, right_0, left_1)


def solution(mesh):
    split = Mesh(
        mesh.devices.reshape(4, 4, mesh.shape["head"], mesh.shape["batch"]),
        ("seq_0", "seq_1", "head", "batch"),
    )
    placed = (
        P(BATCH_SEQ, "head"),
        P(BATCH_SEQ),
        P(None, "head"),
        P(None, "head"),
        P(),
        P(None, "head"),
        P("head"),
        P("head"),
        P("head"),
        P("head"),
        P("head", None),
    )
    return jax.shard_map(
        on_device, mesh=split, in_specs=placed, out_specs=P(BATCH_SEQ, "head"), check_vma=False
    )
```

```python
import functools

import jax
import jax.numpy as jnp
from jax import lax
from jax.experimental import pallas as pl
from jax.experimental.pallas import tpu as pltpu
from jax.sharding import Mesh
from jax.sharding import PartitionSpec as P

DI = 5120
HEADDIM = 64
NSTATE = 128
GROUP = 256
ROWS = 512
FEAT = 640
WIDTH = 1280
TILE = 256
STEPS = WIDTH // TILE
PER = TILE // HEADDIM
LANES = 128
BD = 384
TAILED = GROUP + 8
QUARTER = NSTATE // 4
MSG = WIDTH + LANES
LOG2E = 1.4426950408889634
BATCH_SEQ = ("batch", "seq_0", "seq_1")
F32 = jnp.float32
BF16 = jnp.bfloat16
MIB = 1 << 20


def dot(a, b):
    return lax.dot_general(a, b, (((1,), (0,)), ((), ())), preferred_element_type=F32)


def dot_nt(a, b):
    return lax.dot_general(a, b, (((1,), (1,)), ((), ())), preferred_element_type=F32)


def dot_tn(a, b):
    return lax.dot_general(a, b, (((0,), (0,)), ((), ())), preferred_element_type=F32)


def silu(v):
    return v / (1.0 + jnp.exp(-v))


def three(v):
    hi = v.astype(BF16)
    rest = v - hi.astype(F32)
    mid = rest.astype(BF16)
    return hi, mid, (rest - mid.astype(F32)).astype(BF16)


def swapped(array, axis, bits):
    return lax.ppermute(array, axis, [(i, i ^ bits) for i in range(4)])


VMEM = pl.BlockSpec(memory_space=pltpu.VMEM)
HBM = pl.BlockSpec(memory_space=pltpu.HBM)
SMEM = pl.BlockSpec(memory_space=pltpu.SMEM)


def cost(flops, nbytes, trans=0):
    return pl.CostEstimate(flops=int(flops), bytes_accessed=int(nbytes), transcendentals=int(trans))


def call(body, name, idx, args, outs, scratch=(), mib=16, flops=1e8, aliases=None, kept=True):
    args = [pltpu.with_memory_space_constraint(a, pltpu.VMEM) for a in args]
    made = [pltpu.VMEM(*o) if kept else jax.ShapeDtypeStruct(*o) for o in outs]
    return pl.pallas_call(
        body,
        in_specs=[SMEM, *[VMEM] * len(args)],
        out_specs=[VMEM] * len(outs),
        out_shape=made,
        scratch_shapes=[pltpu.VMEM(*s) for s in scratch],
        input_output_aliases=aliases or {},
        compiler_params=pltpu.CompilerParams(vmem_limit_bytes=mib * MIB),
        cost_estimate=cost(flops, 1e6),
        name=name,
    )(idx, *args)


def span(j, size=TILE):
    return slice(j * size, (j + 1) * size)


def block_of(idx, bits):
    owner = idx[0] ^ bits
    return pl.ds(pl.multiple_of(owner * FEAT, FEAT), FEAT)


def own_parts(idx, tokens, w_x, w_bc, w_dt, out_x, out_bd):
    feats = block_of(idx, 0)
    for j in range(STEPS):
        out_x[:, span(j)] = dot(tokens, w_x[feats, span(j)])
    out_bd[:, : 2 * NSTATE] = dot(tokens, w_bc[feats, :])
    out_bd[:, 2 * NSTATE :] = dot_nt(tokens, w_dt[:, feats])


def load_body(
    idx, w_dt, tok, w_x, w_z, w_bc, acc_x, acc_bd, v_tok, v_dt, v_x, v_z, v_bc, narrow, sems
):
    copies = [
        pltpu.make_async_copy(w_dt, narrow, sems.at[0]),
        pltpu.make_async_copy(tok, v_tok, sems.at[1]),
    ]
    for bits in range(4):
        feats = block_of(idx, bits)
        for source, target in ((w_x, v_x), (w_bc, v_bc)):
            sem = sems.at[len(copies)]
            copies.append(pltpu.make_async_copy(source.at[feats, :], target.at[feats, :], sem))
    copies.append(pltpu.make_async_copy(w_z, v_z, sems.at[len(copies)]))
    for copy in copies:
        copy.start()
    v_dt[...] = jnp.zeros_like(v_dt)
    copies[0].wait()
    v_dt[: w_dt.shape[0], :] = narrow[...]
    for copy in copies[1:4]:
        copy.wait()
    own_parts(idx, v_tok[...], v_x, v_bc, v_dt, acc_x, acc_bd)
    for copy in copies[4:]:
        copy.wait()


def load_weights(idx, tok, w_dt, w_x, w_z, w_bc):
    return pl.pallas_call(
        load_body,
        in_specs=[SMEM, *[HBM] * 5],
        out_specs=[VMEM] * 7,
        out_shape=[
            pltpu.VMEM((ROWS, WIDTH), F32),
            pltpu.VMEM((ROWS, BD), F32),
            pltpu.VMEM(tok.shape, BF16),
            pltpu.VMEM((LANES, w_dt.shape[1]), BF16),
            pltpu.VMEM(w_x.shape, BF16),
            pltpu.VMEM(w_z.shape, BF16),
            pltpu.VMEM(w_bc.shape, BF16),
        ],
        scratch_shapes=[pltpu.VMEM(w_dt.shape, BF16), pltpu.SemaphoreType.DMA((11,))],
        compiler_params=pltpu.CompilerParams(vmem_limit_bytes=36 * MIB),
        cost_estimate=cost(2 * ROWS * FEAT * (WIDTH + BD), 15e6),
        name="load_weights",
    )(idx, w_dt, tok, w_x, w_z, w_bc)


def near_tokens(l_0, l_1, r_0, r_1):
    left = jnp.concatenate([l_0[...], l_1[...]], 0)
    return jnp.concatenate([left, jnp.concatenate([r_0[...], r_1[...]], 0)], 1)


def project_body(idx, l_0, l_1, r_0, r_1, w_x, w_bc, w_dt, acc_x, acc_bd, out_x, out_bd):
    tokens = near_tokens(l_0, l_1, r_0, r_1)
    one, other = block_of(idx, 1), block_of(idx, 3)
    for j in range(STEPS):
        weight = jnp.concatenate([w_x[one, span(j)], w_x[other, span(j)]], 0)
        out_x[:, span(j)] = acc_x[:, span(j)] + dot(tokens, weight)
    weight = jnp.concatenate([w_bc[one, :], w_bc[other, :]], 0)
    out_bd[:, : 2 * NSTATE] = acc_bd[:, : 2 * NSTATE] + dot(tokens, weight)
    weight = jnp.concatenate([w_dt[:, one], w_dt[:, other]], 1)
    out_bd[:, 2 * NSTATE :] = acc_bd[:, 2 * NSTATE :] + dot_nt(tokens, weight)


def project(idx, near, w_x, w_bc, w_dt, sums):
    return call(
        project_body,
        "project",
        idx,
        [*near, w_x, w_bc, w_dt, *sums],
        [((ROWS, WIDTH), F32), ((ROWS, BD), F32)],
        flops=4 * ROWS * FEAT * (WIDTH + BD),
        aliases={8: 0, 9: 1},
    )


def head_rows(j):
    head = lax.broadcasted_iota(jnp.int32, (LANES, TILE), 0)
    channel = lax.broadcasted_iota(jnp.int32, (LANES, TILE), 1)
    return (head == PER * j + channel // HEADDIM).astype(BF16)


def terms(v, rows, width):
    hi, mid, lo = (part.astype(F32) for part in three(v))
    row = lax.broadcasted_iota(jnp.int32, (rows, width), 0)
    return jnp.where(row == 0, hi, jnp.where(row == 1, mid, jnp.where(row == 2, lo, 0.0)))


def state_body(
    idx, tok_0, tok_1, w_x, w_bc, w_dt, acc_x, acc_bd, resets, bias, rate,
    inner_o, b_o, c_o, cum_o, step_o, first_o, thr_o, m0, m1, m2, m3, state_s,
):
    tokens = jnp.concatenate([tok_0[...], tok_1[...]], 0)
    feats = block_of(idx, 2)
    mapped = silu(acc_bd[:, : 2 * NSTATE] + dot(tokens, w_bc[feats, :]))
    b_t = mapped[:, :NSTATE].T.astype(BF16)
    b_o[...] = mapped[:, :NSTATE].astype(BF16)
    c_o[...] = mapped[:, NSTATE:].astype(BF16)
    logits = acc_bd[:, 2 * NSTATE :] + dot_nt(tokens, w_dt[:, feats]) + bias[...]
    step = jnp.maximum(logits, 0.0) + jnp.log1p(jnp.exp(-jnp.abs(logits)))
    step_o[...] = step
    lane = lax.broadcasted_iota(jnp.int32, (ROWS, LANES), 1)
    first_row = lax.broadcasted_iota(jnp.int32, (16, ROWS), 0) == 0
    marks = jnp.where(first_row, resets[...].astype(F32), 0.0).astype(BF16)
    marks = dot_tn(marks, jnp.ones((16, LANES), BF16))
    decay = jnp.where(lane == LANES - 1, marks, -step * rate[...])
    row = lax.broadcasted_iota(jnp.int32, (GROUP, GROUP), 0)
    col = lax.broadcasted_iota(jnp.int32, (GROUP, GROUP), 1)
    lower = (row >= col).astype(BF16)
    keeps, throughs = [], []
    for g in range(2):
        sums = dot(lower, jnp.concatenate(three(decay[span(g, GROUP)]), 1))
        cum = sums[:, :LANES] + (sums[:, LANES : 2 * LANES] + sums[:, 2 * LANES :])
        cum_o[span(g, GROUP), :] = cum
        last = cum[GROUP - 1 :, :]
        seg, closing = cum[:, LANES - 1 :], last[:, LANES - 1 :]
        keeps.append(jnp.where(seg == closing, jnp.exp(last - cum), 0.0) * step[span(g, GROUP)])
        throughs.append(jnp.where(closing == 0.0, jnp.exp(last), 0.0))
    keep = jnp.concatenate(keeps, 0)
    keep_hi = keep.astype(BF16)
    keep_lo = (keep - keep_hi.astype(F32)).astype(BF16)
    keep = jnp.concatenate([keep_hi, keep_lo], 1)
    through = jnp.concatenate([terms(t, 8, LANES) for t in throughs], 0).astype(BF16)
    tail = terms(throughs[0] * throughs[1], QUARTER, LANES).astype(BF16)
    for j in range(STEPS):
        inner = silu(acc_x[:, span(j)] + dot(tokens, w_x[feats, span(j)])).astype(BF16)
        inner_o[:, span(j)] = inner
        heads = head_rows(j)
        wide = dot(keep, jnp.concatenate([heads, heads], 0))
        scaled = (wide * inner.astype(F32)).astype(BF16)
        state0 = dot(b_t[:, :GROUP], scaled[:GROUP])
        state1 = dot(b_t[:, GROUP:], scaled[GROUP:])
        thr = dot(through, heads)
        thr0 = thr[0:1] + thr[1:2] + thr[2:3]
        thr1 = thr[8:9] + thr[9:10] + thr[10:11]
        first_o[:, span(j)] = state0
        thr_o[:, span(j)] = jnp.broadcast_to(thr0, (8, TILE))
        state_s[:, span(j)] = thr1 * state0 + state1
    for d, message in enumerate((m0, m1, m2, m3)):
        start = pl.multiple_of((idx[2] ^ d) * QUARTER, QUARTER)
        message[:, :WIDTH] = state_s[pl.ds(start, QUARTER), :].astype(BF16)
        message[:, WIDTH:] = tail


def device_state(idx, far, w_x, w_bc, w_dt, sums, resets, bias, rate):
    small = (ROWS, LANES)
    return call(
        state_body,
        "device_state",
        idx,
        [*far, w_x, w_bc, w_dt, *sums, resets, bias, rate],
        [
            ((ROWS, WIDTH), BF16), (small, BF16), (small, BF16), (small, F32), (small, F32),
            ((NSTATE, WIDTH), F32), ((8, WIDTH), F32), *[((QUARTER, MSG), BF16)] * 4,
        ],
        [((NSTATE, WIDTH), F32)],
        flops=2 * ROWS * FEAT * (WIDTH + BD),
    )


def tail_of(message):
    tail = message[:, WIDTH:].astype(F32)
    return tail[0:1] + tail[1:2] + tail[2:3]


def decays_of(messages, j):
    tails = jnp.concatenate([m[:16, WIDTH:] for m in messages], 0)
    wide = dot(tails, head_rows(j))
    rows = range(0, 16 * len(messages), 16)
    return [wide[k : k + 1] + wide[k + 1 : k + 2] + wide[k + 2 : k + 3] for k in rows]


def total_body(idx, m0, m1, m2, m3, out, held):
    for d, message in enumerate((m0, m1, m2, m3)):
        held[idx[2] ^ d] = message[...]
    messages = [held.at[k] for k in range(4)]
    through = tail_of(messages[0])
    for message in messages[1:]:
        through = through * tail_of(message)
    out[:, WIDTH:] = terms(through, QUARTER, LANES).astype(BF16)
    for j in range(STEPS):
        decays = decays_of(messages, j)
        state = messages[0][:, span(j)].astype(F32)
        for k in range(1, 4):
            state = decays[k] * state + messages[k][:, span(j)].astype(F32)
        out[:, span(j)] = state.astype(BF16)


def prefix_body(idx, m0, m1, m2, m3, t0, t1, t2, t3, h0, h1, h2, h3, held, rows, found):
    for d, message in enumerate((m0, m1, m2, m3)):
        held[idx[2] ^ d] = message[...]
    for d, message in enumerate((t0, t1, t2, t3)):
        rows[idx[1] ^ d] = message[...]
    messages = [held.at[k] for k in range(4)]
    totals = [rows.at[k] for k in range(4)]
    for j in range(STEPS):
        decays = decays_of([*messages, *totals], j)
        state = jnp.zeros((QUARTER, TILE), F32)
        for k in range(3):
            after = decays[4 + k] * state + totals[k][:, span(j)].astype(F32)
            state = jnp.where(k < idx[1], after, state)
        for k in range(4):
            found[k, :, span(j)] = state.astype(BF16)
            if k < 3:
                state = decays[k] * state + messages[k][:, span(j)].astype(F32)
    for d, out in enumerate((h0, h1, h2, h3)):
        out[...] = found[idx[2] ^ d]


def row_total(idx, messages):
    return call(
        total_body,
        "row_total",
        idx,
        messages,
        [((QUARTER, MSG), BF16)],
        [((4, QUARTER, MSG), BF16)],
        mib=8,
    )[0]


def prefixes(idx, messages, totals):
    return call(
        prefix_body,
        "prefixes",
        idx,
        [*messages, *totals],
        [((QUARTER, WIDTH), BF16)] * 4,
        [((4, QUARTER, MSG), BF16), ((4, QUARTER, MSG), BF16), ((4, QUARTER, WIDTH), BF16)],
        mib=8,
    )


def gate_first_body(idx, tok, l_0, r_1, w_z, out):
    own, one, other = (block_of(idx, bits) for bits in (0, 1, 3))
    for j in range(STEPS):
        part = dot(tok[...], w_z[own, span(j)])
        out[:GROUP, span(j)] = part[:GROUP] + dot(l_0[...], w_z[one, span(j)])
        out[GROUP:, span(j)] = part[GROUP:] + dot(r_1[...], w_z[other, span(j)])


def gate_first(idx, tok, l_0, r_1, w_z):
    return call(
        gate_first_body,
        "gate_first",
        idx,
        [tok, l_0, r_1, w_z],
        [((ROWS, WIDTH), F32)],
        flops=4 * ROWS * FEAT * WIDTH,
    )[0]


def gate_second_body(idx, l_1, r_0, w_z, acc_z, out):
    one, other = block_of(idx, 1), block_of(idx, 3)
    for j in range(STEPS):
        out[:GROUP, span(j)] = acc_z[:GROUP, span(j)] + dot(r_0[...], w_z[other, span(j)])
        out[GROUP:, span(j)] = acc_z[GROUP:, span(j)] + dot(l_1[...], w_z[one, span(j)])


def gate_second(idx, l_1, r_0, w_z, acc_z):
    return call(
        gate_second_body,
        "gate_second",
        idx,
        [l_1, r_0, w_z, acc_z],
        [((ROWS, WIDTH), F32)],
        flops=2 * ROWS * FEAT * WIDTH,
        aliases={4: 0},
    )[0]


def gate_body(idx, t_0, t_1, w_z, acc_z, out):
    tokens = jnp.concatenate([t_0[...], t_1[...]], 0)
    feats = block_of(idx, 2)
    for j in range(STEPS):
        gating = acc_z[:, span(j)] + dot(tokens, w_z[feats, span(j)])
        out[:, span(j)] = silu(gating.astype(BF16).astype(F32))


def gate(idx, far, w_z, acc_z):
    return call(
        gate_body,
        "gate",
        idx,
        [*far, w_z, acc_z],
        [((ROWS, WIDTH), F32)],
        flops=2 * ROWS * FEAT * WIDTH,
        aliases={4: 0},
    )[0]


def mix_body(g, idx, inner_r, b_r, c_r, cum_r, step_r, skip, out, ent_o, scores, cum_t, step_t):
    half = GROUP // 2
    rows = span(g, GROUP)
    cum = cum_r[rows, :]
    across = cum.T
    cum_2 = cum * LOG2E
    cum_t[...] = across * LOG2E
    step_t[...] = step_r[rows, :].T
    row = lax.broadcasted_iota(jnp.int32, (GROUP, GROUP), 0)
    col = lax.broadcasted_iota(jnp.int32, (GROUP, GROUP), 1)
    seg = cum[:, LANES - 1 :]
    same = (seg == across[LANES - 1 :, :]) & (row >= col)
    scores[...] = jnp.where(same, dot_nt(c_r[rows, :], b_r[rows, :]), 0.0)
    enter = jnp.where(seg == 0.0, jnp.exp(cum), 0.0)
    hi = enter.astype(BF16)
    lo = (enter - hi.astype(F32)).astype(BF16)
    lane = lax.broadcasted_iota(jnp.int32, (GROUP, LANES), 1)
    skips = []
    for j in range(STEPS):
        heads = head_rows(j)
        ent_o[:, span(j)] = dot(hi, heads) + dot(lo, heads)
        wide = dot(terms(skip[...], 16, LANES).astype(BF16), heads)
        wide = wide[0:1] + wide[1:2] + wide[2:3]
        skips += [wide[:, :LANES], wide[:, LANES:]]
    for pair in range(WIDTH // LANES):
        both = inner_r[rows, span(pair, LANES)]
        ys = []
        for head in (2 * pair, 2 * pair + 1):
            before = cum_t[head : head + 1, :]
            step = step_t[head : head + 1, :]
            top = jnp.exp2(jnp.minimum(cum_2[:half, head : head + 1] - before[:, :half], 0.0))
            top = (top * scores[:half, :half] * step[:, :half]).astype(BF16)
            low = jnp.exp2(jnp.minimum(cum_2[half:, head : head + 1] - before, 0.0))
            low = (low * scores[half:, :] * step).astype(BF16)
            ys.append(jnp.concatenate([dot(top, both[:half]), dot(low, both)], 0))
        y = jnp.where(lane < HEADDIM, ys[0], ys[1])
        out[:, span(pair, LANES)] = y + skips[pair] * both.astype(F32)


def mix(g, idx, inner, b, c, cum, step, skip):
    return call(
        functools.partial(mix_body, g),
        "mix",
        idx,
        [inner, b, c, cum, step, skip],
        [((GROUP, WIDTH), F32), ((GROUP, WIDTH), F32)],
        [((GROUP, GROUP), F32), ((LANES, GROUP), F32), ((LANES, GROUP), F32)],
        flops=2e9,
    )


def block_cols(idx, bits):
    target = idx[0] ^ bits
    return pl.ds(pl.multiple_of(target * FEAT, FEAT), FEAT)


def tail_rows(squares):
    zeros = jnp.zeros((8, FEAT - ROWS), F32)
    return jnp.concatenate([terms(squares, 8, ROWS), zeros], 1).astype(BF16)


def squares_of(message):
    tail = message[GROUP:, :ROWS].astype(F32)
    return tail[0:1] + (tail[1:2] + tail[2:3])


def gated_body(
    idx, h0, h1, h2, h3, first, thr, c_r, u0, u1, e0, e1, zs_r, gain, w_out,
    rows_o, sums_o, top, low, state,
):
    for d, part in enumerate((h0, h1, h2, h3)):
        start = pl.multiple_of((idx[2] ^ d) * QUARTER, QUARTER)
        state[pl.ds(start, QUARTER), :] = part[...]
    ones = jnp.ones((8, LANES), BF16)
    for g, (u, ent) in enumerate(((u0, e0), (u1, e1))):
        rows = span(g, GROUP)
        squares = jnp.zeros((GROUP, LANES), F32)
        for j in range(STEPS):
            enter = state[:, span(j)]
            if g:
                enter = first[:, span(j)] + thr[0:1, span(j)] * enter.astype(F32)
                enter = enter.astype(BF16)
            carried = dot(c_r[rows, :], enter)
            gated = (u[:, span(j)] + ent[:, span(j)] * carried) * zs_r[rows, span(j)]
            rows_o[rows, span(j)] = (gated * gain[:, span(j)]).astype(BF16)
            square = gated * gated
            squares = squares + (square[:, :LANES] + square[:, LANES:])
        hi, mid, lo = three(squares)
        sums_o[:, rows] = dot_nt(ones, hi) + (dot_nt(ones, mid) + dot_nt(ones, lo))
    part = dot(rows_o[...], w_out[:, block_cols(idx, 2)]).astype(BF16)
    tail = tail_rows(sums_o[0:1, :])
    for g, out in enumerate((top, low)):
        out[:GROUP, :] = part[span(g, GROUP)]
        out[GROUP:, :] = tail


def gated_rows(idx, parts, first, thr, c, us, ents, zs, gain, w_out):
    return call(
        gated_body,
        "gated_rows",
        idx,
        [*parts, first, thr, c, *us, *ents, zs, gain, w_out],
        [((ROWS, WIDTH), BF16), ((8, ROWS), F32), *[((TAILED, FEAT), BF16)] * 2],
        [((NSTATE, WIDTH), BF16)],
        flops=2.6 * ROWS * WIDTH * FEAT,
    )


def near_body(bits, g, idx, rows, w_out, message, part):
    value = dot(rows[...], w_out[:, block_cols(idx, bits)])
    part[...] = value[span(g, GROUP)]
    message[...] = value[span(1 - g, GROUP)].astype(BF16)


def near_block(bits, g, idx, rows, w_out):
    return call(
        functools.partial(near_body, bits, g),
        "near_block",
        idx,
        [rows, w_out],
        [((GROUP, FEAT), BF16), ((GROUP, FEAT), F32)],
        flops=1e6,
    )


def own_body(idx, rows, w_out, out):
    out[...] = dot(rows[...], w_out[:, block_cols(idx, 0)])


def own_block(idx, rows, w_out):
    return call(
        own_body,
        "own_block",
        idx,
        [rows, w_out],
        [((ROWS, FEAT), F32)],
        flops=1e6,
    )[0]


def join_body(idx, part, half, out):
    out[:GROUP, :] = (part[...] + half[:GROUP, :].astype(F32)).astype(BF16)
    out[GROUP:, :] = half[GROUP:, :]


def join(idx, part, half):
    return call(join_body, "join", idx, [part, half], [((TAILED, FEAT), BF16)], mib=8)[0]


def add_body(idx, own, left_0, right_1, out):
    out[:GROUP, :] = own[:GROUP, :] + left_0[...].astype(F32)
    out[GROUP:, :] = own[GROUP:, :] + right_1[...].astype(F32)


def add_near(idx, own, left_0, right_1):
    return call(
        add_body,
        "add_near",
        idx,
        [own, left_0, right_1],
        [((ROWS, FEAT), F32)],
        mib=8,
        flops=5e9,
        aliases={1: 0},
    )[0]


def settle_body(idx, own, sums, near, other, left_1, out, factor, made, sem):
    squares = sums[0:1, :] + squares_of(left_1)
    squares = squares + (squares_of(near) + squares_of(other))
    stack = terms(squares, 16, ROWS).astype(BF16)
    scale = lax.rsqrt(dot_tn(stack, jnp.ones((16, LANES), BF16)) / DI + 1e-05)
    factor[...] = scale[:GROUP]
    for k in range(FEAT // LANES):
        lanes = span(k, LANES)
        value = own[GROUP:, lanes] + left_1[:GROUP, lanes].astype(F32)
        made[:, lanes] = (value * scale[GROUP:]).astype(BF16)
    copy = pltpu.make_async_copy(made, out.at[GROUP:, :], sem)
    copy.start()
    copy.wait()


def end_call(body, name, idx, args, outs, specs, more=()):
    args = [pltpu.with_memory_space_constraint(a, pltpu.VMEM) for a in args]
    return pl.pallas_call(
        body,
        in_specs=[SMEM, *[VMEM] * len(args), *[HBM] * len(more)],
        out_specs=specs,
        out_shape=outs,
        scratch_shapes=[pltpu.VMEM((GROUP, FEAT), BF16), pltpu.SemaphoreType.DMA],
        input_output_aliases={1 + len(args): 0} if more else {},
        compiler_params=pltpu.CompilerParams(vmem_limit_bytes=8 * MIB),
        cost_estimate=cost(1e6, 1e6),
        name=name,
    )(idx, *args, *more)


def settle(idx, *args):
    outs = [jax.ShapeDtypeStruct((ROWS, FEAT), BF16), pltpu.VMEM((GROUP, LANES), F32)]
    return end_call(settle_body, "settle", idx, args, outs, [HBM, VMEM])


def norm_body(idx, own, factor, right_0, so_far, out, made, sem):
    for k in range(FEAT // LANES):
        lanes = span(k, LANES)
        value = own[:GROUP, lanes] + right_0[:GROUP, lanes].astype(F32)
        made[:, lanes] = (value * factor[...]).astype(BF16)
    copy = pltpu.make_async_copy(made, out.at[:GROUP, :], sem)
    copy.start()
    copy.wait()


def norm(idx, own, factor, right_0, so_far):
    outs = jax.ShapeDtypeStruct((ROWS, FEAT), BF16)
    return end_call(norm_body, "norm", idx, (own, factor, right_0), outs, HBM, (so_far,))


def on_device(tokens, resets, w_x, w_z, w_bc, w_dt, dt_bias, decay_rate, d_skip, norm_gain, w_out):
    places = ("head", "seq_0", "seq_1")
    idx = jnp.stack([lax.axis_index(axis) for axis in places]).astype(jnp.int32)
    heads = w_dt.shape[1]
    top, low = tokens[:GROUP], tokens[GROUP:]
    l_0, r_1 = swapped(top, "head", 1), swapped(low, "head", 3)
    top, low, idx = lax.optimization_barrier((top, low, idx))
    l_1, r_0 = swapped(low, "head", 1), swapped(top, "head", 3)
    bias = jnp.pad(dt_bias, (0, LANES - heads)).reshape(1, LANES)
    rate = jnp.pad(decay_rate, (0, LANES - heads)).reshape(1, LANES)
    starts = resets.reshape(1, ROWS)
    skip = jnp.pad(d_skip, (0, LANES - heads)).reshape(1, LANES)
    gain = norm_gain.reshape(1, WIDTH)

    acc_x, acc_bd, tokens, w_dt, w_x, w_z, w_bc = load_weights(
        idx, tokens, w_dt.T, w_x, w_z, w_bc
    )
    far = [swapped(l_0, "head", 3), swapped(r_1, "head", 1)]
    acc_z = gate_first(idx, tokens, l_0, r_1, w_z)
    near = (l_0, l_1, r_0, r_1)
    sums = project(idx, near, w_x, w_bc, w_dt, (acc_x, acc_bd))
    acc_z = gate_second(idx, l_1, r_0, w_z, acc_z)
    far, acc_z, sums = lax.optimization_barrier((far, acc_z, sums))
    inner, b, c, cum, step, first, thr, *messages = device_state(
        idx, far, w_x, w_bc, w_dt, sums, starts, bias, rate
    )
    quarters = [messages[0], *(swapped(messages[d], "seq_1", d) for d in (1, 2, 3))]
    u0, e0 = mix(0, idx, inner, b, c, cum, step, skip)
    quarters, u0, e0, cum = lax.optimization_barrier((quarters, u0, e0, cum))
    total = row_total(idx, quarters)
    totals = [total, *(swapped(total, "seq_0", d) for d in (1, 2, 3))]
    u1, e1 = mix(1, idx, inner, b, c, cum, step, skip)
    totals, u1, e1, w_z = lax.optimization_barrier((totals, u1, e1, w_z))
    parts = prefixes(idx, quarters, totals)
    parts = [parts[0], *(swapped(parts[d], "seq_1", d) for d in (1, 2, 3))]
    zs = gate(idx, far, w_z, acc_z)
    rows, sums, top, low = gated_rows(
        idx, parts, first, thr, c, (u0, u1), (e0, e1), zs, gain, w_out
    )
    top, low = swapped(top, "head", 1), swapped(low, "head", 3)
    left_0, part_1 = near_block(1, 1, idx, rows, w_out)
    left_0 = swapped(left_0, "head", 1)
    right_1, part_0 = near_block(3, 0, idx, rows, w_out)
    right_1 = swapped(right_1, "head", 3)
    own = own_block(idx, rows, w_out)
    right_0 = swapped(join(idx, part_0, top), "head", 3)
    left_1 = swapped(join(idx, part_1, low), "head", 1)
    own = add_near(idx, own, left_0, right_1)
    half, factor = settle(idx, own, sums, top, low, left_1)
    return norm(idx, own, factor, right_0, half)


def solution(mesh):
    split = Mesh(
        mesh.devices.reshape(4, 4, mesh.shape["head"], mesh.shape["batch"]),
        ("seq_0", "seq_1", "head", "batch"),
    )
    placed = (
        P(BATCH_SEQ, "head"),
        P(BATCH_SEQ),
        P(None, "head"),
        P(None, "head"),
        P(),
        P(None, "head"),
        P("head"),
        P("head"),
        P("head"),
        P("head"),
        P("head", None),
    )
    return jax.shard_map(
        on_device, mesh=split, in_specs=placed, out_specs=P(BATCH_SEQ, "head"), check_vma=False
    )
```

```python
import functools

import jax
import jax.numpy as jnp
from jax import lax
from jax.experimental import pallas as pl
from jax.experimental.pallas import tpu as pltpu
from jax.sharding import Mesh
from jax.sharding import PartitionSpec as P

DI = 5120
HEADDIM = 64
NSTATE = 128
GROUP = 256
ROWS = 512
FEAT = 640
WIDTH = 1280
TILE = 256
STEPS = WIDTH // TILE
PER = TILE // HEADDIM
LANES = 128
BD = 384
TAILED = GROUP + 8
QUARTER = NSTATE // 4
MSG = WIDTH + LANES
LOG2E = 1.4426950408889634
BATCH_SEQ = ("batch", "seq_0", "seq_1")
F32 = jnp.float32
BF16 = jnp.bfloat16
MIB = 1 << 20


def dot(a, b):
    return lax.dot_general(a, b, (((1,), (0,)), ((), ())), preferred_element_type=F32)


def dot_nt(a, b):
    return lax.dot_general(a, b, (((1,), (1,)), ((), ())), preferred_element_type=F32)


def dot_tn(a, b):
    return lax.dot_general(a, b, (((0,), (0,)), ((), ())), preferred_element_type=F32)


def silu(v):
    return v / (1.0 + jnp.exp(-v))


def three(v):
    hi = v.astype(BF16)
    rest = v - hi.astype(F32)
    mid = rest.astype(BF16)
    return hi, mid, (rest - mid.astype(F32)).astype(BF16)


def swapped(array, axis, bits):
    return lax.ppermute(array, axis, [(i, i ^ bits) for i in range(4)])


VMEM = pl.BlockSpec(memory_space=pltpu.VMEM)
HBM = pl.BlockSpec(memory_space=pltpu.HBM)
SMEM = pl.BlockSpec(memory_space=pltpu.SMEM)


def cost(flops, nbytes, trans=0):
    return pl.CostEstimate(flops=int(flops), bytes_accessed=int(nbytes), transcendentals=int(trans))


def call(body, name, idx, args, outs, scratch=(), mib=16, flops=1e8, aliases=None, kept=True):
    args = [pltpu.with_memory_space_constraint(a, pltpu.VMEM) for a in args]
    made = [pltpu.VMEM(*o) if kept else jax.ShapeDtypeStruct(*o) for o in outs]
    return pl.pallas_call(
        body,
        in_specs=[SMEM, *[VMEM] * len(args)],
        out_specs=[VMEM] * len(outs),
        out_shape=made,
        scratch_shapes=[pltpu.VMEM(*s) for s in scratch],
        input_output_aliases=aliases or {},
        compiler_params=pltpu.CompilerParams(vmem_limit_bytes=mib * MIB),
        cost_estimate=cost(flops, 1e6),
        name=name,
    )(idx, *args)


def span(j, size=TILE):
    return slice(j * size, (j + 1) * size)


def block_of(idx, bits):
    owner = idx[0] ^ bits
    return pl.ds(pl.multiple_of(owner * FEAT, FEAT), FEAT)


def own_parts(idx, tokens, w_x, w_bc, w_dt, out_x, out_bd):
    feats = block_of(idx, 0)
    for j in range(STEPS):
        out_x[:, span(j)] = dot(tokens, w_x[feats, span(j)])
    out_bd[:, : 2 * NSTATE] = dot(tokens, w_bc[feats, :])
    out_bd[:, 2 * NSTATE :] = dot_nt(tokens, w_dt[:, feats])


def load_body(
    idx, w_dt, tok, w_x, w_z, w_bc, acc_x, acc_bd, v_tok, v_dt, v_x, v_z, v_bc, narrow, sems
):
    copies = [
        pltpu.make_async_copy(w_dt, narrow, sems.at[0]),
        pltpu.make_async_copy(tok, v_tok, sems.at[1]),
    ]
    for bits in range(4):
        feats = block_of(idx, bits)
        for source, target in ((w_x, v_x), (w_bc, v_bc)):
            sem = sems.at[len(copies)]
            copies.append(pltpu.make_async_copy(source.at[feats, :], target.at[feats, :], sem))
    copies.append(pltpu.make_async_copy(w_z, v_z, sems.at[len(copies)]))
    for copy in copies:
        copy.start()
    v_dt[...] = jnp.zeros_like(v_dt)
    copies[0].wait()
    v_dt[: w_dt.shape[0], :] = narrow[...]
    for copy in copies[1:4]:
        copy.wait()
    own_parts(idx, v_tok[...], v_x, v_bc, v_dt, acc_x, acc_bd)
    for copy in copies[4:]:
        copy.wait()


def load_weights(idx, tok, w_dt, w_x, w_z, w_bc):
    return pl.pallas_call(
        load_body,
        in_specs=[SMEM, *[HBM] * 5],
        out_specs=[VMEM] * 7,
        out_shape=[
            pltpu.VMEM((ROWS, WIDTH), F32),
            pltpu.VMEM((ROWS, BD), F32),
            pltpu.VMEM(tok.shape, BF16),
            pltpu.VMEM((LANES, w_dt.shape[1]), BF16),
            pltpu.VMEM(w_x.shape, BF16),
            pltpu.VMEM(w_z.shape, BF16),
            pltpu.VMEM(w_bc.shape, BF16),
        ],
        scratch_shapes=[pltpu.VMEM(w_dt.shape, BF16), pltpu.SemaphoreType.DMA((11,))],
        compiler_params=pltpu.CompilerParams(vmem_limit_bytes=36 * MIB),
        cost_estimate=cost(2 * ROWS * FEAT * (WIDTH + BD), 15e6),
        name="load_weights",
    )(idx, w_dt, tok, w_x, w_z, w_bc)


def near_tokens(l_0, l_1, r_0, r_1):
    left = jnp.concatenate([l_0[...], l_1[...]], 0)
    return jnp.concatenate([left, jnp.concatenate([r_0[...], r_1[...]], 0)], 1)


def project_body(idx, l_0, l_1, r_0, r_1, w_x, w_bc, w_dt, acc_x, acc_bd, out_x, out_bd):
    tokens = near_tokens(l_0, l_1, r_0, r_1)
    one, other = block_of(idx, 1), block_of(idx, 3)
    for j in range(STEPS):
        weight = jnp.concatenate([w_x[one, span(j)], w_x[other, span(j)]], 0)
        out_x[:, span(j)] = acc_x[:, span(j)] + dot(tokens, weight)
    weight = jnp.concatenate([w_bc[one, :], w_bc[other, :]], 0)
    out_bd[:, : 2 * NSTATE] = acc_bd[:, : 2 * NSTATE] + dot(tokens, weight)
    weight = jnp.concatenate([w_dt[:, one], w_dt[:, other]], 1)
    out_bd[:, 2 * NSTATE :] = acc_bd[:, 2 * NSTATE :] + dot_nt(tokens, weight)


def project(idx, near, w_x, w_bc, w_dt, sums):
    return call(
        project_body,
        "project",
        idx,
        [*near, w_x, w_bc, w_dt, *sums],
        [((ROWS, WIDTH), F32), ((ROWS, BD), F32)],
        flops=4 * ROWS * FEAT * (WIDTH + BD),
        aliases={8: 0, 9: 1},
    )


def head_rows(j):
    head = lax.broadcasted_iota(jnp.int32, (LANES, TILE), 0)
    channel = lax.broadcasted_iota(jnp.int32, (LANES, TILE), 1)
    return (head == PER * j + channel // HEADDIM).astype(BF16)


def terms(v, rows, width):
    hi, mid, lo = (part.astype(F32) for part in three(v))
    row = lax.broadcasted_iota(jnp.int32, (rows, width), 0)
    return jnp.where(row == 0, hi, jnp.where(row == 1, mid, jnp.where(row == 2, lo, 0.0)))


def state_body(
    idx, tok_0, tok_1, w_x, w_bc, w_dt, acc_x, acc_bd, resets, bias, rate,
    inner_o, b_o, c_o, cum_o, step_o, first_o, thr_o, m0, m1, m2, m3, state_s,
):
    tokens = jnp.concatenate([tok_0[...], tok_1[...]], 0)
    feats = block_of(idx, 2)
    logits_part = dot_nt(tokens, w_dt[:, feats])
    mapped = silu(acc_bd[:, : 2 * NSTATE] + dot(tokens, w_bc[feats, :]))
    ahead = dot(tokens, w_x[feats, span(0)])
    b_t = mapped[:, :NSTATE].T.astype(BF16)
    b_o[...] = mapped[:, :NSTATE].astype(BF16)
    c_o[...] = mapped[:, NSTATE:].astype(BF16)
    logits = acc_bd[:, 2 * NSTATE :] + logits_part + bias[...]
    step = jnp.maximum(logits, 0.0) + jnp.log1p(jnp.exp(-jnp.abs(logits)))
    step_o[...] = step
    lane = lax.broadcasted_iota(jnp.int32, (ROWS, LANES), 1)
    first_row = lax.broadcasted_iota(jnp.int32, (16, ROWS), 0) == 0
    marks = jnp.where(first_row, resets[...].astype(F32), 0.0).astype(BF16)
    marks = dot_tn(marks, jnp.ones((16, LANES), BF16))
    decay = jnp.where(lane == LANES - 1, marks, -step * rate[...])
    row = lax.broadcasted_iota(jnp.int32, (GROUP, GROUP), 0)
    col = lax.broadcasted_iota(jnp.int32, (GROUP, GROUP), 1)
    lower = (row >= col).astype(BF16)
    keeps, throughs = [], []
    for g in range(2):
        sums = dot(lower, jnp.concatenate(three(decay[span(g, GROUP)]), 1))
        cum = sums[:, :LANES] + (sums[:, LANES : 2 * LANES] + sums[:, 2 * LANES :])
        cum_o[span(g, GROUP), :] = cum
        last = cum[GROUP - 1 :, :]
        seg, closing = cum[:, LANES - 1 :], last[:, LANES - 1 :]
        keeps.append(jnp.where(seg == closing, jnp.exp(last - cum), 0.0) * step[span(g, GROUP)])
        throughs.append(jnp.where(closing == 0.0, jnp.exp(last), 0.0))
    keep = jnp.concatenate(keeps, 0)
    keep_hi = keep.astype(BF16)
    keep_lo = (keep - keep_hi.astype(F32)).astype(BF16)
    keep = jnp.concatenate([keep_hi, keep_lo], 1)
    through = jnp.concatenate([terms(t, 8, LANES) for t in throughs], 0).astype(BF16)
    tail = terms(throughs[0] * throughs[1], QUARTER, LANES).astype(BF16)
    for j in range(STEPS):
        part = ahead
        if j + 1 < STEPS:
            ahead = dot(tokens, w_x[feats, span(j + 1)])
        inner = silu(acc_x[:, span(j)] + part).astype(BF16)
        inner_o[:, span(j)] = inner
        heads = head_rows(j)
        wide = dot(keep, jnp.concatenate([heads, heads], 0))
        scaled = (wide * inner.astype(F32)).astype(BF16)
        state0 = dot(b_t[:, :GROUP], scaled[:GROUP])
        state1 = dot(b_t[:, GROUP:], scaled[GROUP:])
        thr = dot(through, heads)
        thr0 = thr[0:1] + thr[1:2] + thr[2:3]
        thr1 = thr[8:9] + thr[9:10] + thr[10:11]
        first_o[:, span(j)] = state0
        thr_o[:, span(j)] = jnp.broadcast_to(thr0, (8, TILE))
        state_s[:, span(j)] = thr1 * state0 + state1
    for d, message in enumerate((m0, m1, m2, m3)):
        start = pl.multiple_of((idx[2] ^ d) * QUARTER, QUARTER)
        message[:, :WIDTH] = state_s[pl.ds(start, QUARTER), :].astype(BF16)
        message[:, WIDTH:] = tail


def device_state(idx, far, w_x, w_bc, w_dt, sums, resets, bias, rate):
    small = (ROWS, LANES)
    return call(
        state_body,
        "device_state",
        idx,
        [*far, w_x, w_bc, w_dt, *sums, resets, bias, rate],
        [
            ((ROWS, WIDTH), BF16), (small, BF16), (small, BF16), (small, F32), (small, F32),
            ((NSTATE, WIDTH), F32), ((8, WIDTH), F32), *[((QUARTER, MSG), BF16)] * 4,
        ],
        [((NSTATE, WIDTH), F32)],
        flops=2 * ROWS * FEAT * (WIDTH + BD),
    )


def tail_of(message):
    tail = message[:, WIDTH:].astype(F32)
    return tail[0:1] + tail[1:2] + tail[2:3]


def decays_of(messages, j):
    tails = jnp.concatenate([m[:16, WIDTH:] for m in messages], 0)
    wide = dot(tails, head_rows(j))
    rows = range(0, 16 * len(messages), 16)
    return [wide[k : k + 1] + wide[k + 1 : k + 2] + wide[k + 2 : k + 3] for k in rows]


def total_body(idx, m0, m1, m2, m3, out, held):
    for d, message in enumerate((m0, m1, m2, m3)):
        held[idx[2] ^ d] = message[...]
    messages = [held.at[k] for k in range(4)]
    through = tail_of(messages[0])
    for message in messages[1:]:
        through = through * tail_of(message)
    out[:, WIDTH:] = terms(through, QUARTER, LANES).astype(BF16)
    for j in range(STEPS):
        decays = decays_of(messages, j)
        state = messages[0][:, span(j)].astype(F32)
        for k in range(1, 4):
            state = decays[k] * state + messages[k][:, span(j)].astype(F32)
        out[:, span(j)] = state.astype(BF16)


def prefix_body(idx, m0, m1, m2, m3, t0, t1, t2, t3, h0, h1, h2, h3, held, rows, found):
    for d, message in enumerate((m0, m1, m2, m3)):
        held[idx[2] ^ d] = message[...]
    for d, message in enumerate((t0, t1, t2, t3)):
        rows[idx[1] ^ d] = message[...]
    messages = [held.at[k] for k in range(4)]
    totals = [rows.at[k] for k in range(4)]
    for j in range(STEPS):
        decays = decays_of([*messages, *totals], j)
        state = jnp.zeros((QUARTER, TILE), F32)
        for k in range(3):
            after = decays[4 + k] * state + totals[k][:, span(j)].astype(F32)
            state = jnp.where(k < idx[1], after, state)
        for k in range(4):
            found[k, :, span(j)] = state.astype(BF16)
            if k < 3:
                state = decays[k] * state + messages[k][:, span(j)].astype(F32)
    for d, out in enumerate((h0, h1, h2, h3)):
        out[...] = found[idx[2] ^ d]


def row_total(idx, messages):
    return call(
        total_body,
        "row_total",
        idx,
        messages,
        [((QUARTER, MSG), BF16)],
        [((4, QUARTER, MSG), BF16)],
        mib=8,
    )[0]


def prefixes(idx, messages, totals):
    return call(
        prefix_body,
        "prefixes",
        idx,
        [*messages, *totals],
        [((QUARTER, WIDTH), BF16)] * 4,
        [((4, QUARTER, MSG), BF16), ((4, QUARTER, MSG), BF16), ((4, QUARTER, WIDTH), BF16)],
        mib=8,
    )


def gate_first_body(idx, tok, l_0, r_1, w_z, out):
    own, one, other = (block_of(idx, bits) for bits in (0, 1, 3))
    for j in range(STEPS):
        part = dot(tok[...], w_z[own, span(j)])
        out[:GROUP, span(j)] = part[:GROUP] + dot(l_0[...], w_z[one, span(j)])
        out[GROUP:, span(j)] = part[GROUP:] + dot(r_1[...], w_z[other, span(j)])


def gate_first(idx, tok, l_0, r_1, w_z):
    return call(
        gate_first_body,
        "gate_first",
        idx,
        [tok, l_0, r_1, w_z],
        [((ROWS, WIDTH), F32)],
        flops=4 * ROWS * FEAT * WIDTH,
    )[0]


def gate_second_body(idx, l_1, r_0, w_z, acc_z, out):
    one, other = block_of(idx, 1), block_of(idx, 3)
    for j in range(STEPS):
        out[:GROUP, span(j)] = acc_z[:GROUP, span(j)] + dot(r_0[...], w_z[other, span(j)])
        out[GROUP:, span(j)] = acc_z[GROUP:, span(j)] + dot(l_1[...], w_z[one, span(j)])


def gate_second(idx, l_1, r_0, w_z, acc_z):
    return call(
        gate_second_body,
        "gate_second",
        idx,
        [l_1, r_0, w_z, acc_z],
        [((ROWS, WIDTH), F32)],
        flops=2 * ROWS * FEAT * WIDTH,
        aliases={4: 0},
    )[0]


def gate_body(idx, t_0, t_1, w_z, acc_z, out):
    tokens = jnp.concatenate([t_0[...], t_1[...]], 0)
    feats = block_of(idx, 2)
    for j in range(STEPS):
        gating = acc_z[:, span(j)] + dot(tokens, w_z[feats, span(j)])
        out[:, span(j)] = silu(gating.astype(BF16).astype(F32))


def gate(idx, far, w_z, acc_z):
    return call(
        gate_body,
        "gate",
        idx,
        [*far, w_z, acc_z],
        [((ROWS, WIDTH), F32)],
        flops=2 * ROWS * FEAT * WIDTH,
        aliases={4: 0},
    )[0]


def mix_body(g, idx, inner_r, b_r, c_r, cum_r, step_r, skip, out, ent_o, scores, cum_t, step_t):
    half = GROUP // 2
    rows = span(g, GROUP)
    cum = cum_r[rows, :]
    across = cum.T
    cum_2 = cum * LOG2E
    cum_t[...] = across * LOG2E
    step_t[...] = step_r[rows, :].T
    row = lax.broadcasted_iota(jnp.int32, (GROUP, GROUP), 0)
    col = lax.broadcasted_iota(jnp.int32, (GROUP, GROUP), 1)
    seg = cum[:, LANES - 1 :]
    same = (seg == across[LANES - 1 :, :]) & (row >= col)
    scores[...] = jnp.where(same, dot_nt(c_r[rows, :], b_r[rows, :]), 0.0)
    enter = jnp.where(seg == 0.0, jnp.exp(cum), 0.0)
    hi = enter.astype(BF16)
    lo = (enter - hi.astype(F32)).astype(BF16)
    lane = lax.broadcasted_iota(jnp.int32, (GROUP, LANES), 1)
    skips = []
    for j in range(STEPS):
        heads = head_rows(j)
        ent_o[:, span(j)] = dot(hi, heads) + dot(lo, heads)
        wide = dot(terms(skip[...], 16, LANES).astype(BF16), heads)
        wide = wide[0:1] + wide[1:2] + wide[2:3]
        skips += [wide[:, :LANES], wide[:, LANES:]]
    for pair in range(WIDTH // LANES):
        both = inner_r[rows, span(pair, LANES)]
        ys = []
        for head in (2 * pair, 2 * pair + 1):
            before = cum_t[head : head + 1, :]
            step = step_t[head : head + 1, :]
            top = jnp.exp2(jnp.minimum(cum_2[:half, head : head + 1] - before[:, :half], 0.0))
            top = (top * scores[:half, :half] * step[:, :half]).astype(BF16)
            low = jnp.exp2(jnp.minimum(cum_2[half:, head : head + 1] - before, 0.0))
            low = (low * scores[half:, :] * step).astype(BF16)
            ys.append(jnp.concatenate([dot(top, both[:half]), dot(low, both)], 0))
        y = jnp.where(lane < HEADDIM, ys[0], ys[1])
        out[:, span(pair, LANES)] = y + skips[pair] * both.astype(F32)


def mix(g, idx, inner, b, c, cum, step, skip):
    return call(
        functools.partial(mix_body, g),
        "mix",
        idx,
        [inner, b, c, cum, step, skip],
        [((GROUP, WIDTH), F32), ((GROUP, WIDTH), F32)],
        [((GROUP, GROUP), F32), ((LANES, GROUP), F32), ((LANES, GROUP), F32)],
        flops=2e9,
    )


def block_cols(idx, bits):
    target = idx[0] ^ bits
    return pl.ds(pl.multiple_of(target * FEAT, FEAT), FEAT)


def tail_rows(squares):
    zeros = jnp.zeros((8, FEAT - ROWS), F32)
    return jnp.concatenate([terms(squares, 8, ROWS), zeros], 1).astype(BF16)


def squares_of(message):
    tail = message[GROUP:, :ROWS].astype(F32)
    return tail[0:1] + (tail[1:2] + tail[2:3])


def gated_body(
    idx, h0, h1, h2, h3, first, thr, c_r, u0, u1, e0, e1, zs_r, gain, w_out,
    rows_o, sums_o, top, low, state,
):
    for d, part in enumerate((h0, h1, h2, h3)):
        start = pl.multiple_of((idx[2] ^ d) * QUARTER, QUARTER)
        state[pl.ds(start, QUARTER), :] = part[...]
    def carried(g, j):
        enter = state[:, span(j)]
        if g:
            enter = first[:, span(j)] + thr[0:1, span(j)] * enter.astype(F32)
            enter = enter.astype(BF16)
        return dot(c_r[span(g, GROUP), :], enter)

    ones = jnp.ones((8, LANES), BF16)
    steps = [(g, j) for g in range(2) for j in range(STEPS)]
    squares = [jnp.zeros((GROUP, LANES), F32), jnp.zeros((GROUP, LANES), F32)]
    ahead = carried(0, 0)
    for n, (g, j) in enumerate(steps):
        now = ahead
        if n + 1 < len(steps):
            ahead = carried(*steps[n + 1])
        rows, u, ent = span(g, GROUP), (u0, u1)[g], (e0, e1)[g]
        gated = (u[:, span(j)] + ent[:, span(j)] * now) * zs_r[rows, span(j)]
        rows_o[rows, span(j)] = (gated * gain[:, span(j)]).astype(BF16)
        square = gated * gated
        squares[g] = squares[g] + (square[:, :LANES] + square[:, LANES:])
    part = dot(rows_o[...], w_out[:, block_cols(idx, 2)])
    for g in range(2):
        hi, mid, lo = three(squares[g])
        sums_o[:, span(g, GROUP)] = dot_nt(ones, hi) + (dot_nt(ones, mid) + dot_nt(ones, lo))
    part = part.astype(BF16)
    tail = tail_rows(sums_o[0:1, :])
    for g, out in enumerate((top, low)):
        out[:GROUP, :] = part[span(g, GROUP)]
        out[GROUP:, :] = tail


def gated_rows(idx, parts, first, thr, c, us, ents, zs, gain, w_out):
    return call(
        gated_body,
        "gated_rows",
        idx,
        [*parts, first, thr, c, *us, *ents, zs, gain, w_out],
        [((ROWS, WIDTH), BF16), ((8, ROWS), F32), *[((TAILED, FEAT), BF16)] * 2],
        [((NSTATE, WIDTH), BF16)],
        flops=2.6 * ROWS * WIDTH * FEAT,
    )


def near_body(bits, g, idx, rows, w_out, message, part):
    value = dot(rows[...], w_out[:, block_cols(idx, bits)])
    part[...] = value[span(g, GROUP)]
    message[...] = value[span(1 - g, GROUP)].astype(BF16)


def near_block(bits, g, idx, rows, w_out):
    return call(
        functools.partial(near_body, bits, g),
        "near_block",
        idx,
        [rows, w_out],
        [((GROUP, FEAT), BF16), ((GROUP, FEAT), F32)],
        flops=1e6,
    )


def own_body(idx, rows, w_out, out):
    out[...] = dot(rows[...], w_out[:, block_cols(idx, 0)])


def own_block(idx, rows, w_out):
    return call(
        own_body,
        "own_block",
        idx,
        [rows, w_out],
        [((ROWS, FEAT), F32)],
        flops=1e6,
    )[0]


def join_body(idx, part, half, out):
    out[:GROUP, :] = (part[...] + half[:GROUP, :].astype(F32)).astype(BF16)
    out[GROUP:, :] = half[GROUP:, :]


def join(idx, part, half):
    return call(join_body, "join", idx, [part, half], [((TAILED, FEAT), BF16)], mib=8)[0]


def add_body(idx, own, left_0, right_1, out):
    out[:GROUP, :] = own[:GROUP, :] + left_0[...].astype(F32)
    out[GROUP:, :] = own[GROUP:, :] + right_1[...].astype(F32)


def add_near(idx, own, left_0, right_1):
    return call(
        add_body,
        "add_near",
        idx,
        [own, left_0, right_1],
        [((ROWS, FEAT), F32)],
        mib=8,
        flops=5e9,
        aliases={1: 0},
    )[0]


def settle_body(idx, own, sums, near, other, left_1, out, factor, made, sem):
    squares = sums[0:1, :] + squares_of(left_1)
    squares = squares + (squares_of(near) + squares_of(other))
    stack = terms(squares, 16, ROWS).astype(BF16)
    scale = lax.rsqrt(dot_tn(stack, jnp.ones((16, LANES), BF16)) / DI + 1e-05)
    factor[...] = scale[:GROUP]
    for k in range(FEAT // LANES):
        lanes = span(k, LANES)
        value = own[GROUP:, lanes] + left_1[:GROUP, lanes].astype(F32)
        made[:, lanes] = (value * scale[GROUP:]).astype(BF16)
    copy = pltpu.make_async_copy(made, out.at[GROUP:, :], sem)
    copy.start()
    copy.wait()


def end_call(body, name, idx, args, outs, specs, more=()):
    args = [pltpu.with_memory_space_constraint(a, pltpu.VMEM) for a in args]
    return pl.pallas_call(
        body,
        in_specs=[SMEM, *[VMEM] * len(args), *[HBM] * len(more)],
        out_specs=specs,
        out_shape=outs,
        scratch_shapes=[pltpu.VMEM((GROUP, FEAT), BF16), pltpu.SemaphoreType.DMA],
        input_output_aliases={1 + len(args): 0} if more else {},
        compiler_params=pltpu.CompilerParams(vmem_limit_bytes=8 * MIB),
        cost_estimate=cost(1e6, 1e6),
        name=name,
    )(idx, *args, *more)


def settle(idx, *args):
    outs = [jax.ShapeDtypeStruct((ROWS, FEAT), BF16), pltpu.VMEM((GROUP, LANES), F32)]
    return end_call(settle_body, "settle", idx, args, outs, [HBM, VMEM])


def norm_body(idx, own, factor, right_0, so_far, out, made, sem):
    for k in range(FEAT // LANES):
        lanes = span(k, LANES)
        value = own[:GROUP, lanes] + right_0[:GROUP, lanes].astype(F32)
        made[:, lanes] = (value * factor[...]).astype(BF16)
    copy = pltpu.make_async_copy(made, out.at[:GROUP, :], sem)
    copy.start()
    copy.wait()


def norm(idx, own, factor, right_0, so_far):
    outs = jax.ShapeDtypeStruct((ROWS, FEAT), BF16)
    return end_call(norm_body, "norm", idx, (own, factor, right_0), outs, HBM, (so_far,))


def on_device(tokens, resets, w_x, w_z, w_bc, w_dt, dt_bias, decay_rate, d_skip, norm_gain, w_out):
    places = ("head", "seq_0", "seq_1")
    idx = jnp.stack([lax.axis_index(axis) for axis in places]).astype(jnp.int32)
    heads = w_dt.shape[1]
    top, low = tokens[:GROUP], tokens[GROUP:]
    l_0, r_1 = swapped(top, "head", 1), swapped(low, "head", 3)
    top, low, idx = lax.optimization_barrier((top, low, idx))
    l_1, r_0 = swapped(low, "head", 1), swapped(top, "head", 3)
    bias = jnp.pad(dt_bias, (0, LANES - heads)).reshape(1, LANES)
    rate = jnp.pad(decay_rate, (0, LANES - heads)).reshape(1, LANES)
    starts = resets.reshape(1, ROWS)
    skip = jnp.pad(d_skip, (0, LANES - heads)).reshape(1, LANES)
    gain = norm_gain.reshape(1, WIDTH)

    acc_x, acc_bd, tokens, w_dt, w_x, w_z, w_bc = load_weights(
        idx, tokens, w_dt.T, w_x, w_z, w_bc
    )
    far = [swapped(l_0, "head", 3), swapped(r_1, "head", 1)]
    acc_z = gate_first(idx, tokens, l_0, r_1, w_z)
    near = (l_0, l_1, r_0, r_1)
    sums = project(idx, near, w_x, w_bc, w_dt, (acc_x, acc_bd))
    acc_z = gate_second(idx, l_1, r_0, w_z, acc_z)
    far, acc_z, sums = lax.optimization_barrier((far, acc_z, sums))
    inner, b, c, cum, step, first, thr, *messages = device_state(
        idx, far, w_x, w_bc, w_dt, sums, starts, bias, rate
    )
    quarters = [messages[0], *(swapped(messages[d], "seq_1", d) for d in (1, 2, 3))]
    u0, e0 = mix(0, idx, inner, b, c, cum, step, skip)
    quarters, u0, e0, cum = lax.optimization_barrier((quarters, u0, e0, cum))
    total = row_total(idx, quarters)
    totals = [total, *(swapped(total, "seq_0", d) for d in (1, 2, 3))]
    u1, e1 = mix(1, idx, inner, b, c, cum, step, skip)
    totals, u1, e1, w_z = lax.optimization_barrier((totals, u1, e1, w_z))
    parts = prefixes(idx, quarters, totals)
    parts = [parts[0], *(swapped(parts[d], "seq_1", d) for d in (1, 2, 3))]
    zs = gate(idx, far, w_z, acc_z)
    rows, sums, top, low = gated_rows(
        idx, parts, first, thr, c, (u0, u1), (e0, e1), zs, gain, w_out
    )
    top, low = swapped(top, "head", 1), swapped(low, "head", 3)
    left_0, part_1 = near_block(1, 1, idx, rows, w_out)
    left_0 = swapped(left_0, "head", 1)
    right_1, part_0 = near_block(3, 0, idx, rows, w_out)
    right_1 = swapped(right_1, "head", 3)
    own = own_block(idx, rows, w_out)
    right_0 = swapped(join(idx, part_0, top), "head", 3)
    left_1 = swapped(join(idx, part_1, low), "head", 1)
    own = add_near(idx, own, left_0, right_1)
    half, factor = settle(idx, own, sums, top, low, left_1)
    return norm(idx, own, factor, right_0, half)


def solution(mesh):
    split = Mesh(
        mesh.devices.reshape(4, 4, mesh.shape["head"], mesh.shape["batch"]),
        ("seq_0", "seq_1", "head", "batch"),
    )
    placed = (
        P(BATCH_SEQ, "head"),
        P(BATCH_SEQ),
        P(None, "head"),
        P(None, "head"),
        P(),
        P(None, "head"),
        P("head"),
        P("head"),
        P("head"),
        P("head"),
        P("head", None),
    )
    return jax.shard_map(
        on_device, mesh=split, in_specs=placed, out_specs=P(BATCH_SEQ, "head"), check_vma=False
    )
```

```python
import functools

import jax
import jax.numpy as jnp
from jax import lax
from jax.experimental import pallas as pl
from jax.experimental.pallas import tpu as pltpu
from jax.sharding import Mesh
from jax.sharding import PartitionSpec as P

DI = 5120
HEADDIM = 64
NSTATE = 128
GROUP = 256
ROWS = 512
FEAT = 640
WIDTH = 1280
TILE = 256
STEPS = WIDTH // TILE
PER = TILE // HEADDIM
LANES = 128
BD = 384
TAILED = GROUP + 8
QUARTER = NSTATE // 4
MSG = WIDTH + LANES
LOG2E = 1.4426950408889634
BATCH_SEQ = ("batch", "seq_0", "seq_1")
F32 = jnp.float32
BF16 = jnp.bfloat16
MIB = 1 << 20


def dot(a, b):
    return lax.dot_general(a, b, (((1,), (0,)), ((), ())), preferred_element_type=F32)


def dot_nt(a, b):
    return lax.dot_general(a, b, (((1,), (1,)), ((), ())), preferred_element_type=F32)


def dot_tn(a, b):
    return lax.dot_general(a, b, (((0,), (0,)), ((), ())), preferred_element_type=F32)


def silu(v):
    return v / (1.0 + jnp.exp(-v))


def three(v):
    hi = v.astype(BF16)
    rest = v - hi.astype(F32)
    mid = rest.astype(BF16)
    return hi, mid, (rest - mid.astype(F32)).astype(BF16)


def swapped(array, axis, bits):
    return lax.ppermute(array, axis, [(i, i ^ bits) for i in range(4)])


VMEM = pl.BlockSpec(memory_space=pltpu.VMEM)
HBM = pl.BlockSpec(memory_space=pltpu.HBM)
SMEM = pl.BlockSpec(memory_space=pltpu.SMEM)


def cost(flops, nbytes, trans=0):
    return pl.CostEstimate(flops=int(flops), bytes_accessed=int(nbytes), transcendentals=int(trans))


def call(body, name, idx, args, outs, scratch=(), mib=16, flops=1e8, aliases=None, kept=True):
    args = [pltpu.with_memory_space_constraint(a, pltpu.VMEM) for a in args]
    made = [pltpu.VMEM(*o) if kept else jax.ShapeDtypeStruct(*o) for o in outs]
    return pl.pallas_call(
        body,
        in_specs=[SMEM, *[VMEM] * len(args)],
        out_specs=[VMEM] * len(outs),
        out_shape=made,
        scratch_shapes=[pltpu.VMEM(*s) for s in scratch],
        input_output_aliases=aliases or {},
        compiler_params=pltpu.CompilerParams(vmem_limit_bytes=mib * MIB),
        cost_estimate=cost(flops, 1e6),
        name=name,
    )(idx, *args)


def span(j, size=TILE):
    return slice(j * size, (j + 1) * size)


def block_of(idx, bits):
    owner = idx[0] ^ bits
    return pl.ds(pl.multiple_of(owner * FEAT, FEAT), FEAT)


def own_parts(idx, tokens, w_x, w_bc, w_dt, out_x, out_bd):
    feats = block_of(idx, 0)
    for j in range(STEPS):
        out_x[:, span(j)] = dot(tokens, w_x[feats, span(j)])
    out_bd[:, : 2 * NSTATE] = dot(tokens, w_bc[feats, :])
    out_bd[:, 2 * NSTATE :] = dot_nt(tokens, w_dt[:, feats])


def load_body(
    idx, w_dt, tok, w_x, w_z, w_bc, acc_x, acc_bd, v_tok, v_dt, v_x, v_z, v_bc, narrow, sems
):
    copies = [
        pltpu.make_async_copy(w_dt, narrow, sems.at[0]),
        pltpu.make_async_copy(tok, v_tok, sems.at[1]),
    ]
    for bits in range(4):
        feats = block_of(idx, bits)
        for source, target in ((w_x, v_x), (w_bc, v_bc)):
            sem = sems.at[len(copies)]
            copies.append(pltpu.make_async_copy(source.at[feats, :], target.at[feats, :], sem))
    copies.append(pltpu.make_async_copy(w_z, v_z, sems.at[len(copies)]))
    for copy in copies:
        copy.start()
    v_dt[...] = jnp.zeros_like(v_dt)
    copies[0].wait()
    v_dt[: w_dt.shape[0], :] = narrow[...]
    for copy in copies[1:4]:
        copy.wait()
    own_parts(idx, v_tok[...], v_x, v_bc, v_dt, acc_x, acc_bd)
    for copy in copies[4:]:
        copy.wait()


def load_weights(idx, tok, w_dt, w_x, w_z, w_bc):
    return pl.pallas_call(
        load_body,
        in_specs=[SMEM, *[HBM] * 5],
        out_specs=[VMEM] * 7,
        out_shape=[
            pltpu.VMEM((ROWS, WIDTH), F32),
            pltpu.VMEM((ROWS, BD), F32),
            pltpu.VMEM(tok.shape, BF16),
            pltpu.VMEM((LANES, w_dt.shape[1]), BF16),
            pltpu.VMEM(w_x.shape, BF16),
            pltpu.VMEM(w_z.shape, BF16),
            pltpu.VMEM(w_bc.shape, BF16),
        ],
        scratch_shapes=[pltpu.VMEM(w_dt.shape, BF16), pltpu.SemaphoreType.DMA((11,))],
        compiler_params=pltpu.CompilerParams(vmem_limit_bytes=36 * MIB),
        cost_estimate=cost(2 * ROWS * FEAT * (WIDTH + BD), 15e6),
        name="load_weights",
    )(idx, w_dt, tok, w_x, w_z, w_bc)


def near_tokens(l_0, l_1, r_0, r_1):
    left = jnp.concatenate([l_0[...], l_1[...]], 0)
    return jnp.concatenate([left, jnp.concatenate([r_0[...], r_1[...]], 0)], 1)


def project_body(idx, l_0, l_1, r_0, r_1, w_x, w_bc, w_dt, acc_x, acc_bd, out_x, out_bd):
    tokens = near_tokens(l_0, l_1, r_0, r_1)
    one, other = block_of(idx, 1), block_of(idx, 3)
    for j in range(STEPS):
        weight = jnp.concatenate([w_x[one, span(j)], w_x[other, span(j)]], 0)
        out_x[:, span(j)] = acc_x[:, span(j)] + dot(tokens, weight)
    weight = jnp.concatenate([w_bc[one, :], w_bc[other, :]], 0)
    out_bd[:, : 2 * NSTATE] = acc_bd[:, : 2 * NSTATE] + dot(tokens, weight)
    weight = jnp.concatenate([w_dt[:, one], w_dt[:, other]], 1)
    out_bd[:, 2 * NSTATE :] = acc_bd[:, 2 * NSTATE :] + dot_nt(tokens, weight)


def project(idx, near, w_x, w_bc, w_dt, sums):
    return call(
        project_body,
        "project",
        idx,
        [*near, w_x, w_bc, w_dt, *sums],
        [((ROWS, WIDTH), F32), ((ROWS, BD), F32)],
        flops=4 * ROWS * FEAT * (WIDTH + BD),
        aliases={8: 0, 9: 1},
    )


def head_rows(j):
    head = lax.broadcasted_iota(jnp.int32, (LANES, TILE), 0)
    channel = lax.broadcasted_iota(jnp.int32, (LANES, TILE), 1)
    return (head == PER * j + channel // HEADDIM).astype(BF16)


def terms(v, rows, width):
    hi, mid, lo = (part.astype(F32) for part in three(v))
    row = lax.broadcasted_iota(jnp.int32, (rows, width), 0)
    return jnp.where(row == 0, hi, jnp.where(row == 1, mid, jnp.where(row == 2, lo, 0.0)))


def state_body(
    idx, tok_0, tok_1, w_x, w_bc, w_dt, acc_x, acc_bd, resets, bias, rate,
    inner_o, b_o, c_o, cum_o, step_o, first_o, thr_o, m0, m1, m2, m3, state_s,
):
    tokens = jnp.concatenate([tok_0[...], tok_1[...]], 0)
    feats = block_of(idx, 2)
    logits_part = dot_nt(tokens, w_dt[:, feats])
    mapped = silu(acc_bd[:, : 2 * NSTATE] + dot(tokens, w_bc[feats, :]))
    ahead = dot(tokens, w_x[feats, span(0)])
    b_t = mapped[:, :NSTATE].T.astype(BF16)
    b_o[...] = mapped[:, :NSTATE].astype(BF16)
    c_o[...] = mapped[:, NSTATE:].astype(BF16)
    logits = acc_bd[:, 2 * NSTATE :] + logits_part + bias[...]
    step = jnp.maximum(logits, 0.0) + jnp.log1p(jnp.exp(-jnp.abs(logits)))
    step_o[...] = step
    lane = lax.broadcasted_iota(jnp.int32, (ROWS, LANES), 1)
    first_row = lax.broadcasted_iota(jnp.int32, (16, ROWS), 0) == 0
    marks = jnp.where(first_row, resets[...].astype(F32), 0.0).astype(BF16)
    marks = dot_tn(marks, jnp.ones((16, LANES), BF16))
    decay = jnp.where(lane == LANES - 1, marks, -step * rate[...])
    row = lax.broadcasted_iota(jnp.int32, (GROUP, GROUP), 0)
    col = lax.broadcasted_iota(jnp.int32, (GROUP, GROUP), 1)
    lower = (row >= col).astype(BF16)
    keeps, throughs = [], []
    for g in range(2):
        sums = dot(lower, jnp.concatenate(three(decay[span(g, GROUP)]), 1))
        cum = sums[:, :LANES] + (sums[:, LANES : 2 * LANES] + sums[:, 2 * LANES :])
        cum_o[span(g, GROUP), :] = cum
        last = cum[GROUP - 1 :, :]
        seg, closing = cum[:, LANES - 1 :], last[:, LANES - 1 :]
        keeps.append(jnp.where(seg == closing, jnp.exp(last - cum), 0.0) * step[span(g, GROUP)])
        throughs.append(jnp.where(closing == 0.0, jnp.exp(last), 0.0))
    keep = jnp.concatenate(keeps, 0)
    keep_hi = keep.astype(BF16)
    keep_lo = (keep - keep_hi.astype(F32)).astype(BF16)
    keep = jnp.concatenate([keep_hi, keep_lo], 1)
    through = jnp.concatenate([terms(t, 8, LANES) for t in throughs], 0).astype(BF16)
    tail = terms(throughs[0] * throughs[1], QUARTER, LANES).astype(BF16)
    for j in range(STEPS):
        part = ahead
        if j + 1 < STEPS:
            ahead = dot(tokens, w_x[feats, span(j + 1)])
        inner = silu(acc_x[:, span(j)] + part).astype(BF16)
        inner_o[:, span(j)] = inner
        heads = head_rows(j)
        wide = dot(keep, jnp.concatenate([heads, heads], 0))
        scaled = (wide * inner.astype(F32)).astype(BF16)
        state0 = dot(b_t[:, :GROUP], scaled[:GROUP])
        state1 = dot(b_t[:, GROUP:], scaled[GROUP:])
        thr = dot(through, heads)
        thr0 = thr[0:1] + thr[1:2] + thr[2:3]
        thr1 = thr[8:9] + thr[9:10] + thr[10:11]
        first_o[:, span(j)] = state0
        thr_o[:, span(j)] = jnp.broadcast_to(thr0, (8, TILE))
        state_s[:, span(j)] = thr1 * state0 + state1
    for d, message in enumerate((m0, m1, m2, m3)):
        start = pl.multiple_of((idx[2] ^ d) * QUARTER, QUARTER)
        message[:, :WIDTH] = state_s[pl.ds(start, QUARTER), :].astype(BF16)
        message[:, WIDTH:] = tail


def device_state(idx, far, w_x, w_bc, w_dt, sums, resets, bias, rate):
    small = (ROWS, LANES)
    return call(
        state_body,
        "device_state",
        idx,
        [*far, w_x, w_bc, w_dt, *sums, resets, bias, rate],
        [
            ((ROWS, WIDTH), BF16), (small, BF16), (small, BF16), (small, F32), (small, F32),
            ((NSTATE, WIDTH), F32), ((8, WIDTH), F32), *[((QUARTER, MSG), BF16)] * 4,
        ],
        [((NSTATE, WIDTH), F32)],
        flops=2 * ROWS * FEAT * (WIDTH + BD),
    )


def tail_of(message):
    tail = message[:, WIDTH:].astype(F32)
    return tail[0:1] + tail[1:2] + tail[2:3]


def decays_of(messages, j):
    tails = jnp.concatenate([m[:16, WIDTH:] for m in messages], 0)
    wide = dot(tails, head_rows(j))
    rows = range(0, 16 * len(messages), 16)
    return [wide[k : k + 1] + wide[k + 1 : k + 2] + wide[k + 2 : k + 3] for k in rows]


def total_body(idx, m0, m1, m2, m3, out, held):
    for d, message in enumerate((m0, m1, m2, m3)):
        held[idx[2] ^ d] = message[...]
    messages = [held.at[k] for k in range(4)]
    through = tail_of(messages[0])
    for message in messages[1:]:
        through = through * tail_of(message)
    out[:, WIDTH:] = terms(through, QUARTER, LANES).astype(BF16)
    for j in range(STEPS):
        decays = decays_of(messages, j)
        state = messages[0][:, span(j)].astype(F32)
        for k in range(1, 4):
            state = decays[k] * state + messages[k][:, span(j)].astype(F32)
        out[:, span(j)] = state.astype(BF16)


def prefix_body(idx, m0, m1, m2, m3, t0, t1, t2, t3, h0, h1, h2, h3, held, rows, found):
    for d, message in enumerate((m0, m1, m2, m3)):
        held[idx[2] ^ d] = message[...]
    for d, message in enumerate((t0, t1, t2, t3)):
        rows[idx[1] ^ d] = message[...]
    messages = [held.at[k] for k in range(4)]
    totals = [rows.at[k] for k in range(4)]
    for j in range(STEPS):
        decays = decays_of([*messages, *totals], j)
        state = jnp.zeros((QUARTER, TILE), F32)
        for k in range(3):
            after = decays[4 + k] * state + totals[k][:, span(j)].astype(F32)
            state = jnp.where(k < idx[1], after, state)
        for k in range(4):
            found[k, :, span(j)] = state.astype(BF16)
            if k < 3:
                state = decays[k] * state + messages[k][:, span(j)].astype(F32)
    for d, out in enumerate((h0, h1, h2, h3)):
        out[...] = found[idx[2] ^ d]


def row_total(idx, messages):
    return call(
        total_body,
        "row_total",
        idx,
        messages,
        [((QUARTER, MSG), BF16)],
        [((4, QUARTER, MSG), BF16)],
        mib=8,
    )[0]


def prefixes(idx, messages, totals):
    return call(
        prefix_body,
        "prefixes",
        idx,
        [*messages, *totals],
        [((QUARTER, WIDTH), BF16)] * 4,
        [((4, QUARTER, MSG), BF16), ((4, QUARTER, MSG), BF16), ((4, QUARTER, WIDTH), BF16)],
        mib=8,
    )


def gate_first_body(idx, tok, l_0, r_1, w_z, out):
    own, one, other = (block_of(idx, bits) for bits in (0, 1, 3))
    for j in range(STEPS):
        part = dot(tok[...], w_z[own, span(j)])
        out[:GROUP, span(j)] = part[:GROUP] + dot(l_0[...], w_z[one, span(j)])
        out[GROUP:, span(j)] = part[GROUP:] + dot(r_1[...], w_z[other, span(j)])


def gate_first(idx, tok, l_0, r_1, w_z):
    return call(
        gate_first_body,
        "gate_first",
        idx,
        [tok, l_0, r_1, w_z],
        [((ROWS, WIDTH), F32)],
        flops=4 * ROWS * FEAT * WIDTH,
    )[0]


def gate_second_body(idx, l_1, r_0, w_z, acc_z, out):
    one, other = block_of(idx, 1), block_of(idx, 3)
    for j in range(STEPS):
        out[:GROUP, span(j)] = acc_z[:GROUP, span(j)] + dot(r_0[...], w_z[other, span(j)])
        out[GROUP:, span(j)] = acc_z[GROUP:, span(j)] + dot(l_1[...], w_z[one, span(j)])


def gate_second(idx, l_1, r_0, w_z, acc_z):
    return call(
        gate_second_body,
        "gate_second",
        idx,
        [l_1, r_0, w_z, acc_z],
        [((ROWS, WIDTH), F32)],
        flops=2 * ROWS * FEAT * WIDTH,
        aliases={4: 0},
    )[0]


def gate_body(idx, t_0, t_1, w_z, acc_z, out):
    tokens = jnp.concatenate([t_0[...], t_1[...]], 0)
    feats = block_of(idx, 2)
    for j in range(STEPS):
        gating = acc_z[:, span(j)] + dot(tokens, w_z[feats, span(j)])
        out[:, span(j)] = silu(gating.astype(BF16).astype(F32))


def gate(idx, far, w_z, acc_z):
    return call(
        gate_body,
        "gate",
        idx,
        [*far, w_z, acc_z],
        [((ROWS, WIDTH), F32)],
        flops=2 * ROWS * FEAT * WIDTH,
        aliases={4: 0},
    )[0]


def mix_body(g, idx, inner_r, b_r, c_r, cum_r, step_r, skip, out, ent_o, scores, cum_t, step_t):
    half = GROUP // 2
    rows = span(g, GROUP)
    cum = cum_r[rows, :]
    across = cum.T
    cum_2 = cum * LOG2E
    cum_t[...] = across * LOG2E
    step_t[...] = step_r[rows, :].T
    row = lax.broadcasted_iota(jnp.int32, (GROUP, GROUP), 0)
    col = lax.broadcasted_iota(jnp.int32, (GROUP, GROUP), 1)
    seg = cum[:, LANES - 1 :]
    same = (seg == across[LANES - 1 :, :]) & (row >= col)
    scores[...] = jnp.where(same, dot_nt(c_r[rows, :], b_r[rows, :]), 0.0)
    enter = jnp.where(seg == 0.0, jnp.exp(cum), 0.0)
    hi = enter.astype(BF16)
    lo = (enter - hi.astype(F32)).astype(BF16)
    lane = lax.broadcasted_iota(jnp.int32, (GROUP, LANES), 1)
    skips = []
    for j in range(STEPS):
        heads = head_rows(j)
        ent_o[:, span(j)] = dot(hi, heads) + dot(lo, heads)
        wide = dot(terms(skip[...], 16, LANES).astype(BF16), heads)
        wide = wide[0:1] + wide[1:2] + wide[2:3]
        skips += [wide[:, :LANES], wide[:, LANES:]]
    for pair in range(WIDTH // LANES):
        both = inner_r[rows, span(pair, LANES)]
        ys = []
        for head in (2 * pair, 2 * pair + 1):
            before = cum_t[head : head + 1, :]
            step = step_t[head : head + 1, :]
            top = jnp.exp2(jnp.minimum(cum_2[:half, head : head + 1] - before[:, :half], 0.0))
            top = (top * scores[:half, :half] * step[:, :half]).astype(BF16)
            low = jnp.exp2(jnp.minimum(cum_2[half:, head : head + 1] - before, 0.0))
            low = (low * scores[half:, :] * step).astype(BF16)
            ys.append(jnp.concatenate([dot(top, both[:half]), dot(low, both)], 0))
        y = jnp.where(lane < HEADDIM, ys[0], ys[1])
        out[:, span(pair, LANES)] = y + skips[pair] * both.astype(F32)


def mix(g, idx, inner, b, c, cum, step, skip):
    return call(
        functools.partial(mix_body, g),
        "mix",
        idx,
        [inner, b, c, cum, step, skip],
        [((GROUP, WIDTH), F32), ((GROUP, WIDTH), F32)],
        [((GROUP, GROUP), F32), ((LANES, GROUP), F32), ((LANES, GROUP), F32)],
        flops=2e9,
    )


def block_cols(idx, bits):
    target = idx[0] ^ bits
    return pl.ds(pl.multiple_of(target * FEAT, FEAT), FEAT)


def tail_rows(squares):
    zeros = jnp.zeros((8, FEAT - ROWS), F32)
    return jnp.concatenate([terms(squares, 8, ROWS), zeros], 1).astype(BF16)


def squares_of(message):
    tail = message[GROUP:, :ROWS].astype(F32)
    return tail[0:1] + (tail[1:2] + tail[2:3])


def gated_body(
    idx, h0, h1, h2, h3, first, thr, c_r, u0, u1, e0, e1, zs_r, gain, w_out,
    rows_o, sums_o, top, low, state,
):
    for d, part in enumerate((h0, h1, h2, h3)):
        start = pl.multiple_of((idx[2] ^ d) * QUARTER, QUARTER)
        state[pl.ds(start, QUARTER), :] = part[...]
    def carried(g, j):
        enter = state[:, span(j)]
        if g:
            enter = first[:, span(j)] + thr[0:1, span(j)] * enter.astype(F32)
            enter = enter.astype(BF16)
        return dot(c_r[span(g, GROUP), :], enter)

    ones = jnp.ones((8, LANES), BF16)
    steps = [(g, j) for g in range(2) for j in range(STEPS)]
    squares = [jnp.zeros((GROUP, LANES), F32), jnp.zeros((GROUP, LANES), F32)]
    ahead = carried(0, 0)
    for n, (g, j) in enumerate(steps):
        now = ahead
        if n + 1 < len(steps):
            ahead = carried(*steps[n + 1])
        rows, u, ent = span(g, GROUP), (u0, u1)[g], (e0, e1)[g]
        gated = (u[:, span(j)] + ent[:, span(j)] * now) * zs_r[rows, span(j)]
        rows_o[rows, span(j)] = (gated * gain[:, span(j)]).astype(BF16)
        square = gated * gated
        squares[g] = squares[g] + (square[:, :LANES] + square[:, LANES:])
    part = dot(rows_o[...], w_out[:, block_cols(idx, 2)])
    for g in range(2):
        hi, mid, lo = three(squares[g])
        sums_o[:, span(g, GROUP)] = dot_nt(ones, hi) + (dot_nt(ones, mid) + dot_nt(ones, lo))
    part = part.astype(BF16)
    tail = tail_rows(sums_o[0:1, :])
    for g, out in enumerate((top, low)):
        out[:GROUP, :] = part[span(g, GROUP)]
        out[GROUP:, :] = tail


def gated_rows(idx, parts, first, thr, c, us, ents, zs, gain, w_out):
    return call(
        gated_body,
        "gated_rows",
        idx,
        [*parts, first, thr, c, *us, *ents, zs, gain, w_out],
        [((ROWS, WIDTH), BF16), ((8, ROWS), F32), *[((TAILED, FEAT), BF16)] * 2],
        [((NSTATE, WIDTH), BF16)],
        flops=2.6 * ROWS * WIDTH * FEAT,
    )


def near_body(bits, g, idx, rows, w_out, message, part):
    value = dot(rows[...], w_out[:, block_cols(idx, bits)])
    part[...] = value[span(g, GROUP)]
    message[...] = value[span(1 - g, GROUP)].astype(BF16)


def near_block(bits, g, idx, rows, w_out):
    return call(
        functools.partial(near_body, bits, g),
        "near_block",
        idx,
        [rows, w_out],
        [((GROUP, FEAT), BF16), ((GROUP, FEAT), F32)],
        flops=1e6,
    )


def own_body(idx, rows, w_out, out):
    out[...] = dot(rows[...], w_out[:, block_cols(idx, 0)])


def own_block(idx, rows, w_out):
    return call(
        own_body,
        "own_block",
        idx,
        [rows, w_out],
        [((ROWS, FEAT), F32)],
        flops=1e6,
    )[0]


def join_body(idx, part, half, out):
    out[:GROUP, :] = (part[...] + half[:GROUP, :].astype(F32)).astype(BF16)
    out[GROUP:, :] = half[GROUP:, :]


def join(idx, part, half):
    return call(join_body, "join", idx, [part, half], [((TAILED, FEAT), BF16)], mib=8)[0]


def add_body(idx, own, left_0, right_1, out):
    out[:GROUP, :] = own[:GROUP, :] + left_0[...].astype(F32)
    out[GROUP:, :] = own[GROUP:, :] + right_1[...].astype(F32)


def add_near(idx, own, left_0, right_1):
    return call(
        add_body,
        "add_near",
        idx,
        [own, left_0, right_1],
        [((ROWS, FEAT), F32)],
        mib=8,
        flops=5e9,
        aliases={1: 0},
    )[0]


def settle_body(idx, own, sums, near, other, left_1, out, factor, made, sems):
    squares = sums[0:1, :] + squares_of(left_1)
    squares = squares + (squares_of(near) + squares_of(other))
    stack = terms(squares, 16, ROWS).astype(BF16)
    scale = lax.rsqrt(dot_tn(stack, jnp.ones((16, LANES), BF16)) / DI + 1e-05)
    factor[...] = scale[:GROUP]
    for k in range(FEAT // LANES):
        lanes = span(k, LANES)
        value = own[GROUP:, lanes] + left_1[:GROUP, lanes].astype(F32)
        made[:, lanes] = (value * scale[GROUP:]).astype(BF16)
    copy = pltpu.make_async_copy(made, out.at[GROUP:, :], sems.at[0])
    copy.start()
    copy.wait()


def end_call(body, name, idx, args, outs, specs, more=()):
    args = [pltpu.with_memory_space_constraint(a, pltpu.VMEM) for a in args]
    return pl.pallas_call(
        body,
        in_specs=[SMEM, *[VMEM] * len(args), *[HBM] * len(more)],
        out_specs=specs,
        out_shape=outs,
        scratch_shapes=[pltpu.VMEM((GROUP, FEAT), BF16), pltpu.SemaphoreType.DMA((2,))],
        input_output_aliases={1 + len(args): 0} if more else {},
        compiler_params=pltpu.CompilerParams(vmem_limit_bytes=8 * MIB),
        cost_estimate=cost(1e6, 1e6),
        name=name,
    )(idx, *args, *more)


def settle(idx, *args):
    outs = [jax.ShapeDtypeStruct((ROWS, FEAT), BF16), pltpu.VMEM((GROUP, LANES), F32)]
    return end_call(settle_body, "settle", idx, args, outs, [HBM, VMEM])


def norm_body(idx, own, factor, right_0, so_far, out, made, sems):
    copies = []
    for part in range(2):
        rows = span(part, GROUP // 2)
        for k in range(FEAT // LANES):
            lanes = span(k, LANES)
            value = own[rows, lanes] + right_0[rows, lanes].astype(F32)
            made[rows, lanes] = (value * factor[rows, :]).astype(BF16)
        copies.append(pltpu.make_async_copy(made.at[rows, :], out.at[rows, :], sems.at[part]))
        copies[-1].start()
    for copy in copies:
        copy.wait()


def norm(idx, own, factor, right_0, so_far):
    outs = jax.ShapeDtypeStruct((ROWS, FEAT), BF16)
    return end_call(norm_body, "norm", idx, (own, factor, right_0), outs, HBM, (so_far,))


def on_device(tokens, resets, w_x, w_z, w_bc, w_dt, dt_bias, decay_rate, d_skip, norm_gain, w_out):
    places = ("head", "seq_0", "seq_1")
    idx = jnp.stack([lax.axis_index(axis) for axis in places]).astype(jnp.int32)
    heads = w_dt.shape[1]
    top, low = tokens[:GROUP], tokens[GROUP:]
    l_0, r_1 = swapped(top, "head", 1), swapped(low, "head", 3)
    top, low, idx = lax.optimization_barrier((top, low, idx))
    l_1, r_0 = swapped(low, "head", 1), swapped(top, "head", 3)
    bias = jnp.pad(dt_bias, (0, LANES - heads)).reshape(1, LANES)
    rate = jnp.pad(decay_rate, (0, LANES - heads)).reshape(1, LANES)
    starts = resets.reshape(1, ROWS)
    skip = jnp.pad(d_skip, (0, LANES - heads)).reshape(1, LANES)
    gain = norm_gain.reshape(1, WIDTH)

    acc_x, acc_bd, tokens, w_dt, w_x, w_z, w_bc = load_weights(
        idx, tokens, w_dt.T, w_x, w_z, w_bc
    )
    far = [swapped(l_0, "head", 3), swapped(r_1, "head", 1)]
    acc_z = gate_first(idx, tokens, l_0, r_1, w_z)
    near = (l_0, l_1, r_0, r_1)
    sums = project(idx, near, w_x, w_bc, w_dt, (acc_x, acc_bd))
    acc_z = gate_second(idx, l_1, r_0, w_z, acc_z)
    far, acc_z, sums = lax.optimization_barrier((far, acc_z, sums))
    inner, b, c, cum, step, first, thr, *messages = device_state(
        idx, far, w_x, w_bc, w_dt, sums, starts, bias, rate
    )
    quarters = [messages[0], *(swapped(messages[d], "seq_1", d) for d in (1, 2, 3))]
    u0, e0 = mix(0, idx, inner, b, c, cum, step, skip)
    quarters, u0, e0, cum = lax.optimization_barrier((quarters, u0, e0, cum))
    total = row_total(idx, quarters)
    totals = [total, *(swapped(total, "seq_0", d) for d in (1, 2, 3))]
    u1, e1 = mix(1, idx, inner, b, c, cum, step, skip)
    totals, u1, e1, w_z = lax.optimization_barrier((totals, u1, e1, w_z))
    parts = prefixes(idx, quarters, totals)
    parts = [parts[0], *(swapped(parts[d], "seq_1", d) for d in (1, 2, 3))]
    zs = gate(idx, far, w_z, acc_z)
    rows, sums, top, low = gated_rows(
        idx, parts, first, thr, c, (u0, u1), (e0, e1), zs, gain, w_out
    )
    top, low = swapped(top, "head", 1), swapped(low, "head", 3)
    left_0, part_1 = near_block(1, 1, idx, rows, w_out)
    left_0 = swapped(left_0, "head", 1)
    right_1, part_0 = near_block(3, 0, idx, rows, w_out)
    right_1 = swapped(right_1, "head", 3)
    own = own_block(idx, rows, w_out)
    right_0 = swapped(join(idx, part_0, top), "head", 3)
    left_1 = swapped(join(idx, part_1, low), "head", 1)
    own = add_near(idx, own, left_0, right_1)
    half, factor = settle(idx, own, sums, top, low, left_1)
    return norm(idx, own, factor, right_0, half)


def solution(mesh):
    split = Mesh(
        mesh.devices.reshape(4, 4, mesh.shape["head"], mesh.shape["batch"]),
        ("seq_0", "seq_1", "head", "batch"),
    )
    placed = (
        P(BATCH_SEQ, "head"),
        P(BATCH_SEQ),
        P(None, "head"),
        P(None, "head"),
        P(),
        P(None, "head"),
        P("head"),
        P("head"),
        P("head"),
        P("head"),
        P("head", None),
    )
    return jax.shard_map(
        on_device, mesh=split, in_specs=placed, out_specs=P(BATCH_SEQ, "head"), check_vma=False
    )
```

```python
import functools

import jax
import jax.numpy as jnp
from jax import lax
from jax.experimental import pallas as pl
from jax.experimental.pallas import tpu as pltpu
from jax.sharding import Mesh
from jax.sharding import PartitionSpec as P

DI = 5120
HEADDIM = 64
NSTATE = 128
GROUP = 256
ROWS = 512
FEAT = 640
WIDTH = 1280
TILE = 256
STEPS = WIDTH // TILE
PER = TILE // HEADDIM
LANES = 128
BD = 384
TAILED = GROUP + 8
QUARTER = NSTATE // 4
MSG = WIDTH + LANES
LOG2E = 1.4426950408889634
BATCH_SEQ = ("batch", "seq_0", "seq_1")
F32 = jnp.float32
BF16 = jnp.bfloat16
MIB = 1 << 20


def dot(a, b):
    return lax.dot_general(a, b, (((1,), (0,)), ((), ())), preferred_element_type=F32)


def dot_nt(a, b):
    return lax.dot_general(a, b, (((1,), (1,)), ((), ())), preferred_element_type=F32)


def dot_tn(a, b):
    return lax.dot_general(a, b, (((0,), (0,)), ((), ())), preferred_element_type=F32)


def silu(v):
    return v / (1.0 + jnp.exp(-v))


def three(v):
    hi = v.astype(BF16)
    rest = v - hi.astype(F32)
    mid = rest.astype(BF16)
    return hi, mid, (rest - mid.astype(F32)).astype(BF16)


def swapped(array, axis, bits):
    return lax.ppermute(array, axis, [(i, i ^ bits) for i in range(4)])


VMEM = pl.BlockSpec(memory_space=pltpu.VMEM)
HBM = pl.BlockSpec(memory_space=pltpu.HBM)
SMEM = pl.BlockSpec(memory_space=pltpu.SMEM)


def cost(flops, nbytes, trans=0):
    return pl.CostEstimate(flops=int(flops), bytes_accessed=int(nbytes), transcendentals=int(trans))


def call(body, name, idx, args, outs, scratch=(), mib=16, flops=1e8, aliases=None, kept=True):
    args = [pltpu.with_memory_space_constraint(a, pltpu.VMEM) for a in args]
    made = [pltpu.VMEM(*o) if kept else jax.ShapeDtypeStruct(*o) for o in outs]
    return pl.pallas_call(
        body,
        in_specs=[SMEM, *[VMEM] * len(args)],
        out_specs=[VMEM] * len(outs),
        out_shape=made,
        scratch_shapes=[pltpu.VMEM(*s) for s in scratch],
        input_output_aliases=aliases or {},
        compiler_params=pltpu.CompilerParams(vmem_limit_bytes=mib * MIB),
        cost_estimate=cost(flops, 1e6),
        name=name,
    )(idx, *args)


def span(j, size=TILE):
    return slice(j * size, (j + 1) * size)


def block_of(idx, bits):
    owner = idx[0] ^ bits
    return pl.ds(pl.multiple_of(owner * FEAT, FEAT), FEAT)


def own_parts(idx, tokens, w_x, w_bc, w_dt, out_x, out_bd):
    feats = block_of(idx, 0)
    for j in range(STEPS):
        out_x[:, span(j)] = dot(tokens, w_x[feats, span(j)])
    out_bd[:, : 2 * NSTATE] = dot(tokens, w_bc[feats, :])
    out_bd[:, 2 * NSTATE :] = dot_nt(tokens, w_dt[:, feats])


def load_body(
    idx, w_dt, tok, w_x, w_z, w_bc, acc_x, acc_bd, v_tok, v_dt, v_x, v_z, v_bc, narrow, sems
):
    copies = [
        pltpu.make_async_copy(w_dt, narrow, sems.at[0]),
        pltpu.make_async_copy(tok, v_tok, sems.at[1]),
    ]
    for bits in range(4):
        feats = block_of(idx, bits)
        for source, target in ((w_x, v_x), (w_bc, v_bc)):
            sem = sems.at[len(copies)]
            copies.append(pltpu.make_async_copy(source.at[feats, :], target.at[feats, :], sem))
    copies.append(pltpu.make_async_copy(w_z, v_z, sems.at[len(copies)]))
    for copy in copies:
        copy.start()
    v_dt[...] = jnp.zeros_like(v_dt)
    copies[0].wait()
    v_dt[: w_dt.shape[0], :] = narrow[...]
    for copy in copies[1:4]:
        copy.wait()
    own_parts(idx, v_tok[...], v_x, v_bc, v_dt, acc_x, acc_bd)
    for copy in copies[4:]:
        copy.wait()


def load_weights(idx, tok, w_dt, w_x, w_z, w_bc):
    return pl.pallas_call(
        load_body,
        in_specs=[SMEM, *[HBM] * 5],
        out_specs=[VMEM] * 7,
        out_shape=[
            pltpu.VMEM((ROWS, WIDTH), F32),
            pltpu.VMEM((ROWS, BD), F32),
            pltpu.VMEM(tok.shape, BF16),
            pltpu.VMEM((LANES, w_dt.shape[1]), BF16),
            pltpu.VMEM(w_x.shape, BF16),
            pltpu.VMEM(w_z.shape, BF16),
            pltpu.VMEM(w_bc.shape, BF16),
        ],
        scratch_shapes=[pltpu.VMEM(w_dt.shape, BF16), pltpu.SemaphoreType.DMA((11,))],
        compiler_params=pltpu.CompilerParams(vmem_limit_bytes=36 * MIB),
        cost_estimate=cost(2 * ROWS * FEAT * (WIDTH + BD), 15e6),
        name="load_weights",
    )(idx, w_dt, tok, w_x, w_z, w_bc)


def near_tokens(l_0, l_1, r_0, r_1):
    left = jnp.concatenate([l_0[...], l_1[...]], 0)
    return jnp.concatenate([left, jnp.concatenate([r_0[...], r_1[...]], 0)], 1)


def project_body(idx, l_0, l_1, r_0, r_1, w_x, w_bc, w_dt, acc_x, acc_bd, out_x, out_bd):
    tokens = near_tokens(l_0, l_1, r_0, r_1)
    one, other = block_of(idx, 1), block_of(idx, 3)
    for j in range(STEPS):
        weight = jnp.concatenate([w_x[one, span(j)], w_x[other, span(j)]], 0)
        out_x[:, span(j)] = acc_x[:, span(j)] + dot(tokens, weight)
    weight = jnp.concatenate([w_bc[one, :], w_bc[other, :]], 0)
    out_bd[:, : 2 * NSTATE] = acc_bd[:, : 2 * NSTATE] + dot(tokens, weight)
    weight = jnp.concatenate([w_dt[:, one], w_dt[:, other]], 1)
    out_bd[:, 2 * NSTATE :] = acc_bd[:, 2 * NSTATE :] + dot_nt(tokens, weight)


def project(idx, near, w_x, w_bc, w_dt, sums):
    return call(
        project_body,
        "project",
        idx,
        [*near, w_x, w_bc, w_dt, *sums],
        [((ROWS, WIDTH), F32), ((ROWS, BD), F32)],
        flops=4 * ROWS * FEAT * (WIDTH + BD),
        aliases={8: 0, 9: 1},
    )


def head_rows(j):
    head = lax.broadcasted_iota(jnp.int32, (LANES, TILE), 0)
    channel = lax.broadcasted_iota(jnp.int32, (LANES, TILE), 1)
    return (head == PER * j + channel // HEADDIM).astype(BF16)


def terms(v, rows, width):
    hi, mid, lo = (part.astype(F32) for part in three(v))
    row = lax.broadcasted_iota(jnp.int32, (rows, width), 0)
    return jnp.where(row == 0, hi, jnp.where(row == 1, mid, jnp.where(row == 2, lo, 0.0)))


def state_body(
    idx, tok_0, tok_1, w_x, w_bc, w_dt, acc_x, acc_bd, resets, bias, rate,
    inner_o, b_o, c_o, cum_o, step_o, first_o, thr_o, m0, m1, m2, m3, state_s,
):
    tokens = jnp.concatenate([tok_0[...], tok_1[...]], 0)
    feats = block_of(idx, 2)
    logits_part = dot_nt(tokens, w_dt[:, feats])
    mapped = silu(acc_bd[:, : 2 * NSTATE] + dot(tokens, w_bc[feats, :]))
    ahead = dot(tokens, w_x[feats, span(0)])
    b_t = mapped[:, :NSTATE].T.astype(BF16)
    b_o[...] = mapped[:, :NSTATE].astype(BF16)
    c_o[...] = mapped[:, NSTATE:].astype(BF16)
    logits = acc_bd[:, 2 * NSTATE :] + logits_part + bias[...]
    step = jnp.maximum(logits, 0.0) + jnp.log1p(jnp.exp(-jnp.abs(logits)))
    step_o[...] = step
    lane = lax.broadcasted_iota(jnp.int32, (ROWS, LANES), 1)
    first_row = lax.broadcasted_iota(jnp.int32, (16, ROWS), 0) == 0
    marks = jnp.where(first_row, resets[...].astype(F32), 0.0).astype(BF16)
    marks = dot_tn(marks, jnp.ones((16, LANES), BF16))
    decay = jnp.where(lane == LANES - 1, marks, -step * rate[...])
    row = lax.broadcasted_iota(jnp.int32, (GROUP, GROUP), 0)
    col = lax.broadcasted_iota(jnp.int32, (GROUP, GROUP), 1)
    lower = (row >= col).astype(BF16)
    keeps, throughs = [], []
    for g in range(2):
        sums = dot(lower, jnp.concatenate(three(decay[span(g, GROUP)]), 1))
        cum = sums[:, :LANES] + (sums[:, LANES : 2 * LANES] + sums[:, 2 * LANES :])
        cum_o[span(g, GROUP), :] = cum
        last = cum[GROUP - 1 :, :]
        seg, closing = cum[:, LANES - 1 :], last[:, LANES - 1 :]
        keeps.append(jnp.where(seg == closing, jnp.exp(last - cum), 0.0) * step[span(g, GROUP)])
        throughs.append(jnp.where(closing == 0.0, jnp.exp(last), 0.0))
    keep = jnp.concatenate(keeps, 0)
    keep_hi = keep.astype(BF16)
    keep_lo = (keep - keep_hi.astype(F32)).astype(BF16)
    keep = jnp.concatenate([keep_hi, keep_lo], 1)
    through = jnp.concatenate([terms(t, 8, LANES) for t in throughs], 0).astype(BF16)
    tail = terms(throughs[0] * throughs[1], QUARTER, LANES).astype(BF16)
    for j in range(STEPS):
        part = ahead
        if j + 1 < STEPS:
            ahead = dot(tokens, w_x[feats, span(j + 1)])
        inner = silu(acc_x[:, span(j)] + part).astype(BF16)
        inner_o[:, span(j)] = inner
        heads = head_rows(j)
        wide = dot(keep, jnp.concatenate([heads, heads], 0))
        scaled = (wide * inner.astype(F32)).astype(BF16)
        state0 = dot(b_t[:, :GROUP], scaled[:GROUP])
        state1 = dot(b_t[:, GROUP:], scaled[GROUP:])
        thr = dot(through, heads)
        thr0 = thr[0:1] + thr[1:2] + thr[2:3]
        thr1 = thr[8:9] + thr[9:10] + thr[10:11]
        first_o[:, span(j)] = state0
        thr_o[:, span(j)] = jnp.broadcast_to(thr0, (8, TILE))
        state_s[:, span(j)] = thr1 * state0 + state1
    for d, message in enumerate((m0, m1, m2, m3)):
        start = pl.multiple_of((idx[2] ^ d) * QUARTER, QUARTER)
        message[:, :WIDTH] = state_s[pl.ds(start, QUARTER), :].astype(BF16)
        message[:, WIDTH:] = tail


def device_state(idx, far, w_x, w_bc, w_dt, sums, resets, bias, rate):
    small = (ROWS, LANES)
    return call(
        state_body,
        "device_state",
        idx,
        [*far, w_x, w_bc, w_dt, *sums, resets, bias, rate],
        [
            ((ROWS, WIDTH), BF16), (small, BF16), (small, BF16), (small, F32), (small, F32),
            ((NSTATE, WIDTH), F32), ((8, WIDTH), F32), *[((QUARTER, MSG), BF16)] * 4,
        ],
        [((NSTATE, WIDTH), F32)],
        flops=2 * ROWS * FEAT * (WIDTH + BD),
    )


def tail_of(message):
    tail = message[:, WIDTH:].astype(F32)
    return tail[0:1] + tail[1:2] + tail[2:3]


def decays_of(messages, j):
    tails = jnp.concatenate([m[:16, WIDTH:] for m in messages], 0)
    wide = dot(tails, head_rows(j))
    rows = range(0, 16 * len(messages), 16)
    return [wide[k : k + 1] + wide[k + 1 : k + 2] + wide[k + 2 : k + 3] for k in rows]


def total_body(idx, m0, m1, m2, m3, out, held):
    for d, message in enumerate((m0, m1, m2, m3)):
        held[idx[2] ^ d] = message[...]
    messages = [held.at[k] for k in range(4)]
    through = tail_of(messages[0])
    for message in messages[1:]:
        through = through * tail_of(message)
    out[:, WIDTH:] = terms(through, QUARTER, LANES).astype(BF16)
    for j in range(STEPS):
        decays = decays_of(messages, j)
        state = messages[0][:, span(j)].astype(F32)
        for k in range(1, 4):
            state = decays[k] * state + messages[k][:, span(j)].astype(F32)
        out[:, span(j)] = state.astype(BF16)


def prefix_body(idx, m0, m1, m2, m3, t0, t1, t2, t3, h0, h1, h2, h3, held, rows, found):
    for d, message in enumerate((m0, m1, m2, m3)):
        held[idx[2] ^ d] = message[...]
    for d, message in enumerate((t0, t1, t2, t3)):
        rows[idx[1] ^ d] = message[...]
    messages = [held.at[k] for k in range(4)]
    totals = [rows.at[k] for k in range(4)]
    for j in range(STEPS):
        decays = decays_of([*messages, *totals], j)
        state = jnp.zeros((QUARTER, TILE), F32)
        for k in range(3):
            after = decays[4 + k] * state + totals[k][:, span(j)].astype(F32)
            state = jnp.where(k < idx[1], after, state)
        for k in range(4):
            found[k, :, span(j)] = state.astype(BF16)
            if k < 3:
                state = decays[k] * state + messages[k][:, span(j)].astype(F32)
    for d, out in enumerate((h0, h1, h2, h3)):
        out[...] = found[idx[2] ^ d]


def row_total(idx, messages):
    return call(
        total_body,
        "row_total",
        idx,
        messages,
        [((QUARTER, MSG), BF16)],
        [((4, QUARTER, MSG), BF16)],
        mib=8,
    )[0]


def prefixes(idx, messages, totals):
    return call(
        prefix_body,
        "prefixes",
        idx,
        [*messages, *totals],
        [((QUARTER, WIDTH), BF16)] * 4,
        [((4, QUARTER, MSG), BF16), ((4, QUARTER, MSG), BF16), ((4, QUARTER, WIDTH), BF16)],
        mib=8,
    )


def gate_first_body(idx, tok, l_0, r_1, w_z, out):
    own, one, other = (block_of(idx, bits) for bits in (0, 1, 3))
    for j in range(STEPS):
        part = dot(tok[...], w_z[own, span(j)])
        out[:GROUP, span(j)] = part[:GROUP] + dot(l_0[...], w_z[one, span(j)])
        out[GROUP:, span(j)] = part[GROUP:] + dot(r_1[...], w_z[other, span(j)])


def gate_first(idx, tok, l_0, r_1, w_z):
    return call(
        gate_first_body,
        "gate_first",
        idx,
        [tok, l_0, r_1, w_z],
        [((ROWS, WIDTH), F32)],
        flops=4 * ROWS * FEAT * WIDTH,
    )[0]


def gate_second_body(idx, l_1, r_0, w_z, acc_z, out):
    one, other = block_of(idx, 1), block_of(idx, 3)
    for j in range(STEPS):
        out[:GROUP, span(j)] = acc_z[:GROUP, span(j)] + dot(r_0[...], w_z[other, span(j)])
        out[GROUP:, span(j)] = acc_z[GROUP:, span(j)] + dot(l_1[...], w_z[one, span(j)])


def gate_second(idx, l_1, r_0, w_z, acc_z):
    return call(
        gate_second_body,
        "gate_second",
        idx,
        [l_1, r_0, w_z, acc_z],
        [((ROWS, WIDTH), F32)],
        flops=2 * ROWS * FEAT * WIDTH,
        aliases={4: 0},
    )[0]


def gate_body(idx, t_0, t_1, w_z, acc_z, out):
    tokens = jnp.concatenate([t_0[...], t_1[...]], 0)
    feats = block_of(idx, 2)
    for j in range(STEPS):
        gating = acc_z[:, span(j)] + dot(tokens, w_z[feats, span(j)])
        out[:, span(j)] = silu(gating.astype(BF16).astype(F32))


def gate(idx, far, w_z, acc_z):
    return call(
        gate_body,
        "gate",
        idx,
        [*far, w_z, acc_z],
        [((ROWS, WIDTH), F32)],
        flops=2 * ROWS * FEAT * WIDTH,
        aliases={4: 0},
    )[0]


def mix_body(g, idx, inner_r, b_r, c_r, cum_r, step_r, skip, out, ent_o, scores, cum_t, step_t):
    half = GROUP // 2
    rows = span(g, GROUP)
    cum = cum_r[rows, :]
    across = cum.T
    cum_2 = cum * LOG2E
    cum_t[...] = across * LOG2E
    step_t[...] = step_r[rows, :].T
    row = lax.broadcasted_iota(jnp.int32, (GROUP, GROUP), 0)
    col = lax.broadcasted_iota(jnp.int32, (GROUP, GROUP), 1)
    seg = cum[:, LANES - 1 :]
    same = (seg == across[LANES - 1 :, :]) & (row >= col)
    scores[...] = jnp.where(same, dot_nt(c_r[rows, :], b_r[rows, :]), 0.0)
    enter = jnp.where(seg == 0.0, jnp.exp(cum), 0.0)
    hi = enter.astype(BF16)
    lo = (enter - hi.astype(F32)).astype(BF16)
    lane = lax.broadcasted_iota(jnp.int32, (GROUP, LANES), 1)
    skips = []
    for j in range(STEPS):
        heads = head_rows(j)
        ent_o[:, span(j)] = dot(hi, heads) + dot(lo, heads)
        wide = dot(terms(skip[...], 16, LANES).astype(BF16), heads)
        wide = wide[0:1] + wide[1:2] + wide[2:3]
        skips += [wide[:, :LANES], wide[:, LANES:]]
    for pair in range(WIDTH // LANES):
        both = inner_r[rows, span(pair, LANES)]
        ys = []
        for head in (2 * pair, 2 * pair + 1):
            before = cum_t[head : head + 1, :]
            step = step_t[head : head + 1, :]
            top = jnp.exp2(jnp.minimum(cum_2[:half, head : head + 1] - before[:, :half], 0.0))
            top = (top * scores[:half, :half] * step[:, :half]).astype(BF16)
            low = jnp.exp2(jnp.minimum(cum_2[half:, head : head + 1] - before, 0.0))
            low = (low * scores[half:, :] * step).astype(BF16)
            ys.append(jnp.concatenate([dot(top, both[:half]), dot(low, both)], 0))
        y = jnp.where(lane < HEADDIM, ys[0], ys[1])
        out[:, span(pair, LANES)] = y + skips[pair] * both.astype(F32)


def mix(g, idx, inner, b, c, cum, step, skip):
    return call(
        functools.partial(mix_body, g),
        "mix",
        idx,
        [inner, b, c, cum, step, skip],
        [((GROUP, WIDTH), F32), ((GROUP, WIDTH), F32)],
        [((GROUP, GROUP), F32), ((LANES, GROUP), F32), ((LANES, GROUP), F32)],
        flops=2e9,
    )


def block_cols(idx, bits):
    target = idx[0] ^ bits
    return pl.ds(pl.multiple_of(target * FEAT, FEAT), FEAT)


def tail_rows(squares):
    zeros = jnp.zeros((8, FEAT - ROWS), F32)
    return jnp.concatenate([terms(squares, 8, ROWS), zeros], 1).astype(BF16)


def squares_of(message):
    tail = message[GROUP:, :ROWS].astype(F32)
    return tail[0:1] + (tail[1:2] + tail[2:3])


def gated_body(
    idx, h0, h1, h2, h3, first, thr, c_r, u0, u1, e0, e1, zs_r, gain, w_out,
    rows_o, sums_o, top, low, state,
):
    for d, part in enumerate((h0, h1, h2, h3)):
        start = pl.multiple_of((idx[2] ^ d) * QUARTER, QUARTER)
        state[pl.ds(start, QUARTER), :] = part[...]
    def carried(g, j):
        enter = state[:, span(j)]
        if g:
            enter = first[:, span(j)] + thr[0:1, span(j)] * enter.astype(F32)
            enter = enter.astype(BF16)
        return dot(c_r[span(g, GROUP), :], enter)

    ones = jnp.ones((8, LANES), BF16)
    steps = [(g, j) for g in range(2) for j in range(STEPS)]
    squares = [jnp.zeros((GROUP, LANES), F32), jnp.zeros((GROUP, LANES), F32)]
    ahead = carried(0, 0)
    for n, (g, j) in enumerate(steps):
        now = ahead
        if n + 1 < len(steps):
            ahead = carried(*steps[n + 1])
        rows, u, ent = span(g, GROUP), (u0, u1)[g], (e0, e1)[g]
        gated = (u[:, span(j)] + ent[:, span(j)] * now) * zs_r[rows, span(j)]
        rows_o[rows, span(j)] = (gated * gain[:, span(j)]).astype(BF16)
        square = gated * gated
        squares[g] = squares[g] + (square[:, :LANES] + square[:, LANES:])
    part = dot(rows_o[...], w_out[:, block_cols(idx, 2)])
    for g in range(2):
        hi, mid, lo = three(squares[g])
        sums_o[:, span(g, GROUP)] = dot_nt(ones, hi) + (dot_nt(ones, mid) + dot_nt(ones, lo))
    part = part.astype(BF16)
    tail = tail_rows(sums_o[0:1, :])
    for g, out in enumerate((top, low)):
        out[:GROUP, :] = part[span(g, GROUP)]
        out[GROUP:, :] = tail


def gated_rows(idx, parts, first, thr, c, us, ents, zs, gain, w_out):
    return call(
        gated_body,
        "gated_rows",
        idx,
        [*parts, first, thr, c, *us, *ents, zs, gain, w_out],
        [((ROWS, WIDTH), BF16), ((8, ROWS), F32), *[((TAILED, FEAT), BF16)] * 2],
        [((NSTATE, WIDTH), BF16)],
        flops=2.6 * ROWS * WIDTH * FEAT,
    )


def near_body(bits, g, idx, rows, w_out, message, part):
    value = dot(rows[...], w_out[:, block_cols(idx, bits)])
    part[...] = value[span(g, GROUP)]
    message[...] = value[span(1 - g, GROUP)].astype(BF16)


def near_block(bits, g, idx, rows, w_out):
    return call(
        functools.partial(near_body, bits, g),
        "near_block",
        idx,
        [rows, w_out],
        [((GROUP, FEAT), BF16), ((GROUP, FEAT), F32)],
        flops=1e6,
    )


def own_body(idx, rows, w_out, out):
    out[...] = dot(rows[...], w_out[:, block_cols(idx, 0)])


def own_block(idx, rows, w_out):
    return call(
        own_body,
        "own_block",
        idx,
        [rows, w_out],
        [((ROWS, FEAT), F32)],
        flops=1e6,
    )[0]


def join_body(idx, part, half, out):
    out[:GROUP, :] = (part[...] + half[:GROUP, :].astype(F32)).astype(BF16)
    out[GROUP:, :] = half[GROUP:, :]


def join(idx, part, half):
    return call(join_body, "join", idx, [part, half], [((TAILED, FEAT), BF16)], mib=8)[0]


def add_body(idx, own, left_0, right_1, out):
    out[:GROUP, :] = own[:GROUP, :] + left_0[...].astype(F32)
    out[GROUP:, :] = own[GROUP:, :] + right_1[...].astype(F32)


def add_near(idx, own, left_0, right_1):
    return call(
        add_body,
        "add_near",
        idx,
        [own, left_0, right_1],
        [((ROWS, FEAT), F32)],
        mib=8,
        flops=5e9,
        aliases={1: 0},
    )[0]


def settle_body(idx, own, sums, near, other, left_1, out, factor, made, sem):
    squares = sums[0:1, :] + squares_of(left_1)
    squares = squares + (squares_of(near) + squares_of(other))
    stack = terms(squares, 16, ROWS).astype(BF16)
    scale = lax.rsqrt(dot_tn(stack, jnp.ones((16, LANES), BF16)) / DI + 1e-05)
    factor[...] = scale[:GROUP]
    for k in range(FEAT // LANES):
        lanes = span(k, LANES)
        value = own[GROUP:, lanes] + left_1[:GROUP, lanes].astype(F32)
        made[:, lanes] = (value * scale[GROUP:]).astype(BF16)
    copy = pltpu.make_async_copy(made, out.at[GROUP:, :], sem)
    copy.start()
    copy.wait()


def end_call(body, name, idx, args, outs, specs, more=()):
    args = [pltpu.with_memory_space_constraint(a, pltpu.VMEM) for a in args]
    return pl.pallas_call(
        body,
        in_specs=[SMEM, *[VMEM] * len(args), *[HBM] * len(more)],
        out_specs=specs,
        out_shape=outs,
        scratch_shapes=[pltpu.VMEM((GROUP, FEAT), BF16), pltpu.SemaphoreType.DMA],
        input_output_aliases={1 + len(args): 0} if more else {},
        compiler_params=pltpu.CompilerParams(vmem_limit_bytes=8 * MIB),
        cost_estimate=cost(1e6, 1e6),
        name=name,
    )(idx, *args, *more)


def settle(idx, *args):
    outs = [jax.ShapeDtypeStruct((ROWS, FEAT), BF16), pltpu.VMEM((GROUP, LANES), F32)]
    return end_call(settle_body, "settle", idx, args, outs, [HBM, VMEM])


def norm_body(idx, own, factor, right_0, so_far, out, made, sem):
    for k in range(FEAT // LANES):
        lanes = span(k, LANES)
        value = own[:GROUP, lanes] + right_0[:GROUP, lanes].astype(F32)
        made[:, lanes] = (value * factor[...]).astype(BF16)
    copy = pltpu.make_async_copy(made, out.at[:GROUP, :], sem)
    copy.start()
    copy.wait()


def norm(idx, own, factor, right_0, so_far):
    outs = jax.ShapeDtypeStruct((ROWS, FEAT), BF16)
    return end_call(norm_body, "norm", idx, (own, factor, right_0), outs, HBM, (so_far,))


def on_device(tokens, resets, w_x, w_z, w_bc, w_dt, dt_bias, decay_rate, d_skip, norm_gain, w_out):
    places = ("head", "seq_0", "seq_1")
    idx = jnp.stack([lax.axis_index(axis) for axis in places]).astype(jnp.int32)
    heads = w_dt.shape[1]
    top, low = tokens[:GROUP], tokens[GROUP:]
    l_0, r_1 = swapped(top, "head", 1), swapped(low, "head", 3)
    top, low, idx = lax.optimization_barrier((top, low, idx))
    l_1, r_0 = swapped(low, "head", 1), swapped(top, "head", 3)
    bias = jnp.pad(dt_bias, (0, LANES - heads)).reshape(1, LANES)
    rate = jnp.pad(decay_rate, (0, LANES - heads)).reshape(1, LANES)
    starts = resets.reshape(1, ROWS)
    skip = jnp.pad(d_skip, (0, LANES - heads)).reshape(1, LANES)
    gain = norm_gain.reshape(1, WIDTH)

    acc_x, acc_bd, tokens, w_dt, w_x, w_z, w_bc = load_weights(
        idx, tokens, w_dt.T, w_x, w_z, w_bc
    )
    far = [swapped(l_0, "head", 3), swapped(r_1, "head", 1)]
    acc_z = gate_first(idx, tokens, l_0, r_1, w_z)
    near = (l_0, l_1, r_0, r_1)
    sums = project(idx, near, w_x, w_bc, w_dt, (acc_x, acc_bd))
    acc_z = gate_second(idx, l_1, r_0, w_z, acc_z)
    far, acc_z, sums = lax.optimization_barrier((far, acc_z, sums))
    inner, b, c, cum, step, first, thr, *messages = device_state(
        idx, far, w_x, w_bc, w_dt, sums, starts, bias, rate
    )
    quarters = [messages[0], *(swapped(messages[d], "seq_1", d) for d in (1, 2, 3))]
    u0, e0 = mix(0, idx, inner, b, c, cum, step, skip)
    quarters, u0, e0, cum = lax.optimization_barrier((quarters, u0, e0, cum))
    total = row_total(idx, quarters)
    totals = [total, *(swapped(total, "seq_0", d) for d in (1, 2, 3))]
    u1, e1 = mix(1, idx, inner, b, c, cum, step, skip)
    totals, u1, e1, w_z = lax.optimization_barrier((totals, u1, e1, w_z))
    parts = prefixes(idx, quarters, totals)
    parts = [parts[0], *(swapped(parts[d], "seq_1", d) for d in (1, 2, 3))]
    zs = gate(idx, far, w_z, acc_z)
    rows, sums, top, low = gated_rows(
        idx, parts, first, thr, c, (u0, u1), (e0, e1), zs, gain, w_out
    )
    top, low = swapped(top, "head", 1), swapped(low, "head", 3)
    left_0, part_1 = near_block(1, 1, idx, rows, w_out)
    left_0 = swapped(left_0, "head", 1)
    right_1, part_0 = near_block(3, 0, idx, rows, w_out)
    right_1 = swapped(right_1, "head", 3)
    right_0, left_1 = join(idx, part_0, top), join(idx, part_1, low)
    right_0, left_1, rows = lax.optimization_barrier((right_0, left_1, rows))
    own = own_block(idx, rows, w_out)
    right_0, left_1 = swapped(right_0, "head", 3), swapped(left_1, "head", 1)
    own = add_near(idx, own, left_0, right_1)
    half, factor = settle(idx, own, sums, top, low, left_1)
    return norm(idx, own, factor, right_0, half)


def solution(mesh):
    split = Mesh(
        mesh.devices.reshape(4, 4, mesh.shape["head"], mesh.shape["batch"]),
        ("seq_0", "seq_1", "head", "batch"),
    )
    placed = (
        P(BATCH_SEQ, "head"),
        P(BATCH_SEQ),
        P(None, "head"),
        P(None, "head"),
        P(),
        P(None, "head"),
        P("head"),
        P("head"),
        P("head"),
        P("head"),
        P("head", None),
    )
    return jax.shard_map(
        on_device, mesh=split, in_specs=placed, out_specs=P(BATCH_SEQ, "head"), check_vma=False
    )
```
